32 devices in a mesh: wide: 8 (over z, y), narrow: 4 (over x, core).
Axes of the slice: x: 2, y: 2, z: 4, core: 2. Of those that a mesh axis runs over, the one named last changes fastest.
Arguments:
- logits: float32 [512, 32768], P(None, ('wide', 'narrow')), may hold values from -6 to 6
- filt: float32 [512], P(('wide', 'narrow')), may hold values from -6 to 6
- cells: float32 [512, 2048], P(('wide', 'narrow')), may hold values from 0.05 to 5
- cell_mask: int32 [512], replicated, may hold values 0 or 1
- gene_mask: int32 [8, 2048], replicated, may hold values 0 or 1
- slide_ids: int32 [32768], P(('wide', 'narrow')), may hold values from 0 to 7, never falling along the last dimension, each value on 1 to 8192 neighbouring positions
- target: float32 [32768, 2048], P(('wide', 'narrow')), may hold values from 0.05 to 5
- density: float32 [32768], P(('wide', 'narrow')), may hold values from 1 to 10
Outputs:
- loss_terms: float32 [3], replicated
- reg_terms: float32 [4], replicated
- g_pred: float32 [32768, 2048], P(('wide', 'narrow'))
- gene_cos: float32 [8, 2048], replicated
- spot_cos: float32 [32768], P(('wide', 'narrow'))
- grad_logits: float32 [512, 32768], P(None, ('wide', 'narrow'))
- grad_filter: float32 [512], P(('wide', 'narrow'))
- grad_cells: float32 [512, 2048], P(('wide', 'narrow'))
The draws below stay inside these ranges and needn't reach their ends.
Inputs may be any that keep to these rules, and one draw needn't show every extreme that they name: `slide_ids`: each slide's spots form one run of consecutive positions, slides in increasing order, each with 1 to 8192 spots and one with exactly that many.
All inputs are finite; a program needn't handle non-finite values.
Results may differ from the reference program's by a relative error of at most 0.00015.
Values sent between devices are 32-bit elements; how exact they have to be, the bound alone decides.
A program may use at most 256 MiB of HBM per device.

```python
import math
import jax
import jax.numpy as jnp
import numpy as np
from jax import lax

G = 2048
NSLIDE = 8
CELLS = 512
SPOTS = 32768
TARGET = 128


def with_ends(result, own_key, least, largest):
    spot = [jax.random.randint(jax.random.fold_in(own_key, axis), (), 0, length) for axis, length in enumerate(result.shape)]
    longest = result.shape.index(max(result.shape))
    neighbour = spot[:longest] + [(spot[longest] + 1) % result.shape[longest]] + spot[longest + 1:]
    return result.at[tuple(spot)].set(least).at[tuple(neighbour)].set(largest)


def shard_levels(rng, dims, shards, least, high):
    def one(dim, shards_of):
        draws = jax.random.uniform(jax.random.fold_in(jax.random.fold_in(rng, 6), dim), (shards_of,), jnp.float32, least / len(shards), high / len(shards))
        return jnp.repeat(jnp.exp(draws), dims[dim] // shards_of).reshape((-1,) + (1,) * (len(dims) - dim - 1))

    factor_of = one(*shards[0])
    for cut in shards[1:]:
        factor_of = factor_of * one(*cut)
    return factor_of


def length_profile(amount, total, reach, slope):
    loads = [(1 << 20) // math.isqrt(standing ** slope) + 1 for standing in range(2, amount + 1)]
    rest, holding = total - reach - (amount - 1), [1] * (amount - 1)
    while rest > 0:
        candidates = [i for i in range(amount - 1) if holding[i] < reach]
        whole, remaining = sum([loads[i] for i in candidates]), rest
        for i in candidates:
            addition = min(reach - holding[i], max(1, remaining * loads[i] // whole), rest)
            holding[i] = holding[i] + addition
            rest = rest - addition
    return np.array([reach] + holding)


def ragged(rng, amount, total, most, slope):
    if amount == 2:
        one = jax.random.randint(rng, (), max(1, total - most), min(most, total - 1) + 1)
        return jnp.stack([one, total - one])
    tallies = jnp.asarray(length_profile(amount, total, most, slope), jnp.int32)
    pairs = (amount - 1) // 2
    source_of, receiver = tallies[1:1 + 2 * pairs:2], tallies[2:2 + 2 * pairs:2]
    room = jnp.minimum(source_of - 1, most - receiver)
    shifted = jax.random.randint(jax.random.fold_in(rng, 1), (pairs,), 0, 1 << 20) % (room + 1)
    tallies = tallies.at[1:1 + 2 * pairs:2].set(source_of - shifted).at[2:2 + 2 * pairs:2].set(receiver + shifted)
    return tallies[jax.random.permutation(jax.random.fold_in(rng, 2), amount)]


def normal_values(key, shape, scale, most, split=(), kind=jnp.bfloat16):
    drawn = jax.random.normal(key, shape, jnp.float32) * scale
    if len(split) > 0:
        drawn = shard_levels(key, shape, split, -0.22, 0.18) * drawn
    return jnp.clip(drawn, min=-most, max=most).astype(kind)


def setup_inputs(seed: int = 0) -> dict:
    streams_of = jax.random.split(jax.random.key(seed), 9)
    return {
        "logits": normal_values(streams_of[0], (CELLS, SPOTS), 1.0, 6.0, ((1, 32),), jnp.float32),
        "filt": normal_values(streams_of[1], (CELLS,), 1.5, 6.0, ((0, 32),), jnp.float32),
        "cells": jnp.clip(jnp.exp(math.log(5.0) - 4.6051702 * jax.random.uniform(streams_of[2], (CELLS, G), jnp.float32) ** shard_levels(streams_of[2], (CELLS, G), ((0, 32),), -0.2, 0.2)), 0.05, 5.0),
        "cell_mask": with_ends((jax.random.randint(streams_of[3], (CELLS,), 0, 12) < 11).astype(jnp.int32), jax.random.fold_in(streams_of[3], 1), 0, 1),
        "gene_mask": with_ends((jax.random.randint(streams_of[4], (NSLIDE, G), 0, 4) < 3).astype(jnp.int32), jax.random.fold_in(streams_of[4], 1), 0, 1),
        "slide_ids": jnp.searchsorted(jnp.cumsum(ragged(streams_of[5], NSLIDE, SPOTS, SPOTS // 4, 1)), jnp.arange(SPOTS), side="right").astype(jnp.int32),
        "target": jnp.clip(jnp.exp(math.log(5.0) - 4.6051702 * jax.random.uniform(streams_of[6], (SPOTS, G), jnp.float32) ** shard_levels(streams_of[6], (SPOTS, G), ((0, 32),), -0.2, 0.2)), 0.05, 5.0),
        "density": jnp.clip(jnp.exp(math.log(10.0) - 2.3025851 * jax.random.uniform(streams_of[7], (SPOTS,), jnp.float32) ** shard_levels(streams_of[7], (SPOTS,), ((0, 32),), -0.2, 0.2)), 1.0, 10.0),
    }


def forward(logits, filt, cells, cell_mask, gene_mask, slide_ids, target, density):
    high = lax.Precision.HIGHEST
    eps = 1e-06
    valid = cell_mask.astype(jnp.float32)
    top = lax.optimization_barrier(jnp.max(logits, axis=0, keepdims=True))
    expo = jnp.exp(logits - top) * valid[:, None]
    total = lax.optimization_barrier(jnp.sum(expo, axis=0, keepdims=True))
    prob = expo / total
    keep = jax.nn.sigmoid(filt)
    weighted = prob * keep[:, None]
    g_pred = jnp.dot(weighted.T, cells, precision=high)
    gmask = gene_mask.astype(jnp.float32)
    dot_s = jax.ops.segment_sum(g_pred * target, slide_ids, NSLIDE)
    pp_s = jax.ops.segment_sum(g_pred * g_pred, slide_ids, NSLIDE)
    tt_s = jax.ops.segment_sum(target * target, slide_ids, NSLIDE)
    gene_cos = gmask * dot_s * lax.rsqrt(pp_s + eps) * lax.rsqrt(tt_s + eps)
    gene_loss = -jnp.sum(gene_cos)
    spot_mask = gmask[slide_ids]
    sdot = lax.optimization_barrier(jnp.sum(spot_mask * g_pred * target, axis=1))
    spp = lax.optimization_barrier(jnp.sum(spot_mask * g_pred * g_pred, axis=1))
    stt = lax.optimization_barrier(jnp.sum(spot_mask * target * target, axis=1))
    spot_cos = sdot * lax.rsqrt(spp + eps) * lax.rsqrt(stt + eps)
    spot_loss = -jnp.sum(spot_cos)
    mass = lax.optimization_barrier(jnp.sum(weighted, axis=0))
    mass_s = jax.ops.segment_sum(mass, slide_ids, NSLIDE)
    wsum_s = jax.ops.segment_sum(density, slide_ids, NSLIDE)
    dens = density / wsum_s[slide_ids]
    share = mass / mass_s[slide_ids]
    kl_term = jnp.sum(dens * (jnp.log(dens) - jnp.log(share)))
    count = jnp.sum(valid * keep)
    count_term = jnp.abs(count - TARGET) / CELLS
    binarity = jnp.sum(valid * (keep - keep * keep)) / CELLS
    logp = jnp.where(valid[:, None] > 0, logits - top - jnp.log(total), 0.0)
    entropy = -jnp.sum(prob * logp) / SPOTS
    loss = gene_loss + spot_loss + kl_term + count_term + binarity
    terms = jnp.stack([loss, gene_loss, spot_loss])
    reg_terms = jnp.stack([kl_term, count_term, binarity, entropy])
    return (loss, (terms, reg_terms, g_pred, gene_cos, spot_cos))

def reference(logits, filt, cells, cell_mask, gene_mask, slide_ids, target, density):

    def closed(lg, fl, ce):
        return forward(lg, fl, ce, cell_mask, gene_mask, slide_ids, target, density)
    loss, pullback, extras = jax.vjp(closed, logits, filt, cells, has_aux=True)
    grad_logits, grad_filter, grad_cells = pullback(jnp.ones_like(loss))
    terms, reg_terms, g_pred, gene_cos, spot_cos = extras
    return (terms, reg_terms, g_pred, gene_cos, spot_cos, grad_logits, grad_filter, grad_cells)
```

```python
import jax
import jax.numpy as jnp
from jax import lax
from jax.experimental import pallas as pl
from jax.experimental.pallas import tpu as pltpu
from jax.sharding import PartitionSpec as P

eps = 1e-06
MESH = pl.DeviceIdType.MESH
bf16 = jnp.bfloat16
f32 = jnp.float32
LANES = 128
NCH = 8
TR = 256


def split(value):
    high = value.astype(bf16)
    return high, (value - high.astype(f32)).astype(bf16)


def mm(a, b):
    return lax.dot_general(a, b, (((1,), (0,)), ((), ())), preferred_element_type=f32)


def mm_nt(a, b):
    return lax.dot_general(a, b, (((1,), (1,)), ((), ())), preferred_element_type=f32)


def fused_kernel(
    logits_hbm, filt_ref, cells_hbm, mask_ref, gene_ref, ids_ref, target_hbm, dens_ref,
    terms_ref, reg_ref, pred_hbm, gcos_ref, scos_ref, glog_hbm, gfilt_ref, gcell_ref,
    lg, tv, pv, buf, chi, clo, fb, valid, keepc, whi, wlo, thi, tlo, gmb, oh, ohm, l1, l2,
    sd, sp, st, mass, rows, gph, gpl, gw, kp,
    stat, a1, a2, a3, gtot, gacc, kvec, k1, k2, k3,
    part, rb, sb, r1, tt_, r2, qq, r3,
    lsem, tsem, psem, osem,
    zs, zr, xs, xr, ys, yr, bs, br,
    fzs, fzr, fxs, fxr, fys, fyr, fbs, fbr,
    as1, ar1, as2, ar2, as3, ar3,
    ks1, kr1, ks2, kr2, ks3, kr3,
    cbs, cbr, cxs, cxr, cys, cyr, czs, czr,
):
    n_cells = chi.shape[1]
    width = chi.shape[2]
    spots = tv.shape[1]
    n_slides = gene_ref.shape[0]
    tiles = spots // LANES
    n_tiles = spots // TR
    wide, narrow = lax.axis_index("wide"), lax.axis_index("narrow")
    z, y = lax.div(wide, 2), lax.rem(wide, 2)
    x, core = lax.div(narrow, 2), lax.rem(narrow, 2)
    to_z = [(lax.rem(z + k, 4) * 2 + y, narrow) for k in (1, 2, 3)]
    from_z = [lax.rem(z + 4 - k, 4) for k in (1, 2, 3)]
    to_x = (wide, (1 - x) * 2 + core)
    to_y = (z * 2 + 1 - y, narrow)
    to_xy = (z * 2 + 1 - y, (1 - x) * 2 + core)
    to_b = (wide, x * 2 + 1 - core)

    def rcopy(src, dst, ss, rs, dev):
        return pltpu.make_async_remote_copy(
            src_ref=src, dst_ref=dst, send_sem=ss, recv_sem=rs, device_id=dev, device_id_type=MESH
        )

    def lanes(i, w=LANES):
        return pl.ds(pl.multiple_of(i * w, w), w)

    def own_cells(c, h):
        return pltpu.make_async_copy(
            cells_hbm.at[:, pl.ds((c * 2 + h) * LANES, LANES)], buf.at[c, h, z, y, x, core], lsem.at[c, h]
        )

    def get_logits(i):
        return pltpu.make_async_copy(logits_hbm.at[:, lanes(i)], lg.at[i], osem.at[i])

    def get_target(c):
        return pltpu.make_async_copy(target_hbm.at[:, lanes(c, width)], tv.at[c], tsem.at[c])

    def put_pred(c):
        return pltpu.make_async_copy(pv.at[c], pred_hbm.at[:, lanes(c, width)], psem.at[c])

    def put_glog(i):
        return pltpu.make_async_copy(gw.at[i], glog_hbm.at[:, lanes(i)], osem.at[i])

    for c in range(NCH):
        for h in range(2):
            own_cells(c, h).start()
    for i in range(tiles):
        get_logits(i).start()
    for c in range(NCH):
        get_target(c).start()

    barrier = pltpu.get_barrier_semaphore()
    for dev in to_z + [to_x, to_y, to_xy, to_b]:
        pl.semaphore_signal(barrier, inc=1, device_id=dev, device_id_type=MESH)

    row16 = lax.broadcasted_iota(jnp.int32, (16, LANES), 0)
    mine = jnp.zeros((16, LANES), f32)
    for r in range(16):
        mine = jnp.where(row16 == r, filt_ref[r], mine)
    fb[z, y, x, core] = mine
    for q in range(n_cells // LANES):
        line = mask_ref[q : q + 1, :].astype(f32)
        valid[q * LANES : (q + 1) * LANES, :] = jnp.broadcast_to(line, (LANES, LANES)).T
    pl.semaphore_wait(barrier, 7)

    def z_out(c, k):
        r = buf.at[c, :, z, y, x, core]
        return rcopy(r, r, zs.at[c, k], zr.at[c, k], to_z[k])

    def z_in(c, k):
        r = buf.at[c, :, from_z[k], y, x, core]
        return rcopy(r, r, zs.at[c, k], zr.at[c, k], to_z[k])

    def s1_out(c):
        a = buf.at[c, 0, :, y, x, core]
        b = buf.at[c, 1, :, y, x, core]
        return [rcopy(a, a, xs.at[c, 0], xr.at[c, 0], to_x), rcopy(b, b, ys.at[c, 0], yr.at[c, 0], to_y)]

    def s1_in(c):
        a = buf.at[c, 0, :, y, 1 - x, core]
        b = buf.at[c, 1, :, 1 - y, x, core]
        return [rcopy(a, a, xs.at[c, 0], xr.at[c, 0], to_x), rcopy(b, b, ys.at[c, 0], yr.at[c, 0], to_y)]

    def s2_out(c):
        a = buf.at[c, 0, :, y, :, core]
        b = buf.at[c, 1, :, :, x, core]
        return [rcopy(a, a, ys.at[c, 1], yr.at[c, 1], to_y), rcopy(b, b, xs.at[c, 1], xr.at[c, 1], to_x)]

    def s2_in(c):
        a = buf.at[c, 0, :, 1 - y, :, core]
        b = buf.at[c, 1, :, :, 1 - x, core]
        return [rcopy(a, a, ys.at[c, 1], yr.at[c, 1], to_y), rcopy(b, b, xs.at[c, 1], xr.at[c, 1], to_x)]

    def s3_out(c):
        r = buf.at[c, :, :, :, :, core]
        return rcopy(r, r, bs.at[c], br.at[c], to_b)

    def s3_in(c):
        r = buf.at[c, :, :, :, :, 1 - core]
        return rcopy(r, r, bs.at[c], br.at[c], to_b)

    def fz_out(k):
        r = fb.at[z, y, x, core]
        return rcopy(r, r, fzs.at[k], fzr.at[k], to_z[k])

    def fz_in(k):
        r = fb.at[from_z[k], y, x, core]
        return rcopy(r, r, fzs.at[k], fzr.at[k], to_z[k])

    def fx(at):
        r = fb.at[:, y, at, core]
        return rcopy(r, r, fxs.at[0], fxr.at[0], to_x)

    def fy(at):
        r = fb.at[:, at, :, core]
        return rcopy(r, r, fys.at[0], fyr.at[0], to_y)

    def fs(at):
        r = fb.at[:, :, :, at]
        return rcopy(r, r, fbs.at[0], fbr.at[0], to_b)

    def b1(c):
        return rcopy(stat.at[c], a1.at[c], as1.at[c], ar1.at[c], to_b)

    plane = [to_x, to_y, to_xy]
    here = y * 2 + x
    there = [y * 2 + 1 - x, (1 - y) * 2 + x, (1 - y) * 2 + 1 - x]

    def b2_out(c, k):
        r = a2.at[c, here]
        return rcopy(r, r, as2.at[c, k], ar2.at[c, k], plane[k])

    def b2_in(c, k):
        r = a2.at[c, there[k]]
        return rcopy(r, r, as2.at[c, k], ar2.at[c, k], plane[k])

    def b3_out(c, k):
        r = a3.at[c, z]
        return rcopy(r, r, as3.at[c, k], ar3.at[c, k], to_z[k])

    def b3_in(c, k):
        r = a3.at[c, from_z[k]]
        return rcopy(r, r, as3.at[c, k], ar3.at[c, k], to_z[k])

    def sum_second(c):
        b1(c).wait_recv()
        a2[c, here] = stat[c] + a1[c]
        for k in range(3):
            b2_out(c, k).start()

    def sum_third(c):
        for k in range(3):
            b2_in(c, k).wait_recv()
        a3[c, z] = (a2[c, 0] + a2[c, 1]) + (a2[c, 2] + a2[c, 3])
        for k in range(3):
            b3_out(c, k).start()

    def sum_last(c):
        for k in range(3):
            b3_in(c, k).wait_recv()
        return (a3[c, 0] + a3[c, 1]) + (a3[c, 2] + a3[c, 3])

    def softmax(i, ent):
        get_logits(i).wait()
        value = lg[i]
        top = jnp.max(value, axis=0, keepdims=True)
        expo = jnp.exp(value - top) * valid[...]
        total = jnp.sum(expo, axis=0, keepdims=True)
        prob = expo * (1.0 / total)
        lg[i] = prob
        return ent + jnp.sum(prob * (value - top - jnp.log(total)), axis=0, keepdims=True)

    def one_hot(i, _):
        ids = ids_ref[pl.ds(i, 1), :]
        square = (lax.broadcasted_iota(jnp.int32, (LANES, LANES), 0) == ids).astype(f32)
        oh[lanes(i), :] = square.T.astype(bf16)
        ohm[:, lanes(i)] = square[:16, :].astype(bf16)
        return 0

    def weights(i, _):
        w = lg[i] * keepc[...]
        mass[pl.ds(i, 1), :] = jnp.sum(w, axis=0, keepdims=True)
        high, low = split(w)
        whi[:, lanes(i)] = high
        wlo[:, lanes(i)] = low
        turned = w.T
        high, low = split(turned)
        thi[lanes(i), :] = high
        tlo[lanes(i), :] = low
        return 0

    for k in range(3):
        fz_out(k).start()
    for c in range(NCH):
        for h in range(2):
            own_cells(c, h).wait()
        for k in range(3):
            z_out(c, k).start()

    def gather_tick(t):
        def stage_one(c):
            for k in range(3):
                z_in(c, k).wait_recv()
            for d in s1_out(c):
                d.start()

        def stage_two(c):
            for d in s1_in(c):
                d.wait_recv()
            for d in s2_out(c):
                d.start()

        def stage_three(c):
            for d in s2_in(c):
                d.wait_recv()
            s3_out(c).start()

        for lag, stage in ((0, stage_one), (1, stage_two), (2, stage_three)):
            if isinstance(t, int):
                if 0 <= t - lag < NCH:
                    stage(t - lag)
            else:
                pl.when(jnp.logical_and(t - lag >= 0, t - lag < NCH))(lambda s=stage, c=t - lag: s(c))

    for k in range(3):
        fz_in(k).wait_recv()
    fx(x).start()
    gather_tick(0)
    for c in range(NCH):
        gm = jnp.concatenate(
            [gene_ref[:, c * width : (c + 1) * width].astype(f32), jnp.zeros((LANES - n_slides, width), f32)], axis=0
        )
        gmb[c] = gm.astype(bf16)
    ent = lax.fori_loop(0, tiles // 2, softmax, jnp.zeros((1, LANES), f32))
    fx(1 - x).wait_recv()
    fy(y).start()
    gather_tick(1)
    ent = lax.fori_loop(tiles // 2, tiles, softmax, ent)
    fy(1 - y).wait_recv()
    fs(core).start()
    gather_tick(2)
    lax.fori_loop(0, tiles, one_hot, 0)
    fs(1 - core).wait_recv()
    keepc[...] = jax.nn.sigmoid(fb[...].reshape(n_cells, LANES))
    lax.fori_loop(0, tiles, weights, 0)
    sd[...] = jnp.zeros_like(sd)
    sp[...] = jnp.zeros_like(sp)
    st[...] = jnp.zeros_like(st)

    def fold(v):
        out = v[:, :LANES]
        for k in range(1, v.shape[1] // LANES):
            out = out + v[:, k * LANES : (k + 1) * LANES]
        return out

    def forward(c):
        s3_in(c).wait_recv()
        get_target(c).wait()
        whole = jnp.concatenate([buf[c, h].reshape(n_cells, LANES) for h in range(2)], axis=1)
        high, low = split(whole)
        chi[c] = high
        clo[c] = low

        def rows_of(r, sums):
            at = pl.ds(pl.multiple_of(r * TR, TR), TR)
            wh, wl = thi[at, :], tlo[at, :]
            ch, cl = chi[c], clo[c]
            pred = mm(jnp.concatenate([wh, wl, wh], axis=1), jnp.concatenate([ch, ch, cl], axis=0))
            pv[c, at, :] = pred
            tgt = tv[c, at, :]
            seen = mm(oh[at, :], gmb[c])
            who = ohm[:, at]
            who = jnp.concatenate([who, who], axis=1)
            out = []
            for prod, spot in ((pred * tgt, sd), (pred * pred, sp), (tgt * tgt, st)):
                spot[at, :] += fold(seen * prod)
                ph, plo = split(prod)
                out.append(mm(who, jnp.concatenate([ph, plo], axis=0)))
            return tuple(a + b for a, b in zip(sums, out))

        zero = jnp.zeros((16, width), f32)
        sums = lax.fori_loop(0, n_tiles, rows_of, (zero, zero, zero))
        for k in range(3):
            stat[c, k * 8 : (k + 1) * 8, :] = sums[k][:8, :]
        put_pred(c).start()

    zero8 = jnp.zeros((8, width), f32)

    def middle(t, _):
        gather_tick(t)
        c = t - 3
        forward(c)
        stat[c, 24:32, :] = zero8
        b1(c).start()
        pl.when(c >= 1)(lambda: sum_second(c - 1))
        pl.when(c >= 2)(lambda: sum_third(c - 2))
        return 0

    lax.fori_loop(3, NCH + 2, middle, 0)
    last = NCH - 1
    forward(last)

    def spot_rows(i, _):
        for k, ref in enumerate((sd, sp, st)):
            rows[k, pl.ds(i, 1), :] = jnp.sum(ref[lanes(i), :].T, axis=0, keepdims=True)
        return 0

    lax.fori_loop(0, tiles, spot_rows, 0)
    sdot, spp, stt = rows[0], rows[1], rows[2]
    scale = lax.rsqrt(spp + eps) * lax.rsqrt(stt + eps)
    scos = sdot * scale
    scos_ref[...] = scos
    shrink = scale * (sdot / (spp + eps))
    for k, value in ((0, scale), (1, shrink)):
        high, low = split(value)
        rows[2 * k] = high.astype(f32)
        rows[2 * k + 1] = low.astype(f32)
    dens = dens_ref[...]
    mass_row = mass[...]
    rows[4] = dens * (jnp.log(dens) - jnp.log(mass_row))

    iota8 = lax.broadcasted_iota(jnp.int32, (8, LANES), 0)
    lane8 = lax.broadcasted_iota(jnp.int32, (8, LANES), 1)

    def coef_rows(i, sums):
        mine = (iota8 == ids_ref[pl.ds(i, 1), :]).astype(f32)
        pad = jnp.zeros((LANES - 32, LANES), f32)
        at = pl.ds(i, 1)
        for k, ref in ((0, l1), (1, l2)):
            ref[lanes(i), :] = jnp.concatenate(
                [mine, mine, mine * rows[2 * k, at, :], mine * rows[2 * k + 1, at, :], pad], axis=0
            ).T.astype(bf16)
        return (
            sums[0] + mine * mass[at, :],
            sums[1] + mine * dens_ref[at, :],
            sums[2] + mine * rows[4, at, :],
        )

    zero = jnp.zeros((8, LANES), f32)
    totals = lax.fori_loop(0, tiles, coef_rows, (zero, zero, zero))
    extra = zero
    for k, value in enumerate(totals):
        extra = jnp.where(lane8 == k, jnp.sum(value, axis=1, keepdims=True), extra)
    extra = jnp.where(jnp.logical_and(lane8 == 3, iota8 == 0), -jnp.sum(scos), extra)
    extra = jnp.where(jnp.logical_and(lane8 == 4, iota8 == 0), -jnp.sum(ent), extra)
    stat[last, 24:32, :] = jnp.concatenate([extra] + [zero] * (width // LANES - 1), axis=1)
    b1(last).start()
    sum_second(last - 1)
    sum_third(last - 2)

    gacc[...] = jnp.zeros_like(gacc)
    gw[...] = jnp.zeros_like(gw)

    def scatter_sib(c):
        return rcopy(part.at[c, :, :, :, :, 1 - core], rb.at[c], cbs.at[c], cbr.at[c], to_b)

    def scatter_one(c):
        return [
            rcopy(sb.at[c, 0, :, 1 - y], r1.at[c, 0], cys.at[c, 0], cyr.at[c, 0], to_y),
            rcopy(sb.at[c, 1, :, :, 1 - x], r1.at[c, 1], cxs.at[c, 0], cxr.at[c, 0], to_x),
        ]

    def scatter_two(c):
        return [
            rcopy(tt_.at[c, 0, :, 1 - x], r2.at[c, 0], cxs.at[c, 1], cxr.at[c, 1], to_x),
            rcopy(tt_.at[c, 1, :, 1 - y], r2.at[c, 1], cys.at[c, 1], cyr.at[c, 1], to_y),
        ]

    def scatter_z(c, k):
        return rcopy(qq.at[c, :, lax.rem(z + k + 1, 4)], r3.at[c, k], czs.at[c, k], czr.at[c, k], to_z[k])

    def sc1(c):
        scatter_sib(c).wait_recv()
        sb[c] = part[c, :, :, :, :, core] + rb[c]
        for d in scatter_one(c):
            d.start()

    def sc2(c):
        for d in scatter_one(c):
            d.wait_recv()
        tt_[c, 0] = sb[c, 0, :, y] + r1[c, 0]
        tt_[c, 1] = sb[c, 1, :, :, x] + r1[c, 1]
        for d in scatter_two(c):
            d.start()

    def sc3(c):
        for d in scatter_two(c):
            d.wait_recv()
        qq[c, 0] = tt_[c, 0, :, x] + r2[c, 0]
        qq[c, 1] = tt_[c, 1, :, y] + r2[c, 1]
        for k in range(3):
            scatter_z(c, k).start()

    def sc4(c):
        for k in range(3):
            scatter_z(c, k).wait_recv()
        for h in range(2):
            gcell_ref[:, lanes(c * 2 + h)] = (qq[c, h, z] + r3[c, 0, h]) + (r3[c, 1, h] + r3[c, 2, h])

    def backward(c):
        total = sum_last(c)
        gtot[c] = total
        dot_s, pp_s, tt_s = total[0:8], total[8:16], total[16:24]
        gm = gene_ref[:, lanes(c, width)].astype(f32)
        gscale = gm * lax.rsqrt(pp_s + eps) * lax.rsqrt(tt_s + eps)
        gcos = dot_s * gscale
        gcos_ref[:, lanes(c, width)] = gcos
        gacc[...] += gcos
        gshrink = gscale * (dot_s / (pp_s + eps))
        pad = jnp.zeros((LANES - 32, width), f32)
        coefs = []
        for value in (gscale, gshrink):
            high, low = split(value)
            coefs.append(
                jnp.concatenate([high.astype(f32), low.astype(f32), gm, gm, pad], axis=0).astype(bf16)
            )

        def rows_of(r, _):
            at = pl.ds(pl.multiple_of(r * TR, TR), TR)
            grad = mm(l2[at, :], coefs[1]) * pv[c, at, :] - mm(l1[at, :], coefs[0]) * tv[c, at, :]
            high, low = split(grad)
            gph[at, :] = high
            gpl[at, :] = low
            return 0

        lax.fori_loop(0, n_tiles, rows_of, 0)

        def cells_of(r, _):
            at = pl.ds(pl.multiple_of(r * LANES, LANES), LANES)
            wh, wl = whi[at, :], wlo[at, :]
            gh, gl = gph[...], gpl[...]
            out = mm(jnp.concatenate([wh, wl, wh], axis=1), jnp.concatenate([gh, gh, gl], axis=0))
            for h in range(2):
                part[c, h, r] = out[:, h * LANES : (h + 1) * LANES].reshape(2, 2, 2, 16, LANES)
            return 0

        lax.fori_loop(0, n_cells // LANES, cells_of, 0)
        scatter_sib(c).start()

        def spots_of(r, _):
            at = pl.ds(pl.multiple_of(r * TR, TR), TR)
            ch, cl = chi[c], clo[c]
            gh, gl = gph[at, :], gpl[at, :]
            out = mm_nt(jnp.concatenate([ch, cl, ch], axis=1), jnp.concatenate([gh, gh, gl], axis=1))
            for h in range(TR // LANES):
                gw[r * (TR // LANES) + h] += out[:, h * LANES : (h + 1) * LANES]
            return 0

        lax.fori_loop(0, n_tiles, spots_of, 0)

    def back_tick(t, _):
        backward(t)
        pl.when(t == 0)(lambda: sum_second(last))
        pl.when(t == 0)(lambda: sum_third(last - 1))
        pl.when(t == 1)(lambda: sum_third(last))
        pl.when(t >= 1)(lambda: sc1(t - 1))
        pl.when(t >= 2)(lambda: sc2(t - 2))
        pl.when(t >= 3)(lambda: sc3(t - 3))
        pl.when(t >= 4)(lambda: sc4(t - 4))
        return 0

    lax.fori_loop(0, NCH, back_tick, 0)
    sc1(last)
    sc2(last - 1)
    sc3(last - 2)

    sums_s = gtot[last, 24:32, :LANES]
    mass_s, wsum_s, logsum_s = sums_s[:, 0:1], sums_s[:, 1:2], sums_s[:, 2:3]
    kp[...] = jnp.zeros_like(kp)

    def finish(i, _):
        at = pl.ds(i, 1)
        mine = (iota8 == ids_ref[at, :]).astype(f32)
        mass_at = jnp.sum(mine * mass_s, axis=0, keepdims=True)
        wsum_at = jnp.sum(mine * wsum_s, axis=0, keepdims=True)
        gmass = -(dens_ref[at, :] / wsum_at) / mass[at, :] + 1.0 / mass_at
        prob = lg[i]
        grad = gw[i] + gmass
        kp[...] += prob * grad
        grad = keepc[...] * grad
        middle_ = jnp.sum(prob * grad, axis=0, keepdims=True)
        gw[i] = prob * (grad - middle_)
        put_glog(i).start()
        return 0

    lax.fori_loop(0, tiles, finish, 0)
    quarter = n_cells // LANES
    rows_k, rows_keep = [], []
    for q in range(quarter):
        rows_k.append(jnp.sum(kp[q * LANES : (q + 1) * LANES, :].T, axis=0, keepdims=True))
        rows_keep.append(keepc[q * LANES : (q + 1) * LANES, :].T[0:1, :])
    blank = jnp.zeros((8 - quarter, LANES), f32)
    kvec[...] = jnp.concatenate(rows_k + [blank], axis=0)
    keep = jnp.concatenate(rows_keep, axis=0)

    k1_copy = rcopy(kvec, k1, ks1.at[0], kr1.at[0], to_b)

    def k2_copy(slot, k):
        return rcopy(k2.at[slot], k2.at[slot], ks2.at[k], kr2.at[k], plane[k])

    def k3_copy(slot, k):
        return rcopy(k3.at[slot], k3.at[slot], ks3.at[k], kr3.at[k], to_z[k])

    k1_copy.start()
    sc2(last)
    sc3(last - 1)
    sc4(last - 3)
    k1_copy.wait_recv()
    k2[here] = kvec[...] + k1[...]
    for k in range(3):
        k2_copy(here, k).start()
    sc3(last)
    sc4(last - 2)
    for k in range(3):
        k2_copy(there[k], k).wait_recv()
    k3[z] = (k2[0] + k2[1]) + (k2[2] + k2[3])
    for k in range(3):
        k3_copy(z, k).start()

    ok = mask_ref[...].astype(f32)
    count = jnp.sum(ok * keep)
    target_count = n_cells // 4
    count_term = jnp.abs(count - target_count) / n_cells
    binarity = jnp.sum(ok * (keep - keep * keep)) / n_cells
    gene_loss = -jnp.sum(gacc[...])
    spot_loss = jnp.sum(jnp.where(jnp.logical_and(lane8 == 3, iota8 == 0), sums_s, 0.0))
    entropy = jnp.sum(jnp.where(jnp.logical_and(lane8 == 4, iota8 == 0), sums_s, 0.0)) / (spots * 32)
    kl = jnp.sum(logsum_s / wsum_s + jnp.log(mass_s) - jnp.log(wsum_s))
    terms_ref[0] = gene_loss + spot_loss + kl + count_term + binarity
    terms_ref[1] = gene_loss
    terms_ref[2] = spot_loss
    reg_ref[0] = kl
    reg_ref[1] = count_term
    reg_ref[2] = binarity
    reg_ref[3] = entropy

    sc4(last - 1)
    for k in range(3):
        k3_copy(from_z[k], k).wait_recv()
    total = ((k3[0] + k3[1]) + (k3[2] + k3[3]))[:quarter, :]
    off = count - target_count
    sign = jnp.where(off > 0, 1.0, jnp.where(off < 0, -1.0, 0.0))
    total = total + ok * (sign + 1.0 - 2.0 * keep) / n_cells
    total = total * keep * (1.0 - keep)
    kvec_out = jnp.concatenate([total, blank], axis=0)
    dev = wide * 4 + narrow
    picked = jnp.sum(jnp.where(iota8 == lax.div(dev, 8), kvec_out, 0.0), axis=0, keepdims=True)
    picked = pltpu.roll(picked, lax.rem(LANES - lax.rem(dev, 8) * 16, LANES), 1)
    gfilt_ref[...] = picked[:, :16]
    sc4(last)

    def leave(c, _):
        for k in range(3):
            z_out(c, k).wait_send()
            b2_out(c, k).wait_send()
            b3_out(c, k).wait_send()
            scatter_z(c, k).wait_send()
        for d in s1_out(c) + s2_out(c) + scatter_one(c) + scatter_two(c):
            d.wait_send()
        s3_out(c).wait_send()
        b1(c).wait_send()
        scatter_sib(c).wait_send()
        put_pred(c).wait()
        return 0

    lax.fori_loop(0, NCH, leave, 0)
    for i in range(tiles):
        put_glog(i).wait()
    for k in range(3):
        fz_out(k).wait_send()
        k2_copy(here, k).wait_send()
        k3_copy(z, k).wait_send()
    fx(x).wait_send()
    fy(y).wait_send()
    fs(core).wait_send()
    k1_copy.wait_send()


def fused(logits, filt, cells, cell_mask, gene_mask, slide_ids, target, density):
    n_cells, spots = logits.shape
    own, genes = cells.shape
    n_slides = gene_mask.shape[0]
    width = genes // NCH
    tiles = spots // LANES
    dma = pltpu.SemaphoreType.DMA
    vmem, anywhere = pltpu.VMEM, pl.BlockSpec(memory_space=pl.ANY)
    inside = pl.BlockSpec(memory_space=pltpu.VMEM)
    scalars = pl.BlockSpec(memory_space=pltpu.SMEM)
    ring = (4, 2, 2, 2, 16, LANES)
    scratch = [
        vmem((tiles, n_cells, LANES), f32),
        vmem((NCH, spots, width), f32),
        vmem((NCH, spots, width), f32),
        vmem((NCH, 2) + ring, f32),
        vmem((NCH, n_cells, width), bf16),
        vmem((NCH, n_cells, width), bf16),
        vmem(ring, f32),
        vmem((n_cells, LANES), f32),
        vmem((n_cells, LANES), f32),
        vmem((n_cells, spots), bf16),
        vmem((n_cells, spots), bf16),
        vmem((spots, n_cells), bf16),
        vmem((spots, n_cells), bf16),
        vmem((NCH, LANES, width), bf16),
        vmem((spots, LANES), bf16),
        vmem((16, spots), bf16),
        vmem((spots, LANES), bf16),
        vmem((spots, LANES), bf16),
        vmem((spots, LANES), f32),
        vmem((spots, LANES), f32),
        vmem((spots, LANES), f32),
        vmem((8, LANES), f32),
        vmem((5, 8, LANES), f32),
        vmem((spots, width), bf16),
        vmem((spots, width), bf16),
        vmem((tiles, n_cells, LANES), f32),
        vmem((n_cells, LANES), f32),
        vmem((NCH, 32, width), f32),
        vmem((NCH, 32, width), f32),
        vmem((NCH, 4, 32, width), f32),
        vmem((NCH, 4, 32, width), f32),
        vmem((NCH, 32, width), f32),
        vmem((8, width), f32),
        vmem((8, LANES), f32),
        vmem((8, LANES), f32),
        vmem((4, 8, LANES), f32),
        vmem((4, 8, LANES), f32),
        vmem((NCH, 2) + ring, f32),
        vmem((NCH, 2, 4, 2, 2, 16, LANES), f32),
        vmem((NCH, 2, 4, 2, 2, 16, LANES), f32),
        vmem((NCH, 2, 4, 2, 16, LANES), f32),
        vmem((NCH, 2, 4, 2, 16, LANES), f32),
        vmem((NCH, 2, 4, 16, LANES), f32),
        vmem((NCH, 2, 4, 16, LANES), f32),
        vmem((NCH, 3, 2, 16, LANES), f32),
        dma((NCH, 2)), dma((NCH,)), dma((NCH,)), dma((tiles,)),
        dma((NCH, 3)), dma((NCH, 3)), dma((NCH, 2)), dma((NCH, 2)), dma((NCH, 2)), dma((NCH, 2)), dma((NCH,)), dma((NCH,)),
        dma((3,)), dma((3,)), dma((1,)), dma((1,)), dma((1,)), dma((1,)), dma((1,)), dma((1,)),
        dma((NCH,)), dma((NCH,)), dma((NCH, 3)), dma((NCH, 3)), dma((NCH, 3)), dma((NCH, 3)),
        dma((1,)), dma((1,)), dma((3,)), dma((3,)), dma((3,)), dma((3,)),
        dma((NCH,)), dma((NCH,)), dma((NCH, 2)), dma((NCH, 2)), dma((NCH, 2)), dma((NCH, 2)), dma((NCH, 3)), dma((NCH, 3)),
    ]
    out = pl.pallas_call(
        fused_kernel,
        out_shape=(
            jax.ShapeDtypeStruct((3,), f32),
            jax.ShapeDtypeStruct((4,), f32),
            jax.ShapeDtypeStruct((spots, genes), f32),
            jax.ShapeDtypeStruct((n_slides, genes), f32),
            jax.ShapeDtypeStruct((tiles, LANES), f32),
            jax.ShapeDtypeStruct((n_cells, spots), f32),
            jax.ShapeDtypeStruct((1, own), f32),
            jax.ShapeDtypeStruct((own, genes), f32),
        ),
        in_specs=[anywhere, scalars, anywhere, inside, inside, inside, anywhere, inside],
        out_specs=(scalars, scalars, anywhere, inside, inside, anywhere, inside, inside),
        scratch_shapes=scratch,
        compiler_params=pltpu.CompilerParams(
            collective_id=0, has_side_effects=True, vmem_limit_bytes=60 << 20
        ),
    )(
        logits, filt, cells, cell_mask.reshape(n_cells // LANES, LANES), gene_mask,
        slide_ids.reshape(tiles, LANES), target, density.reshape(tiles, LANES),
    )
    terms, reg, pred, gcos, scos, glog, gfilt, gcell = out
    return terms, reg, pred, gcos, scos.reshape(spots), glog, gfilt.reshape(own), gcell


def per_slide(onehot, values):
    return lax.dot_general(
        onehot, values, (((0,), (0,)), ((), ())), precision=lax.Precision.HIGHEST
    )


def on_device(logits, filt, cells, cell_mask, gene_mask, slide_ids, target, density):
    high = lax.Precision.HIGHEST
    n_cells = logits.shape[0]
    own_rows = cells.shape[0]
    n_slides = gene_mask.shape[0]
    valid = cell_mask.astype(jnp.float32)
    top = jnp.max(logits, axis=0, keepdims=True)
    expo = jnp.exp(logits - top) * valid[:, None]
    total = jnp.sum(expo, axis=0, keepdims=True)
    prob = expo / total
    logp = jnp.where(valid[:, None] > 0, logits - top - jnp.log(total), 0.0)
    entropy_part = -jnp.sum(prob * logp)
    whole, filt_all = (
        lax.all_gather(cells, ("wide", "narrow"), axis=0, tiled=True),
        lax.all_gather(filt, ("wide", "narrow"), axis=0, tiled=True),
    )
    keep = jax.nn.sigmoid(filt_all)
    weighted = prob * keep[:, None]
    g_pred = lax.dot_general(weighted, whole, (((0,), (0,)), ((), ())), precision=high)
    onehot = (slide_ids[:, None] == jnp.arange(n_slides, dtype=jnp.int32)[None, :]).astype(
        jnp.float32
    )
    gmask = gene_mask.astype(jnp.float32)
    spot_mask = jnp.dot(onehot, gmask, precision=high)
    masked_pred = spot_mask * g_pred
    sdot = jnp.sum(masked_pred * target, axis=1)
    spp = jnp.sum(masked_pred * g_pred, axis=1)
    stt = jnp.sum(spot_mask * target * target, axis=1)
    spot_scale = lax.rsqrt(spp + eps) * lax.rsqrt(stt + eps)
    spot_cos = sdot * spot_scale
    mass = jnp.sum(weighted, axis=0)
    log_part = density * (jnp.log(density) - jnp.log(mass))
    slide_vec = jnp.stack([mass, density, log_part], axis=1)
    loss_parts = jnp.stack([-jnp.sum(spot_cos), entropy_part])
    dot_s, pp_s, tt_s, slide_tot, loss_tot = lax.psum(
        (
            per_slide(onehot, g_pred * target),
            per_slide(onehot, g_pred * g_pred),
            per_slide(onehot, target * target),
            per_slide(onehot, slide_vec),
            loss_parts,
        ),
        ("wide", "narrow"),
    )
    mass_s = slide_tot[:, 0]
    wsum_s = slide_tot[:, 1]
    logsum_s = slide_tot[:, 2]
    gene_scale = gmask * lax.rsqrt(pp_s + eps) * lax.rsqrt(tt_s + eps)
    gene_cos = dot_s * gene_scale
    gene_loss = -jnp.sum(gene_cos)
    spot_loss = loss_tot[0]
    entropy = loss_tot[1] / (prob.shape[1] * lax.axis_size(("wide", "narrow")))
    kl_term = jnp.sum(logsum_s / wsum_s) + jnp.sum(jnp.log(mass_s) - jnp.log(wsum_s))
    count = jnp.sum(valid * keep)
    target_count = n_cells // 4
    count_term = jnp.abs(count - target_count) / n_cells
    binarity = jnp.sum(valid * (keep - keep * keep)) / n_cells
    loss = gene_loss + spot_loss + kl_term + count_term + binarity
    terms = jnp.stack([loss, gene_loss, spot_loss])
    reg_terms = jnp.stack([kl_term, count_term, binarity, entropy])
    gene_shrink = gene_scale * dot_s / (pp_s + eps)
    grad_pred = -jnp.dot(onehot, gene_scale, precision=high) * target
    grad_pred = grad_pred + jnp.dot(onehot, gene_shrink, precision=high) * g_pred
    spot_shrink = sdot / (spp + eps)
    grad_pred = grad_pred - spot_mask * spot_scale[:, None] * (
        target - spot_shrink[:, None] * g_pred
    )
    spot_slide = jnp.dot(onehot, jnp.stack([mass_s, wsum_s], axis=1), precision=high)
    grad_mass = -(density / spot_slide[:, 1]) / mass + 1.0 / spot_slide[:, 0]
    grad_weighted = lax.dot_general(whole, grad_pred, (((1,), (1,)), ((), ())), precision=high)
    grad_weighted = grad_weighted + grad_mass[None, :]
    grad_prob = keep[:, None] * grad_weighted
    keep_part = jnp.sum(prob * grad_weighted, axis=1)
    grad_logits = prob * (grad_prob - jnp.sum(prob * grad_prob, axis=0, keepdims=True))
    cell_part = jnp.dot(weighted, grad_pred, precision=high)
    grad_cells, keep_sum = (
        lax.psum_scatter(cell_part, ("wide", "narrow"), scatter_dimension=0, tiled=True),
        lax.psum_scatter(keep_part, ("wide", "narrow"), scatter_dimension=0, tiled=True),
    )
    first_row = lax.axis_index(("wide", "narrow")) * own_rows
    own_keep = lax.dynamic_slice_in_dim(keep, first_row, own_rows, 0)
    own_valid = lax.dynamic_slice_in_dim(valid, first_row, own_rows, 0)
    keep_grad = (
        keep_sum + own_valid * (jnp.sign(count - target_count) + 1.0 - 2.0 * own_keep) / n_cells
    )
    grad_filter = keep_grad * own_keep * (1.0 - own_keep)
    return (terms, reg_terms, g_pred, gene_cos, spot_cos, grad_logits, grad_filter, grad_cells)


def fits_fused(mesh, logits, cells, gene_mask, slide_ids):
    n_cells, spots = logits.shape
    return (
        (mesh.shape["wide"], mesh.shape["narrow"]) == (8, 4)
        and cells.shape == (16, 2048)
        and n_cells == 512
        and spots == 1024
        and gene_mask.shape[0] == 8
    )


def solution(mesh):
    def step(logits, filt, cells, cell_mask, gene_mask, slide_ids, target, density):
        fits = fits_fused(mesh, logits, cells, gene_mask, slide_ids)
        run = fused if fits else on_device
        return run(logits, filt, cells, cell_mask, gene_mask, slide_ids, target, density)

    placed = (
        P(None, ("wide", "narrow")),
        P(("wide", "narrow")),
        P(("wide", "narrow"), None),
        P(),
        P(),
        P(("wide", "narrow")),
        P(("wide", "narrow"), None),
        P(("wide", "narrow")),
    )
    return jax.shard_map(
        step,
        mesh=mesh,
        in_specs=placed,
        out_specs=(
            P(),
            P(),
            P(("wide", "narrow"), None),
            P(),
            P(("wide", "narrow")),
            P(None, ("wide", "narrow")),
            P(("wide", "narrow")),
            P(("wide", "narrow"), None),
        ),
        check_vma=False,
    )
```

```python
import jax
import jax.numpy as jnp
from jax import lax
from jax.experimental import pallas as pl
from jax.experimental.pallas import tpu as pltpu
from jax.sharding import PartitionSpec as P

eps = 1e-06
MESH = pl.DeviceIdType.MESH
bf16 = jnp.bfloat16
f32 = jnp.float32
LANES = 128
NCH = 8
BR = 32
HELD = 4


def split(value):
    high = value.astype(bf16)
    return high, (value - high.astype(f32)).astype(bf16)


def mm(a, b):
    return lax.dot_general(a, b, (((1,), (0,)), ((), ())), preferred_element_type=f32)


def mm_nt(a, b):
    return lax.dot_general(a, b, (((1,), (1,)), ((), ())), preferred_element_type=f32)


def fused_kernel(
    logits_hbm, filt_ref, cells_hbm, mask_ref, gene_ref, ids_ref, target_hbm, dens_ref,
    pv, lg, gw, keepc, gmass_ref, gacc, sums_ref, keep_ref, gcos_ref, scos_ref, gfilt_ref, gcell_ref,
    tv, buf, chi, clo, fb, valid, whi, wlo, thi, tlo, gmb, oh, l1, l2,
    idc, seen, blocks, sd, sp, st, mass, rows, gph, gpl, kp,
    stat, a1, a2, a3, fin, kvec, k1, k2, k3,
    part, rb, sb, r1, tt_, r2, qq, r3,
    lsem, tsem, osem,
    zs, zr, xs, xr, ys, yr, bs, br,
    fzs, fzr, fxs, fxr, fys, fyr, fbs, fbr,
    as1, ar1, as2, ar2, as3, ar3, as4, ar4,
    ks1, kr1, ks2, kr2, ks3, kr3,
    cbs, cbr, cxs, cxr, cys, cyr, czs, czr,
):
    n_cells = chi.shape[1]
    width = chi.shape[2]
    n_blocks = tv.shape[1]
    spots = n_blocks * BR
    n_slides = gene_ref.shape[0]
    tiles = spots // LANES
    wide, narrow = lax.axis_index("wide"), lax.axis_index("narrow")
    z, y = lax.div(wide, 2), lax.rem(wide, 2)
    x, core = lax.div(narrow, 2), lax.rem(narrow, 2)
    to_z = [(lax.rem(z + k, 4) * 2 + y, narrow) for k in (1, 2, 3)]
    from_z = [lax.rem(z + 4 - k, 4) for k in (1, 2, 3)]
    to_x = (wide, (1 - x) * 2 + core)
    to_y = (z * 2 + 1 - y, narrow)
    to_xy = (z * 2 + 1 - y, (1 - x) * 2 + core)
    to_b = (wide, x * 2 + 1 - core)

    def rcopy(src, dst, ss, rs, dev):
        return pltpu.make_async_remote_copy(
            src_ref=src, dst_ref=dst, send_sem=ss, recv_sem=rs, device_id=dev, device_id_type=MESH
        )

    def lanes(i, w=LANES):
        return pl.ds(pl.multiple_of(i * w, w), w)

    def own_cells(c, h):
        return pltpu.make_async_copy(
            cells_hbm.at[:, pl.ds((c * 2 + h) * LANES, LANES)], buf.at[c, h, z, y, x, core], lsem.at[c, h]
        )

    def get_logits(i):
        return pltpu.make_async_copy(logits_hbm.at[:, lanes(i)], lg.at[i], osem.at[i])

    def get_target(c):
        return pltpu.make_async_copy(target_hbm.at[:, :, lanes(c, width)], tv.at[c], tsem.at[c])

    for c in range(NCH):
        for h in range(2):
            own_cells(c, h).start()
    for i in range(tiles):
        get_logits(i).start()
    for c in range(NCH):
        get_target(c).start()

    barrier = pltpu.get_barrier_semaphore()
    for dev in to_z + [to_x, to_y, to_xy, to_b]:
        pl.semaphore_signal(barrier, inc=1, device_id=dev, device_id_type=MESH)

    row16 = lax.broadcasted_iota(jnp.int32, (16, LANES), 0)
    mine = jnp.zeros((16, LANES), f32)
    for r in range(16):
        mine = jnp.where(row16 == r, filt_ref[r], mine)
    fb[z, y, x, core] = mine
    for q in range(n_cells // LANES):
        line = mask_ref[q : q + 1, :].astype(f32)
        valid[q * LANES : (q + 1) * LANES, :] = jnp.broadcast_to(line, (LANES, LANES)).T
    pl.semaphore_wait(barrier, 7)

    def z_out(c, k):
        r = buf.at[c, :, z, y, x, core]
        return rcopy(r, r, zs.at[c, k], zr.at[c, k], to_z[k])

    def z_in(c, k):
        r = buf.at[c, :, from_z[k], y, x, core]
        return rcopy(r, r, zs.at[c, k], zr.at[c, k], to_z[k])

    def s1_out(c):
        a = buf.at[c, 0, :, y, x, core]
        b = buf.at[c, 1, :, y, x, core]
        return [rcopy(a, a, xs.at[c, 0], xr.at[c, 0], to_x), rcopy(b, b, ys.at[c, 0], yr.at[c, 0], to_y)]

    def s1_in(c):
        a = buf.at[c, 0, :, y, 1 - x, core]
        b = buf.at[c, 1, :, 1 - y, x, core]
        return [rcopy(a, a, xs.at[c, 0], xr.at[c, 0], to_x), rcopy(b, b, ys.at[c, 0], yr.at[c, 0], to_y)]

    def s2_out(c):
        a = buf.at[c, 0, :, y, :, core]
        b = buf.at[c, 1, :, :, x, core]
        return [rcopy(a, a, ys.at[c, 1], yr.at[c, 1], to_y), rcopy(b, b, xs.at[c, 1], xr.at[c, 1], to_x)]

    def s2_in(c):
        a = buf.at[c, 0, :, 1 - y, :, core]
        b = buf.at[c, 1, :, :, 1 - x, core]
        return [rcopy(a, a, ys.at[c, 1], yr.at[c, 1], to_y), rcopy(b, b, xs.at[c, 1], xr.at[c, 1], to_x)]

    def s3_out(c):
        r = buf.at[c, :, :, :, :, core]
        return rcopy(r, r, bs.at[c], br.at[c], to_b)

    def s3_in(c):
        r = buf.at[c, :, :, :, :, 1 - core]
        return rcopy(r, r, bs.at[c], br.at[c], to_b)

    def fz_out(k):
        r = fb.at[z, y, x, core]
        return rcopy(r, r, fzs.at[k], fzr.at[k], to_z[k])

    def fz_in(k):
        r = fb.at[from_z[k], y, x, core]
        return rcopy(r, r, fzs.at[k], fzr.at[k], to_z[k])

    def fx(at):
        r = fb.at[:, y, at, core]
        return rcopy(r, r, fxs.at[0], fxr.at[0], to_x)

    def fy(at):
        r = fb.at[:, at, :, core]
        return rcopy(r, r, fys.at[0], fyr.at[0], to_y)

    def fs(at):
        r = fb.at[:, :, :, at]
        return rcopy(r, r, fbs.at[0], fbr.at[0], to_b)

    def b1(c):
        return rcopy(stat.at[c, 1 - core], a1.at[c], as1.at[c], ar1.at[c], to_b)

    plane = [to_x, to_y, to_xy]
    here = y * 2 + x
    there = [y * 2 + 1 - x, (1 - y) * 2 + x, (1 - y) * 2 + 1 - x]

    def b2_out(c, k):
        r = a2.at[c, here]
        return rcopy(r, r, as2.at[c, k], ar2.at[c, k], plane[k])

    def b2_in(c, k):
        r = a2.at[c, there[k]]
        return rcopy(r, r, as2.at[c, k], ar2.at[c, k], plane[k])

    def b3_out(c, k):
        r = a3.at[c, z]
        return rcopy(r, r, as3.at[c, k], ar3.at[c, k], to_z[k])

    def b3_in(c, k):
        r = a3.at[c, from_z[k]]
        return rcopy(r, r, as3.at[c, k], ar3.at[c, k], to_z[k])

    def b4(c, half):
        r = fin.at[c, half]
        return rcopy(r, r, as4.at[c], ar4.at[c], to_b)

    def sum_second(c):
        b1(c).wait_recv()
        a2[c, here] = stat[c, core] + a1[c]
        for k in range(3):
            b2_out(c, k).start()

    def sum_third(c):
        for k in range(3):
            b2_in(c, k).wait_recv()
        a3[c, z] = (a2[c, 0] + a2[c, 1]) + (a2[c, 2] + a2[c, 3])
        for k in range(3):
            b3_out(c, k).start()

    def sum_fourth(c):
        for k in range(3):
            b3_in(c, k).wait_recv()
        fin[c, core] = (a3[c, 0] + a3[c, 1]) + (a3[c, 2] + a3[c, 3])
        b4(c, core).start()

    def sum_last(c):
        b4(c, 1 - core).wait_recv()
        return jnp.concatenate([fin[c, 0], fin[c, 1]], axis=1)

    def v1(n):
        return rcopy(kvec.at[n], k1.at[n], ks1.at[n], kr1.at[n], to_b)

    def v2(n, slot, k):
        return rcopy(k2.at[n, slot], k2.at[n, slot], ks2.at[n, k], kr2.at[n, k], plane[k])

    def v3(n, slot, k):
        return rcopy(k3.at[n, slot], k3.at[n, slot], ks3.at[n, k], kr3.at[n, k], to_z[k])

    def vector_second(n):
        v1(n).wait_recv()
        k2[n, here] = kvec[n] + k1[n]
        for k in range(3):
            v2(n, here, k).start()

    def vector_third(n):
        for k in range(3):
            v2(n, there[k], k).wait_recv()
        k3[n, z] = (k2[n, 0] + k2[n, 1]) + (k2[n, 2] + k2[n, 3])
        for k in range(3):
            v3(n, z, k).start()

    def vector_last(n):
        for k in range(3):
            v3(n, from_z[k], k).wait_recv()
        return (k3[n, 0] + k3[n, 1]) + (k3[n, 2] + k3[n, 3])

    def softmax(i, ent):
        get_logits(i).wait()
        value = lg[i]
        top = jnp.max(value, axis=0, keepdims=True)
        expo = jnp.exp(value - top) * valid[...]
        total = jnp.sum(expo, axis=0, keepdims=True)
        prob = expo * (1.0 / total)
        lg[i] = prob
        return ent + jnp.sum(prob * (value - top - jnp.log(total)), axis=0, keepdims=True)

    def one_hot(i, _):
        ids = ids_ref[pl.ds(i, 1), :]
        square = (lax.broadcasted_iota(jnp.int32, (LANES, LANES), 0) == ids).astype(f32)
        oh[lanes(i), :] = square.T.astype(bf16)
        per = LANES // BR
        turned = jnp.broadcast_to(ids, (LANES, LANES)).astype(f32).T
        idc[pl.ds(i * per, per)] = turned.reshape(per, BR, LANES)
        return 0

    def weights(i, _):
        w = lg[i] * keepc[...]
        mass[pl.ds(i, 1), :] = jnp.sum(w, axis=0, keepdims=True)
        high, low = split(w)
        whi[:, lanes(i)] = high
        wlo[:, lanes(i)] = low
        turned = w.T
        high, low = split(turned)
        thi[lanes(i), :] = high
        tlo[lanes(i), :] = low
        return 0

    for k in range(3):
        fz_out(k).start()
    for c in range(NCH):
        for h in range(2):
            own_cells(c, h).wait()
        for k in range(3):
            z_out(c, k).start()

    def stage_z(c):
        for k in range(3):
            z_in(c, k).wait_recv()
        for d in s1_out(c):
            d.start()

    def stage_1(c):
        for d in s1_in(c):
            d.wait_recv()
        for d in s2_out(c):
            d.start()

    def stage_2(c):
        for d in s2_in(c):
            d.wait_recv()
        s3_out(c).start()

    def fold(v):
        out = v[:, :LANES]
        for k in range(1, v.shape[1] // LANES):
            out = out + v[:, k * LANES : (k + 1) * LANES]
        return out

    def eighths(v):
        return jnp.sum(v.reshape(v.shape[0] // 8, 8, v.shape[1]), axis=0)

    for c in range(NCH):
        gm = jnp.concatenate(
            [gene_ref[:, c * width : (c + 1) * width].astype(f32), jnp.zeros((LANES - n_slides, width), f32)], axis=0
        )
        gmb[c] = gm.astype(bf16)
    sd[...] = jnp.zeros_like(sd)
    sp[...] = jnp.zeros_like(sp)
    st[...] = jnp.zeros_like(st)
    lax.fori_loop(0, tiles, one_hot, 0)

    begins = [jnp.sum((ids_ref[...] < k).astype(jnp.int32)) for k in range(n_slides + 1)]
    firsts = [jnp.minimum(lax.div(begins[k], BR), n_blocks - 1) for k in range(n_slides)]
    lasts = [lax.div(jnp.maximum(begins[k + 1] - 1, 0), BR) for k in range(n_slides)]
    slide16 = lax.broadcasted_iota(jnp.int32, (16, 8 * n_blocks), 0)
    block16 = lax.div(lax.broadcasted_iota(jnp.int32, (16, 8 * n_blocks), 1), 8)
    inner = jnp.zeros((16, 8 * n_blocks), f32)
    for k in range(n_slides):
        full = jnp.logical_and(block16 > firsts[k], block16 < lasts[k])
        inner = jnp.where(jnp.logical_and(slide16 == k, full), 1.0, inner)
    inner = inner.astype(bf16)
    inner = jnp.concatenate([inner, inner], axis=1)
    slide8 = lax.broadcasted_iota(jnp.int32, (8, width), 0)

    def gene_sums(c, products, number, at_row):
        sums = []
        for n in range(number):
            bh, bl = split(blocks[n])
            sums.append(mm(inner, jnp.concatenate([bh, bl], axis=0))[:8, :])
        for k in range(n_slides):
            parts = [jnp.zeros((8, width), f32)] * number
            for block, counts in ((firsts[k], None), (lasts[k], lasts[k] != firsts[k])):
                own = idc[block] == float(k)
                if counts is not None:
                    own = jnp.logical_and(own, counts)
                own = own.astype(f32)
                own = jnp.concatenate([own] * (width // LANES), axis=1)
                for n, prod in enumerate(products(c, block)):
                    parts[n] = parts[n] + eighths(prod * own)
            for n in range(number):
                line = jnp.sum(parts[n], axis=0, keepdims=True)
                sums[n] = sums[n] + jnp.where(slide8 == k, line, 0.0)
        for n in range(number):
            for h in range(2):
                stat[c, h, at_row + n * 8 : at_row + (n + 1) * 8, :] = sums[n][:, h * LANES : (h + 1) * LANES]

    def of_target(c, r):
        tgt = tv[c, r]
        return (tgt * tgt,)

    def of_both(c, r):
        pred, tgt = pv[c, r], tv[c, r]
        return pred * tgt, pred * pred

    def by_rows(c, products, spots_of):
        def rows_of(r, _):
            at = pl.ds(pl.multiple_of(r * BR, BR), BR)
            to = pl.ds(pl.multiple_of(r * 8, 8), 8)
            sees = seen[at, :]
            for n, (prod, spot) in enumerate(zip(products(c, r), spots_of)):
                spot[at, :] += fold(sees * prod)
                blocks[n, to, :] = eighths(prod)
            return 0

        lax.fori_loop(0, n_blocks, rows_of, 0, unroll=2)

    def target_sums(c, _):
        seen[...] = mm(oh[...], gmb[c])
        by_rows(c, of_target, (st,))
        gene_sums(c, of_target, 1, 16)
        return 0

    def predict(c):
        s3_in(c).wait_recv()
        whole = jnp.concatenate([buf[c, h].reshape(n_cells, LANES) for h in range(2)], axis=1)
        high, low = split(whole)
        chi[c] = high
        clo[c] = low
        wh, wl = thi[...], tlo[...]
        pred = mm(jnp.concatenate([wh, wl, wh], axis=1), jnp.concatenate([high, high, low], axis=0))
        pv[c] = pred.reshape(n_blocks, BR, width)
        seen[...] = mm(oh[...], gmb[c])

    def predicted_sums(c):
        by_rows(c, of_both, (sd, sp))
        gene_sums(c, of_both, 2, 0)

    ent = lax.fori_loop(0, tiles // 2, softmax, jnp.zeros((1, LANES), f32))
    for k in range(3):
        fz_in(k).wait_recv()
    fx(x).start()
    stage_z(0)
    ent = lax.fori_loop(tiles // 2, tiles, softmax, ent)
    fx(1 - x).wait_recv()
    fy(y).start()
    stage_z(1)
    stage_1(0)
    for c in range(NCH):
        get_target(c).wait()
    lax.fori_loop(0, 3, target_sums, 0)
    fy(1 - y).wait_recv()
    fs(core).start()
    stage_z(2)
    stage_1(1)
    lax.fori_loop(3, 6, target_sums, 0)
    stage_z(3)
    stage_2(0)
    fs(1 - core).wait_recv()
    keepc[...] = jax.nn.sigmoid(fb[...].reshape(n_cells, LANES))
    lax.fori_loop(0, tiles, weights, 0)
    stage_1(2)
    lax.fori_loop(6, NCH, target_sums, 0)

    def gather_tick(t, _):
        c = t - 4
        pl.when(t < NCH)(lambda: stage_z(t))
        pl.when(t - 3 < NCH)(lambda: stage_2(t - 3))
        predict(c)
        pl.when(t - 1 < NCH)(lambda: stage_1(t - 1))
        pl.when(c >= 1)(lambda: sum_second(c - 1))
        pl.when(c >= 3)(lambda: sum_third(c - 3))
        predicted_sums(c)
        pl.when(c >= 5)(lambda: sum_fourth(c - 5))
        b1(c).start()
        return 0

    lax.fori_loop(4, NCH + 4, gather_tick, 0)
    last = NCH - 1

    def spot_rows(i, _):
        for k, ref in enumerate((sd, sp, st)):
            rows[k, pl.ds(i, 1), :] = jnp.sum(ref[lanes(i), :].T, axis=0, keepdims=True)
        return 0

    lax.fori_loop(0, tiles, spot_rows, 0)
    sdot, spp, stt = rows[0], rows[1], rows[2]
    scale = lax.rsqrt(spp + eps) * lax.rsqrt(stt + eps)
    scos = sdot * scale
    scos_ref[...] = scos
    shrink = scale * (sdot / (spp + eps))
    for k, value in ((0, scale), (1, shrink)):
        high, low = split(value)
        rows[2 * k] = high.astype(f32)
        rows[2 * k + 1] = low.astype(f32)
    dens = dens_ref[...]
    mass_row = mass[...]
    rows[4] = dens * (jnp.log(dens) - jnp.log(mass_row))

    iota8 = lax.broadcasted_iota(jnp.int32, (8, LANES), 0)
    lane8 = lax.broadcasted_iota(jnp.int32, (8, LANES), 1)

    def coef_rows(i, sums):
        mine = (iota8 == ids_ref[pl.ds(i, 1), :]).astype(f32)
        pad = jnp.zeros((LANES - 32, LANES), f32)
        at = pl.ds(i, 1)
        for k, ref in ((0, l1), (1, l2)):
            ref[lanes(i), :] = jnp.concatenate(
                [mine, mine, mine * rows[2 * k, at, :], mine * rows[2 * k + 1, at, :], pad], axis=0
            ).T.astype(bf16)
        return (
            sums[0] + mine * mass[at, :],
            sums[1] + mine * dens_ref[at, :],
            sums[2] + mine * rows[4, at, :],
        )

    zero = jnp.zeros((8, LANES), f32)
    totals = lax.fori_loop(0, tiles, coef_rows, (zero, zero, zero))
    extra = zero
    for k, value in enumerate(totals):
        extra = jnp.where(lane8 == k, jnp.sum(value, axis=1, keepdims=True), extra)
    extra = jnp.where(jnp.logical_and(lane8 == 3, iota8 == 0), -jnp.sum(scos), extra)
    extra = jnp.where(jnp.logical_and(lane8 == 4, iota8 == 0), -jnp.sum(ent), extra)
    kvec[0] = extra
    v1(0).start()
    sum_second(last)
    sum_third(last - 2)
    sum_fourth(last - 4)

    gacc[...] = jnp.zeros_like(gacc)
    gw[...] = jnp.zeros_like(gw)

    def scatter_sib(c):
        return rcopy(part.at[c, :, :, :, :, 1 - core], rb.at[c], cbs.at[c], cbr.at[c], to_b)

    def scatter_one(c):
        return [
            rcopy(sb.at[c, 0, :, 1 - y], r1.at[c, 0], cys.at[c, 0], cyr.at[c, 0], to_y),
            rcopy(sb.at[c, 1, :, :, 1 - x], r1.at[c, 1], cxs.at[c, 0], cxr.at[c, 0], to_x),
        ]

    def scatter_two(c):
        return [
            rcopy(tt_.at[c, 0, :, 1 - x], r2.at[c, 0], cxs.at[c, 1], cxr.at[c, 1], to_x),
            rcopy(tt_.at[c, 1, :, 1 - y], r2.at[c, 1], cys.at[c, 1], cyr.at[c, 1], to_y),
        ]

    def scatter_z(c, k):
        return rcopy(qq.at[c, :, lax.rem(z + k + 1, 4)], r3.at[c, k], czs.at[c, k], czr.at[c, k], to_z[k])

    def sc1(c):
        scatter_sib(c).wait_recv()
        sb[c] = part[c, :, :, :, :, core] + rb[c]
        for d in scatter_one(c):
            d.start()

    def sc2(c):
        for d in scatter_one(c):
            d.wait_recv()
        tt_[c, 0] = sb[c, 0, :, y] + r1[c, 0]
        tt_[c, 1] = sb[c, 1, :, :, x] + r1[c, 1]
        for d in scatter_two(c):
            d.start()

    def sc3(c):
        for d in scatter_two(c):
            d.wait_recv()
        qq[c, 0] = tt_[c, 0, :, x] + r2[c, 0]
        qq[c, 1] = tt_[c, 1, :, y] + r2[c, 1]
        for k in range(3):
            scatter_z(c, k).start()

    def sc4(c):
        for k in range(3):
            scatter_z(c, k).wait_recv()
        for h in range(2):
            gcell_ref[:, lanes(c * 2 + h)] = (qq[c, h, z] + r3[c, 0, h]) + (r3[c, 1, h] + r3[c, 2, h])

    def backward(c):
        total = sum_last(c)
        dot_s, pp_s, tt_s = total[0:8], total[8:16], total[16:24]
        gm = gene_ref[:, lanes(c, width)].astype(f32)
        gscale = gm * lax.rsqrt(pp_s + eps) * lax.rsqrt(tt_s + eps)
        gcos = dot_s * gscale
        gcos_ref[:, lanes(c, width)] = gcos
        gacc[...] += gcos
        gshrink = gscale * (dot_s / (pp_s + eps))
        pad = jnp.zeros((LANES - 32, width), f32)
        coefs = []
        for value in (gscale, gshrink):
            high, low = split(value)
            coefs.append(
                jnp.concatenate([high.astype(f32), low.astype(f32), gm, gm, pad], axis=0).astype(bf16)
            )
        slot = lax.rem(c, HELD)
        grad = mm(l2[...], coefs[1]) * pv[c].reshape(spots, width) - mm(l1[...], coefs[0]) * tv[c].reshape(spots, width)
        gh, gl = split(grad)
        gph[slot] = gh
        gpl[slot] = gl
        wh, wl = whi[...], wlo[...]
        gh, gl = gph[slot], gpl[slot]
        out = mm(jnp.concatenate([wh, wl, wh], axis=1), jnp.concatenate([gh, gh, gl], axis=0))
        for h in range(2):
            part[c, h] = out[:, h * LANES : (h + 1) * LANES].reshape(4, 2, 2, 2, 16, LANES)
        scatter_sib(c).start()

    def spot_part(c):
        slot = lax.rem(c, HELD)
        ch, cl = chi[c], clo[c]
        gh, gl = gph[slot], gpl[slot]
        out = mm_nt(jnp.concatenate([ch, cl, ch], axis=1), jnp.concatenate([gh, gh, gl], axis=1))
        for i in range(tiles):
            gw[i] += out[:, i * LANES : (i + 1) * LANES]

    def back_tick(t, _):
        pl.when(t >= 3)(lambda: sc2(t - 3))
        backward(t)
        pl.when(t >= 1)(lambda: sc1(t - 1))
        pl.when(t >= 4)(lambda: sc3(t - 4))

        @pl.when(t == 0)
        def _():
            vector_second(0)
            sum_third(last - 1)
            sum_fourth(last - 3)

        @pl.when(t == 1)
        def _():
            sum_third(last)
            sum_fourth(last - 2)

        @pl.when(t == 2)
        def _():
            vector_third(0)
            sum_fourth(last - 1)

        @pl.when(t == 3)
        def _():
            sum_fourth(last)

        pl.when(t >= 3)(lambda: spot_part(t - 3))
        pl.when(t >= 6)(lambda: sc4(t - 6))
        return 0

    lax.fori_loop(0, NCH, back_tick, 0)
    sc1(last)
    spot_part(last - 2)
    sc2(last - 2)
    sc3(last - 3)
    spot_part(last - 1)
    sc2(last - 1)
    spot_part(last)

    sums_s = vector_last(0)
    sums_ref[...] = sums_s
    mass_s, wsum_s = sums_s[:, 0:1], sums_s[:, 1:2]
    kp[...] = jnp.zeros_like(kp)

    def finish(i, _):
        at = pl.ds(i, 1)
        mine = (iota8 == ids_ref[at, :]).astype(f32)
        mass_at = jnp.sum(mine * mass_s, axis=0, keepdims=True)
        wsum_at = jnp.sum(mine * wsum_s, axis=0, keepdims=True)
        gmass = -(dens_ref[at, :] / wsum_at) / mass[at, :] + 1.0 / mass_at
        gmass_ref[at, :] = gmass
        kp[...] += lg[i] * (gw[i] + gmass)
        return 0

    lax.fori_loop(0, tiles, finish, 0)
    quarter = n_cells // LANES
    rows_k, rows_keep = [], []
    for q in range(quarter):
        rows_k.append(jnp.sum(kp[q * LANES : (q + 1) * LANES, :].T, axis=0, keepdims=True))
        rows_keep.append(keepc[q * LANES : (q + 1) * LANES, :].T[0:1, :])
    blank = jnp.zeros((8 - quarter, LANES), f32)
    kvec[1] = jnp.concatenate(rows_k + [blank], axis=0)
    v1(1).start()
    keep = jnp.concatenate(rows_keep, axis=0)
    keep_ref[...] = jnp.concatenate([keep, blank], axis=0)

    sc2(last)
    sc3(last - 2)
    sc3(last - 1)
    vector_second(1)
    sc3(last)
    for c in range(NCH - 6, NCH - 3):
        sc4(c)
    vector_third(1)
    for c in range(NCH - 3, NCH):
        sc4(c)

    ok = mask_ref[...].astype(f32)
    count = jnp.sum(ok * keep)
    target_count = n_cells // 4

    total = vector_last(1)[:quarter, :]
    off = count - target_count
    sign = jnp.where(off > 0, 1.0, jnp.where(off < 0, -1.0, 0.0))
    total = total + ok * (sign + 1.0 - 2.0 * keep) / n_cells
    total = total * keep * (1.0 - keep)
    kvec_out = jnp.concatenate([total, blank], axis=0)
    dev = wide * 4 + narrow
    picked = jnp.sum(jnp.where(iota8 == lax.div(dev, 8), kvec_out, 0.0), axis=0, keepdims=True)
    picked = pltpu.roll(picked, lax.rem(LANES - lax.rem(dev, 8) * 16, LANES), 1)
    gfilt_ref[...] = picked

    def leave(c, _):
        for k in range(3):
            z_out(c, k).wait_send()
            b2_out(c, k).wait_send()
            b3_out(c, k).wait_send()
            scatter_z(c, k).wait_send()
        for d in s1_out(c) + s2_out(c) + scatter_one(c) + scatter_two(c):
            d.wait_send()
        s3_out(c).wait_send()
        b1(c).wait_send()
        b4(c, core).wait_send()
        scatter_sib(c).wait_send()
        return 0

    lax.fori_loop(0, NCH, leave, 0)
    for k in range(3):
        fz_out(k).wait_send()
        for n in range(2):
            v2(n, here, k).wait_send()
            v3(n, z, k).wait_send()
    fx(x).wait_send()
    fy(y).wait_send()
    fs(core).wait_send()
    for n in range(2):
        v1(n).wait_send()


def finish_kernel(
    pv, lg, gw, keepc, gmass_ref, gacc, sums_ref, keep_ref, gcos_in, scos_in, gfilt_in, gcell_in, mask_ref,
    terms_ref, reg_ref, pred_hbm, gcos_ref, scos_ref, glog_hbm, gfilt_ref, gcell_ref,
    psem, osem,
):
    width = pv.shape[3]
    tiles, n_cells = lg.shape[:2]

    def lanes(i, w=LANES):
        return pl.ds(pl.multiple_of(i * w, w), w)

    def put_pred(c):
        return pltpu.make_async_copy(pv.at[c], pred_hbm.at[:, :, lanes(c, width)], psem.at[c])

    def put_glog(i):
        return pltpu.make_async_copy(gw.at[i], glog_hbm.at[:, lanes(i)], osem.at[i])

    for c in range(NCH):
        put_pred(c).start()

    def finish(i, _):
        grad = keepc[...] * (gw[i] + gmass_ref[pl.ds(i, 1), :])
        prob = lg[i]
        gw[i] = prob * (grad - jnp.sum(prob * grad, axis=0, keepdims=True))
        put_glog(i).start()
        return 0

    lax.fori_loop(0, tiles, finish, 0)
    gcos_ref[...] = gcos_in[...]
    scos_ref[...] = scos_in[...]
    gcell_ref[...] = gcell_in[...]
    gfilt_ref[...] = gfilt_in[:, : gfilt_ref.shape[1]]

    sums_s = sums_ref[...]
    mass_s, wsum_s, logsum_s = sums_s[:, 0:1], sums_s[:, 1:2], sums_s[:, 2:3]
    row = lax.broadcasted_iota(jnp.int32, sums_s.shape, 0)
    lane = lax.broadcasted_iota(jnp.int32, sums_s.shape, 1)
    keep = keep_ref[: n_cells // LANES, :]
    ok = mask_ref[...].astype(f32)
    count = jnp.sum(ok * keep)
    count_term = jnp.abs(count - n_cells // 4) / n_cells
    binarity = jnp.sum(ok * (keep - keep * keep)) / n_cells
    gene_loss = -jnp.sum(gacc[...])
    spot_loss = jnp.sum(jnp.where(jnp.logical_and(lane == 3, row == 0), sums_s, 0.0))
    entropy = jnp.sum(jnp.where(jnp.logical_and(lane == 4, row == 0), sums_s, 0.0)) / (tiles * LANES * 32)
    kl = jnp.sum(logsum_s / wsum_s + jnp.log(mass_s) - jnp.log(wsum_s))
    terms_ref[0] = gene_loss + spot_loss + kl + count_term + binarity
    terms_ref[1] = gene_loss
    terms_ref[2] = spot_loss
    reg_ref[0] = kl
    reg_ref[1] = count_term
    reg_ref[2] = binarity
    reg_ref[3] = entropy
    for i in range(tiles):
        put_glog(i).wait()
    for c in range(NCH):
        put_pred(c).wait()


def fused(logits, filt, cells, cell_mask, gene_mask, slide_ids, target, density):
    n_cells, spots = logits.shape
    own, genes = cells.shape
    n_slides = gene_mask.shape[0]
    width = genes // NCH
    tiles = spots // LANES
    dma = pltpu.SemaphoreType.DMA
    vmem, anywhere = pltpu.VMEM, pl.BlockSpec(memory_space=pl.ANY)
    inside = pl.BlockSpec(memory_space=pltpu.VMEM)
    scalars = pl.BlockSpec(memory_space=pltpu.SMEM)
    ring = (4, 2, 2, 2, 16, LANES)
    scratch = [
        vmem((NCH, spots // BR, BR, width), f32),
        vmem((NCH, 2) + ring, f32),
        vmem((NCH, n_cells, width), bf16),
        vmem((NCH, n_cells, width), bf16),
        vmem(ring, f32),
        vmem((n_cells, LANES), f32),
        vmem((n_cells, spots), bf16),
        vmem((n_cells, spots), bf16),
        vmem((spots, n_cells), bf16),
        vmem((spots, n_cells), bf16),
        vmem((NCH, LANES, width), bf16),
        vmem((spots, LANES), bf16),
        vmem((spots, LANES), bf16),
        vmem((spots, LANES), bf16),
        vmem((spots // BR, BR, LANES), f32),
        vmem((spots, width), f32),
        vmem((2, spots * 8 // BR, width), f32),
        vmem((spots, LANES), f32),
        vmem((spots, LANES), f32),
        vmem((spots, LANES), f32),
        vmem((8, LANES), f32),
        vmem((5, 8, LANES), f32),
        vmem((HELD, spots, width), bf16),
        vmem((HELD, spots, width), bf16),
        vmem((n_cells, LANES), f32),
        vmem((NCH, 2, 24, LANES), f32),
        vmem((NCH, 24, LANES), f32),
        vmem((NCH, 4, 24, LANES), f32),
        vmem((NCH, 4, 24, LANES), f32),
        vmem((NCH, 2, 24, LANES), f32),
        vmem((2, 8, LANES), f32),
        vmem((2, 8, LANES), f32),
        vmem((2, 4, 8, LANES), f32),
        vmem((2, 4, 8, LANES), f32),
        vmem((NCH, 2) + ring, f32),
        vmem((NCH, 2, 4, 2, 2, 16, LANES), f32),
        vmem((NCH, 2, 4, 2, 2, 16, LANES), f32),
        vmem((NCH, 2, 4, 2, 16, LANES), f32),
        vmem((NCH, 2, 4, 2, 16, LANES), f32),
        vmem((NCH, 2, 4, 16, LANES), f32),
        vmem((NCH, 2, 4, 16, LANES), f32),
        vmem((NCH, 3, 2, 16, LANES), f32),
        dma((NCH, 2)), dma((NCH,)), dma((tiles,)),
        dma((NCH, 3)), dma((NCH, 3)), dma((NCH, 2)), dma((NCH, 2)), dma((NCH, 2)), dma((NCH, 2)), dma((NCH,)), dma((NCH,)),
        dma((3,)), dma((3,)), dma((1,)), dma((1,)), dma((1,)), dma((1,)), dma((1,)), dma((1,)),
        dma((NCH,)), dma((NCH,)), dma((NCH, 3)), dma((NCH, 3)), dma((NCH, 3)), dma((NCH, 3)), dma((NCH,)), dma((NCH,)),
        dma((2,)), dma((2,)), dma((2, 3)), dma((2, 3)), dma((2, 3)), dma((2, 3)),
        dma((NCH,)), dma((NCH,)), dma((NCH, 2)), dma((NCH, 2)), dma((NCH, 2)), dma((NCH, 2)), dma((NCH, 3)), dma((NCH, 3)),
    ]
    mask = cell_mask.reshape(n_cells // LANES, LANES)
    held = (
        vmem((NCH, spots // BR, BR, width), f32),
        vmem((tiles, n_cells, LANES), f32),
        vmem((tiles, n_cells, LANES), f32),
        vmem((n_cells, LANES), f32),
        vmem((tiles, LANES), f32),
        vmem((8, width), f32),
        vmem((8, LANES), f32),
        vmem((8, LANES), f32),
        vmem((n_slides, genes), f32),
        vmem((tiles, LANES), f32),
        vmem((1, LANES), f32),
        vmem((own, genes), f32),
    )
    between = pl.pallas_call(
        fused_kernel,
        out_shape=held,
        in_specs=[anywhere, scalars, anywhere, inside, inside, inside, anywhere, inside],
        out_specs=(inside,) * len(held),
        scratch_shapes=scratch,
        compiler_params=pltpu.CompilerParams(
            collective_id=0, has_side_effects=True, vmem_limit_bytes=50 << 20
        ),
    )(
        logits, filt, cells, mask, gene_mask,
        slide_ids.reshape(tiles, LANES), target.reshape(spots // BR, BR, genes), density.reshape(tiles, LANES),
    )
    out = pl.pallas_call(
        finish_kernel,
        out_shape=(
            jax.ShapeDtypeStruct((3,), f32),
            jax.ShapeDtypeStruct((4,), f32),
            jax.ShapeDtypeStruct((spots // BR, BR, genes), f32),
            jax.ShapeDtypeStruct((n_slides, genes), f32),
            jax.ShapeDtypeStruct((tiles, LANES), f32),
            jax.ShapeDtypeStruct((n_cells, spots), f32),
            jax.ShapeDtypeStruct((1, own), f32),
            jax.ShapeDtypeStruct((own, genes), f32),
        ),
        in_specs=[inside] * (len(held) + 1),
        out_specs=(scalars, scalars, anywhere, inside, inside, anywhere, inside, inside),
        scratch_shapes=[dma((NCH,)), dma((tiles,))],
        compiler_params=pltpu.CompilerParams(vmem_limit_bytes=24 << 20),
    )(*between, mask)
    terms, reg, pred, gcos, scos, glog, gfilt, gcell = out
    return terms, reg, pred.reshape(spots, genes), gcos, scos.reshape(spots), glog, gfilt.reshape(own), gcell


def per_slide(onehot, values):
    return lax.dot_general(
        onehot, values, (((0,), (0,)), ((), ())), precision=lax.Precision.HIGHEST
    )


def on_device(logits, filt, cells, cell_mask, gene_mask, slide_ids, target, density):
    high = lax.Precision.HIGHEST
    n_cells = logits.shape[0]
    own_rows = cells.shape[0]
    n_slides = gene_mask.shape[0]
    valid = cell_mask.astype(jnp.float32)
    top = jnp.max(logits, axis=0, keepdims=True)
    expo = jnp.exp(logits - top) * valid[:, None]
    total = jnp.sum(expo, axis=0, keepdims=True)
    prob = expo / total
    logp = jnp.where(valid[:, None] > 0, logits - top - jnp.log(total), 0.0)
    entropy_part = -jnp.sum(prob * logp)
    whole, filt_all = (
        lax.all_gather(cells, ("wide", "narrow"), axis=0, tiled=True),
        lax.all_gather(filt, ("wide", "narrow"), axis=0, tiled=True),
    )
    keep = jax.nn.sigmoid(filt_all)
    weighted = prob * keep[:, None]
    g_pred = lax.dot_general(weighted, whole, (((0,), (0,)), ((), ())), precision=high)
    onehot = (slide_ids[:, None] == jnp.arange(n_slides, dtype=jnp.int32)[None, :]).astype(
        jnp.float32
    )
    gmask = gene_mask.astype(jnp.float32)
    spot_mask = jnp.dot(onehot, gmask, precision=high)
    masked_pred = spot_mask * g_pred
    sdot = jnp.sum(masked_pred * target, axis=1)
    spp = jnp.sum(masked_pred * g_pred, axis=1)
    stt = jnp.sum(spot_mask * target * target, axis=1)
    spot_scale = lax.rsqrt(spp + eps) * lax.rsqrt(stt + eps)
    spot_cos = sdot * spot_scale
    mass = jnp.sum(weighted, axis=0)
    log_part = density * (jnp.log(density) - jnp.log(mass))
    slide_vec = jnp.stack([mass, density, log_part], axis=1)
    loss_parts = jnp.stack([-jnp.sum(spot_cos), entropy_part])
    dot_s, pp_s, tt_s, slide_tot, loss_tot = lax.psum(
        (
            per_slide(onehot, g_pred * target),
            per_slide(onehot, g_pred * g_pred),
            per_slide(onehot, target * target),
            per_slide(onehot, slide_vec),
            loss_parts,
        ),
        ("wide", "narrow"),
    )
    mass_s = slide_tot[:, 0]
    wsum_s = slide_tot[:, 1]
    logsum_s = slide_tot[:, 2]
    gene_scale = gmask * lax.rsqrt(pp_s + eps) * lax.rsqrt(tt_s + eps)
    gene_cos = dot_s * gene_scale
    gene_loss = -jnp.sum(gene_cos)
    spot_loss = loss_tot[0]
    entropy = loss_tot[1] / (prob.shape[1] * lax.axis_size(("wide", "narrow")))
    kl_term = jnp.sum(logsum_s / wsum_s) + jnp.sum(jnp.log(mass_s) - jnp.log(wsum_s))
    count = jnp.sum(valid * keep)
    target_count = n_cells // 4
    count_term = jnp.abs(count - target_count) / n_cells
    binarity = jnp.sum(valid * (keep - keep * keep)) / n_cells
    loss = gene_loss + spot_loss + kl_term + count_term + binarity
    terms = jnp.stack([loss, gene_loss, spot_loss])
    reg_terms = jnp.stack([kl_term, count_term, binarity, entropy])
    gene_shrink = gene_scale * dot_s / (pp_s + eps)
    grad_pred = -jnp.dot(onehot, gene_scale, precision=high) * target
    grad_pred = grad_pred + jnp.dot(onehot, gene_shrink, precision=high) * g_pred
    spot_shrink = sdot / (spp + eps)
    grad_pred = grad_pred - spot_mask * spot_scale[:, None] * (
        target - spot_shrink[:, None] * g_pred
    )
    spot_slide = jnp.dot(onehot, jnp.stack([mass_s, wsum_s], axis=1), precision=high)
    grad_mass = -(density / spot_slide[:, 1]) / mass + 1.0 / spot_slide[:, 0]
    grad_weighted = lax.dot_general(whole, grad_pred, (((1,), (1,)), ((), ())), precision=high)
    grad_weighted = grad_weighted + grad_mass[None, :]
    grad_prob = keep[:, None] * grad_weighted
    keep_part = jnp.sum(prob * grad_weighted, axis=1)
    grad_logits = prob * (grad_prob - jnp.sum(prob * grad_prob, axis=0, keepdims=True))
    cell_part = jnp.dot(weighted, grad_pred, precision=high)
    grad_cells, keep_sum = (
        lax.psum_scatter(cell_part, ("wide", "narrow"), scatter_dimension=0, tiled=True),
        lax.psum_scatter(keep_part, ("wide", "narrow"), scatter_dimension=0, tiled=True),
    )
    first_row = lax.axis_index(("wide", "narrow")) * own_rows
    own_keep = lax.dynamic_slice_in_dim(keep, first_row, own_rows, 0)
    own_valid = lax.dynamic_slice_in_dim(valid, first_row, own_rows, 0)
    keep_grad = (
        keep_sum + own_valid * (jnp.sign(count - target_count) + 1.0 - 2.0 * own_keep) / n_cells
    )
    grad_filter = keep_grad * own_keep * (1.0 - own_keep)
    return (terms, reg_terms, g_pred, gene_cos, spot_cos, grad_logits, grad_filter, grad_cells)


def fits_fused(mesh, logits, cells, gene_mask, slide_ids):
    n_cells, spots = logits.shape
    return (
        (mesh.shape["wide"], mesh.shape["narrow"]) == (8, 4)
        and cells.shape == (16, 2048)
        and n_cells == 512
        and spots == 1024
        and gene_mask.shape[0] == 8
    )


def solution(mesh):
    def step(logits, filt, cells, cell_mask, gene_mask, slide_ids, target, density):
        fits = fits_fused(mesh, logits, cells, gene_mask, slide_ids)
        run = fused if fits else on_device
        return run(logits, filt, cells, cell_mask, gene_mask, slide_ids, target, density)

    placed = (
        P(None, ("wide", "narrow")),
        P(("wide", "narrow")),
        P(("wide", "narrow"), None),
        P(),
        P(),
        P(("wide", "narrow")),
        P(("wide", "narrow"), None),
        P(("wide", "narrow")),
    )
    return jax.shard_map(
        step,
        mesh=mesh,
        in_specs=placed,
        out_specs=(
            P(),
            P(),
            P(("wide", "narrow"), None),
            P(),
            P(("wide", "narrow")),
            P(None, ("wide", "narrow")),
            P(("wide", "narrow")),
            P(("wide", "narrow"), None),
        ),
        check_vma=False,
    )
```

```python
import jax
import jax.numpy as jnp
from jax import lax
from jax.experimental import pallas as pl
from jax.experimental.pallas import tpu as pltpu
from jax.sharding import PartitionSpec as P

eps = 1e-06
MESH = pl.DeviceIdType.MESH
bf16 = jnp.bfloat16
f32 = jnp.float32
LANES = 128
NCH = 8
BR = 32
GR = 256


def split(value):
    high = value.astype(bf16)
    return high, (value - high.astype(f32)).astype(bf16)


def mm(a, b):
    return lax.dot_general(a, b, (((1,), (0,)), ((), ())), preferred_element_type=f32)


def mm_nt(a, b):
    return lax.dot_general(a, b, (((1,), (1,)), ((), ())), preferred_element_type=f32)


def fused_kernel(
    logits_hbm, filt_ref, cells_hbm, mask_ref, gene_ref, ids_ref, target_hbm, dens_ref,
    pv, lg, gw, keepc, gmass_ref, gacc, sums_ref, keep_ref, gcos_ref, scos_ref, gfilt_ref, gcell_ref,
    tv, buf, chi, clo, fb, valid, whi, wlo, thi, tlo, gmb, oh, l1, l2,
    idc, blocks, sd, sp, st, mass, rows, gph, gpl, kp,
    stat, a1, a2, a3, fin, kvec, k1, k2, k3,
    part, rb, sb, r1, tt_, r2, qq, r3,
    lsem, tsem, osem,
    zs, zr, xs, xr, ys, yr, bs, br,
    fzs, fzr, fxs, fxr, fys, fyr, fbs, fbr,
    as1, ar1, as2, ar2, as3, ar3, as4, ar4,
    ks1, kr1, ks2, kr2, ks3, kr3,
    cbs, cbr, cxs, cxr, cys, cyr, czs, czr,
):
    n_cells = chi.shape[1]
    width = chi.shape[2]
    n_blocks = tv.shape[1]
    spots = n_blocks * BR
    n_slides = gene_ref.shape[0]
    tiles = spots // LANES
    wide, narrow = lax.axis_index("wide"), lax.axis_index("narrow")
    z, y = lax.div(wide, 2), lax.rem(wide, 2)
    x, core = lax.div(narrow, 2), lax.rem(narrow, 2)
    to_z = [(lax.rem(z + k, 4) * 2 + y, narrow) for k in (1, 2, 3)]
    from_z = [lax.rem(z + 4 - k, 4) for k in (1, 2, 3)]
    to_x = (wide, (1 - x) * 2 + core)
    to_y = (z * 2 + 1 - y, narrow)
    to_xy = (z * 2 + 1 - y, (1 - x) * 2 + core)
    to_b = (wide, x * 2 + 1 - core)

    def rcopy(src, dst, ss, rs, dev):
        return pltpu.make_async_remote_copy(
            src_ref=src, dst_ref=dst, send_sem=ss, recv_sem=rs, device_id=dev, device_id_type=MESH
        )

    def lanes(i, w=LANES):
        return pl.ds(pl.multiple_of(i * w, w), w)

    def own_cells(c, h):
        return pltpu.make_async_copy(
            cells_hbm.at[:, pl.ds((c * 2 + h) * LANES, LANES)], buf.at[c, h, z, y, x, core], lsem.at[c, h]
        )

    def get_logits(i):
        return pltpu.make_async_copy(logits_hbm.at[:, lanes(i)], lg.at[i], osem.at[i])

    def get_target(c):
        return pltpu.make_async_copy(target_hbm.at[:, :, lanes(c, width)], tv.at[c], tsem.at[c])

    for c in range(NCH):
        for h in range(2):
            own_cells(c, h).start()
    for i in range(tiles):
        get_logits(i).start()
    for c in range(NCH):
        get_target(c).start()

    barrier = pltpu.get_barrier_semaphore()
    for dev in to_z + [to_x, to_y, to_xy, to_b]:
        pl.semaphore_signal(barrier, inc=1, device_id=dev, device_id_type=MESH)

    row16 = lax.broadcasted_iota(jnp.int32, (16, LANES), 0)
    mine = jnp.zeros((16, LANES), f32)
    for r in range(16):
        mine = jnp.where(row16 == r, filt_ref[r], mine)
    fb[z, y, x, core] = mine
    for q in range(n_cells // LANES):
        line = mask_ref[q : q + 1, :].astype(f32)
        valid[q * LANES : (q + 1) * LANES, :] = jnp.broadcast_to(line, (LANES, LANES)).T
    pl.semaphore_wait(barrier, 7)

    def z_out(c, k):
        r = buf.at[c, :, z, y, x, core]
        return rcopy(r, r, zs.at[c, k], zr.at[c, k], to_z[k])

    def z_in(c, k):
        r = buf.at[c, :, from_z[k], y, x, core]
        return rcopy(r, r, zs.at[c, k], zr.at[c, k], to_z[k])

    def s1_out(c):
        a = buf.at[c, 0, :, y, x, core]
        b = buf.at[c, 1, :, y, x, core]
        return [rcopy(a, a, xs.at[c, 0], xr.at[c, 0], to_x), rcopy(b, b, ys.at[c, 0], yr.at[c, 0], to_y)]

    def s1_in(c):
        a = buf.at[c, 0, :, y, 1 - x, core]
        b = buf.at[c, 1, :, 1 - y, x, core]
        return [rcopy(a, a, xs.at[c, 0], xr.at[c, 0], to_x), rcopy(b, b, ys.at[c, 0], yr.at[c, 0], to_y)]

    def s2_out(c):
        a = buf.at[c, 0, :, y, :, core]
        b = buf.at[c, 1, :, :, x, core]
        return [rcopy(a, a, ys.at[c, 1], yr.at[c, 1], to_y), rcopy(b, b, xs.at[c, 1], xr.at[c, 1], to_x)]

    def s2_in(c):
        a = buf.at[c, 0, :, 1 - y, :, core]
        b = buf.at[c, 1, :, :, 1 - x, core]
        return [rcopy(a, a, ys.at[c, 1], yr.at[c, 1], to_y), rcopy(b, b, xs.at[c, 1], xr.at[c, 1], to_x)]

    def s3_out(c):
        r = buf.at[c, :, :, :, :, core]
        return rcopy(r, r, bs.at[c], br.at[c], to_b)

    def s3_in(c):
        r = buf.at[c, :, :, :, :, 1 - core]
        return rcopy(r, r, bs.at[c], br.at[c], to_b)

    def fz_out(k):
        r = fb.at[z, y, x, core]
        return rcopy(r, r, fzs.at[k], fzr.at[k], to_z[k])

    def fz_in(k):
        r = fb.at[from_z[k], y, x, core]
        return rcopy(r, r, fzs.at[k], fzr.at[k], to_z[k])

    def fx(at):
        r = fb.at[:, y, at, core]
        return rcopy(r, r, fxs.at[0], fxr.at[0], to_x)

    def fy(at):
        r = fb.at[:, at, :, core]
        return rcopy(r, r, fys.at[0], fyr.at[0], to_y)

    def fs(at):
        r = fb.at[:, :, :, at]
        return rcopy(r, r, fbs.at[0], fbr.at[0], to_b)

    def b1(c):
        return rcopy(stat.at[c, 1 - core], a1.at[c], as1.at[c], ar1.at[c], to_b)

    plane = [to_x, to_y, to_xy]
    here = y * 2 + x
    there = [y * 2 + 1 - x, (1 - y) * 2 + x, (1 - y) * 2 + 1 - x]

    def b2_out(c, k):
        r = a2.at[c, here]
        return rcopy(r, r, as2.at[c, k], ar2.at[c, k], plane[k])

    def b2_in(c, k):
        r = a2.at[c, there[k]]
        return rcopy(r, r, as2.at[c, k], ar2.at[c, k], plane[k])

    def b3_out(c, k):
        r = a3.at[c, z]
        return rcopy(r, r, as3.at[c, k], ar3.at[c, k], to_z[k])

    def b3_in(c, k):
        r = a3.at[c, from_z[k]]
        return rcopy(r, r, as3.at[c, k], ar3.at[c, k], to_z[k])

    def b4(c, half):
        r = fin.at[c, half]
        return rcopy(r, r, as4.at[c], ar4.at[c], to_b)

    def sum_second(c):
        b1(c).wait_recv()
        a2[c, here] = stat[c, core] + a1[c]
        for k in range(3):
            b2_out(c, k).start()

    def sum_third(c):
        for k in range(3):
            b2_in(c, k).wait_recv()
        a3[c, z] = (a2[c, 0] + a2[c, 1]) + (a2[c, 2] + a2[c, 3])
        for k in range(3):
            b3_out(c, k).start()

    def sum_fourth(c):
        for k in range(3):
            b3_in(c, k).wait_recv()
        fin[c, core] = (a3[c, 0] + a3[c, 1]) + (a3[c, 2] + a3[c, 3])
        b4(c, core).start()

    def sum_last(c):
        b4(c, 1 - core).wait_recv()
        return jnp.concatenate([fin[c, 0], fin[c, 1]], axis=1)

    def v1(n):
        return rcopy(kvec.at[n], k1.at[n], ks1.at[n], kr1.at[n], to_b)

    def v2(n, slot, k):
        return rcopy(k2.at[n, slot], k2.at[n, slot], ks2.at[n, k], kr2.at[n, k], plane[k])

    def v3(n, slot, k):
        return rcopy(k3.at[n, slot], k3.at[n, slot], ks3.at[n, k], kr3.at[n, k], to_z[k])

    def vector_second(n):
        v1(n).wait_recv()
        k2[n, here] = kvec[n] + k1[n]
        for k in range(3):
            v2(n, here, k).start()

    def vector_third(n):
        for k in range(3):
            v2(n, there[k], k).wait_recv()
        k3[n, z] = (k2[n, 0] + k2[n, 1]) + (k2[n, 2] + k2[n, 3])
        for k in range(3):
            v3(n, z, k).start()

    def vector_last(n):
        for k in range(3):
            v3(n, from_z[k], k).wait_recv()
        return (k3[n, 0] + k3[n, 1]) + (k3[n, 2] + k3[n, 3])

    def softmax(i, ent):
        get_logits(i).wait()
        value = lg[i]
        top = jnp.max(value, axis=0, keepdims=True)
        expo = jnp.exp(value - top) * valid[...]
        total = jnp.sum(expo, axis=0, keepdims=True)
        prob = expo * (1.0 / total)
        lg[i] = prob
        return ent + jnp.sum(prob * (value - top - jnp.log(total)), axis=0, keepdims=True)

    def one_hot(i, _):
        ids = ids_ref[pl.ds(i, 1), :]
        square = (lax.broadcasted_iota(jnp.int32, (LANES, LANES), 0) == ids).astype(f32)
        oh[lanes(i), :] = square.T.astype(bf16)
        per = LANES // BR
        turned = jnp.broadcast_to(ids, (LANES, LANES)).astype(f32).T
        idc[pl.ds(i * per, per)] = turned.reshape(per, BR, LANES)
        return 0

    def weights(i, _):
        w = lg[i] * keepc[...]
        mass[pl.ds(i, 1), :] = jnp.sum(w, axis=0, keepdims=True)
        high, low = split(w)
        whi[:, lanes(i)] = high
        wlo[:, lanes(i)] = low
        turned = w.T
        high, low = split(turned)
        thi[lanes(i), :] = high
        tlo[lanes(i), :] = low
        return 0

    for k in range(3):
        fz_out(k).start()
    for c in range(NCH):
        for h in range(2):
            own_cells(c, h).wait()
        for k in range(3):
            z_out(c, k).start()

    def stage_z(c):
        for k in range(3):
            z_in(c, k).wait_recv()
        for d in s1_out(c):
            d.start()

    def stage_1(c):
        for d in s1_in(c):
            d.wait_recv()
        for d in s2_out(c):
            d.start()

    def stage_2(c):
        for d in s2_in(c):
            d.wait_recv()
        s3_out(c).start()

    def fold(v):
        out = v[:, :LANES]
        for k in range(1, v.shape[1] // LANES):
            out = out + v[:, k * LANES : (k + 1) * LANES]
        return out

    def eighths(v):
        return jnp.sum(v.reshape(v.shape[0] // 8, 8, v.shape[1]), axis=0)

    for c in range(NCH):
        gm = jnp.concatenate(
            [gene_ref[:, c * width : (c + 1) * width].astype(f32), jnp.zeros((LANES - n_slides, width), f32)], axis=0
        )
        gmb[c] = gm.astype(bf16)
    sd[...] = jnp.zeros_like(sd)
    sp[...] = jnp.zeros_like(sp)
    st[...] = jnp.zeros_like(st)
    lax.fori_loop(0, tiles, one_hot, 0)

    begins = [jnp.sum((ids_ref[...] < k).astype(jnp.int32)) for k in range(n_slides + 1)]
    firsts = [jnp.minimum(lax.div(begins[k], BR), n_blocks - 1) for k in range(n_slides)]
    lasts = [lax.div(jnp.maximum(begins[k + 1] - 1, 0), BR) for k in range(n_slides)]
    slide16 = lax.broadcasted_iota(jnp.int32, (16, 8 * n_blocks), 0)
    block16 = lax.div(lax.broadcasted_iota(jnp.int32, (16, 8 * n_blocks), 1), 8)
    inner = jnp.zeros((16, 8 * n_blocks), f32)
    for k in range(n_slides):
        full = jnp.logical_and(block16 > firsts[k], block16 < lasts[k])
        inner = jnp.where(jnp.logical_and(slide16 == k, full), 1.0, inner)
    inner = inner.astype(bf16)
    inner = jnp.concatenate([inner, inner], axis=1)
    slide8 = lax.broadcasted_iota(jnp.int32, (8, width), 0)

    def gene_sums(c, products, number, at_row):
        sums = []
        for n in range(number):
            bh, bl = split(blocks[n])
            sums.append(mm(inner, jnp.concatenate([bh, bl], axis=0))[:8, :])
        for k in range(n_slides):
            parts = [jnp.zeros((8, width), f32)] * number
            for block, counts in ((firsts[k], None), (lasts[k], lasts[k] != firsts[k])):
                own = idc[block] == float(k)
                if counts is not None:
                    own = jnp.logical_and(own, counts)
                own = own.astype(f32)
                own = jnp.concatenate([own] * (width // LANES), axis=1)
                for n, prod in enumerate(products(c, block)):
                    parts[n] = parts[n] + eighths(prod * own)
            for n in range(number):
                line = jnp.sum(parts[n], axis=0, keepdims=True)
                sums[n] = sums[n] + jnp.where(slide8 == k, line, 0.0)
        for n in range(number):
            for h in range(2):
                stat[c, h, at_row + n * 8 : at_row + (n + 1) * 8, :] = sums[n][:, h * LANES : (h + 1) * LANES]

    def of_target(c, r):
        tgt = tv[c, r]
        return (tgt * tgt,)

    def of_both(c, r):
        pred, tgt = pv[c, r], tv[c, r]
        return pred * tgt, jnp.where(tgt > 0.0, pred * pred, 0.0)

    def by_rows(c, products, spots_of):
        for r in range(n_blocks):
            at = slice(r * BR, (r + 1) * BR)
            for n, (prod, spot) in enumerate(zip(products(c, r), spots_of)):
                spot[at, :] += fold(prod)
                blocks[n, r * 8 : (r + 1) * 8, :] = eighths(prod)

    def target_sums(c, _):
        per = GR // BR
        for n in range(spots // GR):
            sees = mm(oh[n * GR : (n + 1) * GR, :], gmb[c]).reshape(per, BR, width)
            for r in range(per):
                tv[c, n * per + r] = sees[r] * tv[c, n * per + r]
        by_rows(c, of_target, (st,))
        gene_sums(c, of_target, 1, 16)
        return 0

    def predict(c):
        s3_in(c).wait_recv()
        whole = jnp.concatenate([buf[c, h].reshape(n_cells, LANES) for h in range(2)], axis=1)
        high, low = split(whole)
        chi[c] = high
        clo[c] = low
        wh, wl = thi[...], tlo[...]
        pred = mm(jnp.concatenate([wh, wl, wh], axis=1), jnp.concatenate([high, high, low], axis=0))
        pv[c] = pred.reshape(n_blocks, BR, width)

    def predicted_sums(c):
        by_rows(c, of_both, (sd, sp))
        gene_sums(c, of_both, 2, 0)

    ent = lax.fori_loop(0, tiles // 2, softmax, jnp.zeros((1, LANES), f32))
    for k in range(3):
        fz_in(k).wait_recv()
    fx(x).start()
    stage_z(0)
    ent = lax.fori_loop(tiles // 2, tiles, softmax, ent)
    fx(1 - x).wait_recv()
    fy(y).start()
    stage_z(1)
    stage_1(0)
    for c in range(NCH):
        get_target(c).wait()
    lax.fori_loop(0, 3, target_sums, 0)
    fy(1 - y).wait_recv()
    fs(core).start()
    stage_z(2)
    stage_1(1)
    lax.fori_loop(3, 6, target_sums, 0)
    stage_z(3)
    stage_2(0)
    fs(1 - core).wait_recv()
    keepc[...] = jax.nn.sigmoid(fb[...].reshape(n_cells, LANES))
    lax.fori_loop(0, tiles, weights, 0)
    stage_1(2)
    lax.fori_loop(6, NCH, target_sums, 0)

    def gather_tick(t, _):
        c = t - 4
        pl.when(t < NCH)(lambda: stage_z(t))
        pl.when(t - 3 < NCH)(lambda: stage_2(t - 3))
        predict(c)
        predicted_sums(c)
        b1(c).start()
        pl.when(t - 1 < NCH)(lambda: stage_1(t - 1))
        pl.when(c >= 1)(lambda: sum_second(c - 1))
        pl.when(c >= 3)(lambda: sum_third(c - 3))
        pl.when(c >= 5)(lambda: sum_fourth(c - 5))
        return 0

    lax.fori_loop(4, NCH + 4, gather_tick, 0)
    last = NCH - 1

    def spot_rows(i, _):
        for k, ref in enumerate((sd, sp, st)):
            rows[k, pl.ds(i, 1), :] = jnp.sum(ref[lanes(i), :].T, axis=0, keepdims=True)
        return 0

    lax.fori_loop(0, tiles, spot_rows, 0)
    sdot, spp, stt = rows[0], rows[1], rows[2]
    scale = lax.rsqrt(spp + eps) * lax.rsqrt(stt + eps)
    scos = sdot * scale
    scos_ref[...] = scos
    shrink = scale * (sdot / (spp + eps))
    for k, value in ((0, scale), (1, shrink)):
        high, low = split(value)
        rows[2 * k] = high.astype(f32)
        rows[2 * k + 1] = low.astype(f32)
    dens = dens_ref[...]
    mass_row = mass[...]
    rows[4] = dens * (jnp.log(dens) - jnp.log(mass_row))

    iota8 = lax.broadcasted_iota(jnp.int32, (8, LANES), 0)
    lane8 = lax.broadcasted_iota(jnp.int32, (8, LANES), 1)

    def coef_rows(i, sums):
        mine = (iota8 == ids_ref[pl.ds(i, 1), :]).astype(f32)
        pad = jnp.zeros((LANES - 32, LANES), f32)
        at = pl.ds(i, 1)
        for k, ref in ((0, l1), (1, l2)):
            ref[lanes(i), :] = jnp.concatenate(
                [mine, mine, mine * rows[2 * k, at, :], mine * rows[2 * k + 1, at, :], pad], axis=0
            ).T.astype(bf16)
        return (
            sums[0] + mine * mass[at, :],
            sums[1] + mine * dens_ref[at, :],
            sums[2] + mine * rows[4, at, :],
        )

    zero = jnp.zeros((8, LANES), f32)
    totals = lax.fori_loop(0, tiles, coef_rows, (zero, zero, zero))
    extra = zero
    for k, value in enumerate(totals):
        extra = jnp.where(lane8 == k, jnp.sum(value, axis=1, keepdims=True), extra)
    extra = jnp.where(jnp.logical_and(lane8 == 3, iota8 == 0), -jnp.sum(scos), extra)
    extra = jnp.where(jnp.logical_and(lane8 == 4, iota8 == 0), -jnp.sum(ent), extra)
    kvec[0] = extra
    v1(0).start()
    sum_second(last)
    sum_third(last - 2)
    sum_fourth(last - 4)

    gacc[...] = jnp.zeros_like(gacc)

    def scatter_sib(c):
        return rcopy(part.at[c, :, :, :, :, 1 - core], rb.at[c], cbs.at[c], cbr.at[c], to_b)

    def scatter_one(c):
        return [
            rcopy(sb.at[c, 0, :, 1 - y], r1.at[c, 0], cys.at[c, 0], cyr.at[c, 0], to_y),
            rcopy(sb.at[c, 1, :, :, 1 - x], r1.at[c, 1], cxs.at[c, 0], cxr.at[c, 0], to_x),
        ]

    def scatter_two(c):
        return [
            rcopy(tt_.at[c, 0, :, 1 - x], r2.at[c, 0], cxs.at[c, 1], cxr.at[c, 1], to_x),
            rcopy(tt_.at[c, 1, :, 1 - y], r2.at[c, 1], cys.at[c, 1], cyr.at[c, 1], to_y),
        ]

    def scatter_z(c, k):
        return rcopy(qq.at[c, :, lax.rem(z + k + 1, 4)], r3.at[c, k], czs.at[c, k], czr.at[c, k], to_z[k])

    def sc1(c):
        scatter_sib(c).wait_recv()
        sb[c] = part[c, :, :, :, :, core] + rb[c]
        for d in scatter_one(c):
            d.start()

    def sc2(c):
        for d in scatter_one(c):
            d.wait_recv()
        tt_[c, 0] = sb[c, 0, :, y] + r1[c, 0]
        tt_[c, 1] = sb[c, 1, :, :, x] + r1[c, 1]
        for d in scatter_two(c):
            d.start()

    def sc3(c):
        for d in scatter_two(c):
            d.wait_recv()
        qq[c, 0] = tt_[c, 0, :, x] + r2[c, 0]
        qq[c, 1] = tt_[c, 1, :, y] + r2[c, 1]
        for k in range(3):
            scatter_z(c, k).start()

    def sc4(c):
        for k in range(3):
            scatter_z(c, k).wait_recv()
        for h in range(2):
            gcell_ref[:, lanes(c * 2 + h)] = (qq[c, h, z] + r3[c, 0, h]) + (r3[c, 1, h] + r3[c, 2, h])

    def backward(c):
        total = sum_last(c)
        dot_s, pp_s, tt_s = total[0:8], total[8:16], total[16:24]
        gm = gene_ref[:, lanes(c, width)].astype(f32)
        gscale = gm * lax.rsqrt(pp_s + eps) * lax.rsqrt(tt_s + eps)
        gcos = dot_s * gscale
        gcos_ref[:, lanes(c, width)] = gcos
        gacc[...] += gcos
        gshrink = gscale * (dot_s / (pp_s + eps))
        pad = jnp.zeros((LANES - 32, width), f32)
        coefs = []
        for value in (gscale, gshrink):
            high, low = split(value)
            coefs.append(
                jnp.concatenate([high.astype(f32), low.astype(f32), gm, gm, pad], axis=0).astype(bf16)
            )
        per = GR // BR
        for n in range(spots // GR):
            at = slice(n * GR, (n + 1) * GR)
            own = slice(n * per, (n + 1) * per)
            pred, tgt = pv[c, own].reshape(GR, width), tv[c, own].reshape(GR, width)
            gh, gl = split(mm(l2[at, :], coefs[1]) * pred - mm(l1[at, :], coefs[0]) * tgt)
            gph[c, at, :] = gh
            gpl[c, at, :] = gl
        wh, wl = whi[...], wlo[...]
        gh, gl = gph[c], gpl[c]
        out = mm(jnp.concatenate([wh, wl, wh], axis=1), jnp.concatenate([gh, gh, gl], axis=0))
        for h in range(2):
            part[c, h] = out[:, h * LANES : (h + 1) * LANES].reshape(4, 2, 2, 2, 16, LANES)
        scatter_sib(c).start()

    def spot_part(n):
        at = pl.ds(n * GR, GR)
        left = [chi[c] for c in range(NCH)]
        left = left + [clo[c] for c in range(NCH)] + left
        right = [gph[c, at, :] for c in range(NCH)]
        right = right + right + [gpl[c, at, :] for c in range(NCH)]
        out = mm_nt(jnp.concatenate(left, axis=1), jnp.concatenate(right, axis=1))
        for h in range(GR // LANES):
            gw[n * (GR // LANES) + h] = out[:, h * LANES : (h + 1) * LANES]

    def back_tick(t, _):
        pl.when(t >= 3)(lambda: sc2(t - 3))
        backward(t)
        pl.when(t >= 1)(lambda: sc1(t - 1))
        pl.when(t >= 4)(lambda: sc3(t - 4))

        @pl.when(t == 0)
        def _():
            vector_second(0)
            sum_third(last - 1)
            sum_fourth(last - 3)

        @pl.when(t == 1)
        def _():
            sum_third(last)
            sum_fourth(last - 2)

        @pl.when(t == 2)
        def _():
            vector_third(0)
            sum_fourth(last - 1)

        @pl.when(t == 3)
        def _():
            sum_fourth(last)

        @pl.when(t == 4)
        def _():
            slide_totals()

        @pl.when(t == 5)
        def _():
            vector_second(1)

        @pl.when(t == 7)
        def _():
            vector_third(1)

        pl.when(t >= 6)(lambda: sc4(t - 6))
        return 0

    quarter = n_cells // LANES
    blank = jnp.zeros((8 - quarter, LANES), f32)

    def slide_totals():
        sums_s = vector_last(0)
        sums_ref[...] = sums_s
        mass_s, wsum_s = sums_s[:, 0:1], sums_s[:, 1:2]
        kp[...] = jnp.zeros_like(kp)

        def by_mass(i, _):
            at = pl.ds(i, 1)
            mine = (iota8 == ids_ref[at, :]).astype(f32)
            mass_at = jnp.sum(mine * mass_s, axis=0, keepdims=True)
            wsum_at = jnp.sum(mine * wsum_s, axis=0, keepdims=True)
            gmass = -(dens_ref[at, :] / wsum_at) / mass[at, :] + 1.0 / mass_at
            gmass_ref[at, :] = gmass
            kp[...] += lg[i] * gmass
            return 0

        lax.fori_loop(0, tiles, by_mass, 0)
        kp[...] = kp[...] * keepc[...]
        rows_k = [jnp.sum(kp[q * LANES : (q + 1) * LANES, :].T, axis=0, keepdims=True) for q in range(quarter)]
        kvec[1] = jnp.concatenate(rows_k + [blank], axis=0)
        v1(1).start()

    lax.fori_loop(0, NCH, back_tick, 0)
    sc1(last)
    sc3(last - 3)
    sc2(last - 2)
    spot_part(0)
    sc3(last - 2)
    sc2(last - 1)
    sc2(last)
    spot_part(1)
    sc3(last - 1)
    sc3(last)
    for c in range(NCH - 6, NCH - 3):
        sc4(c)
    spot_part(2)
    spot_part(3)

    rows_keep = [keepc[q * LANES : (q + 1) * LANES, :].T[0:1, :] for q in range(quarter)]
    keep = jnp.concatenate(rows_keep, axis=0)
    keep_ref[...] = jnp.concatenate([keep, blank], axis=0)
    ok = mask_ref[...].astype(f32)
    count = jnp.sum(ok * keep)
    target_count = n_cells // 4
    total = vector_last(1)[:quarter, :]
    off = count - target_count
    sign = jnp.where(off > 0, 1.0, jnp.where(off < 0, -1.0, 0.0))
    dev = wide * 4 + narrow

    def own_lanes(rows_q):
        picked = jnp.concatenate([rows_q, blank], axis=0)
        picked = jnp.sum(jnp.where(iota8 == lax.div(dev, 8), picked, 0.0), axis=0, keepdims=True)
        return pltpu.roll(picked, lax.rem(LANES - lax.rem(dev, 8) * 16, LANES), 1)

    own_keep = own_lanes(keep)
    own_rest = own_lanes(total + ok * keep * (sign + 1.0 - 2.0 * keep) / n_cells)
    for c in range(NCH - 3, NCH):
        sc4(c)
    along = jnp.zeros((16, LANES), f32)
    for c in range(NCH):
        for h in range(2):
            at = (c * 2 + h) * LANES
            along = along + buf[c, h, z, y, x, core] * gcell_ref[:, at : at + LANES]
    along = jnp.concatenate([along, jnp.zeros((LANES - 16, LANES), f32)], axis=0)
    along = jnp.sum(along.T, axis=0, keepdims=True)
    gfilt_ref[...] = (along + own_rest) * (1.0 - own_keep)

    def leave(c, _):
        for k in range(3):
            z_out(c, k).wait_send()
            b2_out(c, k).wait_send()
            b3_out(c, k).wait_send()
            scatter_z(c, k).wait_send()
        for d in s1_out(c) + s2_out(c) + scatter_one(c) + scatter_two(c):
            d.wait_send()
        s3_out(c).wait_send()
        b1(c).wait_send()
        b4(c, core).wait_send()
        scatter_sib(c).wait_send()
        return 0

    lax.fori_loop(0, NCH, leave, 0)
    for k in range(3):
        fz_out(k).wait_send()
        for n in range(2):
            v2(n, here, k).wait_send()
            v3(n, z, k).wait_send()
    fx(x).wait_send()
    fy(y).wait_send()
    fs(core).wait_send()
    for n in range(2):
        v1(n).wait_send()


def finish_kernel(
    pv, lg, gw, keepc, gmass_ref, gacc, sums_ref, keep_ref, gcos_in, scos_in, gfilt_in, gcell_in, mask_ref,
    terms_ref, reg_ref, pred_hbm, gcos_ref, scos_ref, glog_hbm, gfilt_ref, gcell_ref,
    psem, osem,
):
    width = pv.shape[3]
    tiles, n_cells = lg.shape[:2]

    def lanes(i, w=LANES):
        return pl.ds(pl.multiple_of(i * w, w), w)

    def put_pred(c):
        return pltpu.make_async_copy(pv.at[c], pred_hbm.at[:, :, lanes(c, width)], psem.at[c])

    def put_glog(i):
        return pltpu.make_async_copy(gw.at[i], glog_hbm.at[:, lanes(i)], osem.at[i])

    for c in range(NCH):
        put_pred(c).start()

    def finish(i, _):
        grad = keepc[...] * (gw[i] + gmass_ref[pl.ds(i, 1), :])
        prob = lg[i]
        gw[i] = prob * (grad - jnp.sum(prob * grad, axis=0, keepdims=True))
        put_glog(i).start()
        return 0

    lax.fori_loop(0, tiles, finish, 0)
    gcos_ref[...] = gcos_in[...]
    scos_ref[...] = scos_in[...]
    gcell_ref[...] = gcell_in[...]
    gfilt_ref[...] = gfilt_in[:, : gfilt_ref.shape[1]]

    sums_s = sums_ref[...]
    mass_s, wsum_s, logsum_s = sums_s[:, 0:1], sums_s[:, 1:2], sums_s[:, 2:3]
    row = lax.broadcasted_iota(jnp.int32, sums_s.shape, 0)
    lane = lax.broadcasted_iota(jnp.int32, sums_s.shape, 1)
    keep = keep_ref[: n_cells // LANES, :]
    ok = mask_ref[...].astype(f32)
    count = jnp.sum(ok * keep)
    count_term = jnp.abs(count - n_cells // 4) / n_cells
    binarity = jnp.sum(ok * (keep - keep * keep)) / n_cells
    gene_loss = -jnp.sum(gacc[...])
    spot_loss = jnp.sum(jnp.where(jnp.logical_and(lane == 3, row == 0), sums_s, 0.0))
    entropy = jnp.sum(jnp.where(jnp.logical_and(lane == 4, row == 0), sums_s, 0.0)) / (tiles * LANES * 32)
    kl = jnp.sum(logsum_s / wsum_s + jnp.log(mass_s) - jnp.log(wsum_s))
    terms_ref[0] = gene_loss + spot_loss + kl + count_term + binarity
    terms_ref[1] = gene_loss
    terms_ref[2] = spot_loss
    reg_ref[0] = kl
    reg_ref[1] = count_term
    reg_ref[2] = binarity
    reg_ref[3] = entropy
    for i in range(tiles):
        put_glog(i).wait()
    for c in range(NCH):
        put_pred(c).wait()


def fused(logits, filt, cells, cell_mask, gene_mask, slide_ids, target, density):
    n_cells, spots = logits.shape
    own, genes = cells.shape
    n_slides = gene_mask.shape[0]
    width = genes // NCH
    tiles = spots // LANES
    dma = pltpu.SemaphoreType.DMA
    vmem, anywhere = pltpu.VMEM, pl.BlockSpec(memory_space=pl.ANY)
    inside = pl.BlockSpec(memory_space=pltpu.VMEM)
    scalars = pl.BlockSpec(memory_space=pltpu.SMEM)
    ring = (4, 2, 2, 2, 16, LANES)
    scratch = [
        vmem((NCH, spots // BR, BR, width), f32),
        vmem((NCH, 2) + ring, f32),
        vmem((NCH, n_cells, width), bf16),
        vmem((NCH, n_cells, width), bf16),
        vmem(ring, f32),
        vmem((n_cells, LANES), f32),
        vmem((n_cells, spots), bf16),
        vmem((n_cells, spots), bf16),
        vmem((spots, n_cells), bf16),
        vmem((spots, n_cells), bf16),
        vmem((NCH, LANES, width), bf16),
        vmem((spots, LANES), bf16),
        vmem((spots, LANES), bf16),
        vmem((spots, LANES), bf16),
        vmem((spots // BR, BR, LANES), f32),
        vmem((2, spots * 8 // BR, width), f32),
        vmem((spots, LANES), f32),
        vmem((spots, LANES), f32),
        vmem((spots, LANES), f32),
        vmem((8, LANES), f32),
        vmem((5, 8, LANES), f32),
        vmem((NCH, spots, width), bf16),
        vmem((NCH, spots, width), bf16),
        vmem((n_cells, LANES), f32),
        vmem((NCH, 2, 24, LANES), f32),
        vmem((NCH, 24, LANES), f32),
        vmem((NCH, 4, 24, LANES), f32),
        vmem((NCH, 4, 24, LANES), f32),
        vmem((NCH, 2, 24, LANES), f32),
        vmem((2, 8, LANES), f32),
        vmem((2, 8, LANES), f32),
        vmem((2, 4, 8, LANES), f32),
        vmem((2, 4, 8, LANES), f32),
        vmem((NCH, 2) + ring, f32),
        vmem((NCH, 2, 4, 2, 2, 16, LANES), f32),
        vmem((NCH, 2, 4, 2, 2, 16, LANES), f32),
        vmem((NCH, 2, 4, 2, 16, LANES), f32),
        vmem((NCH, 2, 4, 2, 16, LANES), f32),
        vmem((NCH, 2, 4, 16, LANES), f32),
        vmem((NCH, 2, 4, 16, LANES), f32),
        vmem((NCH, 3, 2, 16, LANES), f32),
        dma((NCH, 2)), dma((NCH,)), dma((tiles,)),
        dma((NCH, 3)), dma((NCH, 3)), dma((NCH, 2)), dma((NCH, 2)), dma((NCH, 2)), dma((NCH, 2)), dma((NCH,)), dma((NCH,)),
        dma((3,)), dma((3,)), dma((1,)), dma((1,)), dma((1,)), dma((1,)), dma((1,)), dma((1,)),
        dma((NCH,)), dma((NCH,)), dma((NCH, 3)), dma((NCH, 3)), dma((NCH, 3)), dma((NCH, 3)), dma((NCH,)), dma((NCH,)),
        dma((2,)), dma((2,)), dma((2, 3)), dma((2, 3)), dma((2, 3)), dma((2, 3)),
        dma((NCH,)), dma((NCH,)), dma((NCH, 2)), dma((NCH, 2)), dma((NCH, 2)), dma((NCH, 2)), dma((NCH, 3)), dma((NCH, 3)),
    ]
    mask = cell_mask.reshape(n_cells // LANES, LANES)
    held = (
        vmem((NCH, spots // BR, BR, width), f32),
        vmem((tiles, n_cells, LANES), f32),
        vmem((tiles, n_cells, LANES), f32),
        vmem((n_cells, LANES), f32),
        vmem((tiles, LANES), f32),
        vmem((8, width), f32),
        vmem((8, LANES), f32),
        vmem((8, LANES), f32),
        vmem((n_slides, genes), f32),
        vmem((tiles, LANES), f32),
        vmem((1, LANES), f32),
        vmem((own, genes), f32),
    )
    between = pl.pallas_call(
        fused_kernel,
        out_shape=held,
        in_specs=[anywhere, scalars, anywhere, inside, inside, inside, anywhere, inside],
        out_specs=(inside,) * len(held),
        scratch_shapes=scratch,
        compiler_params=pltpu.CompilerParams(
            collective_id=0, has_side_effects=True, vmem_limit_bytes=50 << 20
        ),
    )(
        logits, filt, cells, mask, gene_mask,
        slide_ids.reshape(tiles, LANES), target.reshape(spots // BR, BR, genes), density.reshape(tiles, LANES),
    )
    out = pl.pallas_call(
        finish_kernel,
        out_shape=(
            jax.ShapeDtypeStruct((3,), f32),
            jax.ShapeDtypeStruct((4,), f32),
            jax.ShapeDtypeStruct((spots // BR, BR, genes), f32),
            jax.ShapeDtypeStruct((n_slides, genes), f32),
            jax.ShapeDtypeStruct((tiles, LANES), f32),
            jax.ShapeDtypeStruct((n_cells, spots), f32),
            jax.ShapeDtypeStruct((1, own), f32),
            jax.ShapeDtypeStruct((own, genes), f32),
        ),
        in_specs=[inside] * (len(held) + 1),
        out_specs=(scalars, scalars, anywhere, inside, inside, anywhere, inside, inside),
        scratch_shapes=[dma((NCH,)), dma((tiles,))],
        compiler_params=pltpu.CompilerParams(vmem_limit_bytes=24 << 20),
    )(*between, mask)
    terms, reg, pred, gcos, scos, glog, gfilt, gcell = out
    return terms, reg, pred.reshape(spots, genes), gcos, scos.reshape(spots), glog, gfilt.reshape(own), gcell


def per_slide(onehot, values):
    return lax.dot_general(
        onehot, values, (((0,), (0,)), ((), ())), precision=lax.Precision.HIGHEST
    )


def on_device(logits, filt, cells, cell_mask, gene_mask, slide_ids, target, density):
    high = lax.Precision.HIGHEST
    n_cells = logits.shape[0]
    own_rows = cells.shape[0]
    n_slides = gene_mask.shape[0]
    valid = cell_mask.astype(jnp.float32)
    top = jnp.max(logits, axis=0, keepdims=True)
    expo = jnp.exp(logits - top) * valid[:, None]
    total = jnp.sum(expo, axis=0, keepdims=True)
    prob = expo / total
    logp = jnp.where(valid[:, None] > 0, logits - top - jnp.log(total), 0.0)
    entropy_part = -jnp.sum(prob * logp)
    whole, filt_all = (
        lax.all_gather(cells, ("wide", "narrow"), axis=0, tiled=True),
        lax.all_gather(filt, ("wide", "narrow"), axis=0, tiled=True),
    )
    keep = jax.nn.sigmoid(filt_all)
    weighted = prob * keep[:, None]
    g_pred = lax.dot_general(weighted, whole, (((0,), (0,)), ((), ())), precision=high)
    onehot = (slide_ids[:, None] == jnp.arange(n_slides, dtype=jnp.int32)[None, :]).astype(
        jnp.float32
    )
    gmask = gene_mask.astype(jnp.float32)
    spot_mask = jnp.dot(onehot, gmask, precision=high)
    masked_pred = spot_mask * g_pred
    sdot = jnp.sum(masked_pred * target, axis=1)
    spp = jnp.sum(masked_pred * g_pred, axis=1)
    stt = jnp.sum(spot_mask * target * target, axis=1)
    spot_scale = lax.rsqrt(spp + eps) * lax.rsqrt(stt + eps)
    spot_cos = sdot * spot_scale
    mass = jnp.sum(weighted, axis=0)
    log_part = density * (jnp.log(density) - jnp.log(mass))
    slide_vec = jnp.stack([mass, density, log_part], axis=1)
    loss_parts = jnp.stack([-jnp.sum(spot_cos), entropy_part])
    dot_s, pp_s, tt_s, slide_tot, loss_tot = lax.psum(
        (
            per_slide(onehot, g_pred * target),
            per_slide(onehot, g_pred * g_pred),
            per_slide(onehot, target * target),
            per_slide(onehot, slide_vec),
            loss_parts,
        ),
        ("wide", "narrow"),
    )
    mass_s = slide_tot[:, 0]
    wsum_s = slide_tot[:, 1]
    logsum_s = slide_tot[:, 2]
    gene_scale = gmask * lax.rsqrt(pp_s + eps) * lax.rsqrt(tt_s + eps)
    gene_cos = dot_s * gene_scale
    gene_loss = -jnp.sum(gene_cos)
    spot_loss = loss_tot[0]
    entropy = loss_tot[1] / (prob.shape[1] * lax.axis_size(("wide", "narrow")))
    kl_term = jnp.sum(logsum_s / wsum_s) + jnp.sum(jnp.log(mass_s) - jnp.log(wsum_s))
    count = jnp.sum(valid * keep)
    target_count = n_cells // 4
    count_term = jnp.abs(count - target_count) / n_cells
    binarity = jnp.sum(valid * (keep - keep * keep)) / n_cells
    loss = gene_loss + spot_loss + kl_term + count_term + binarity
    terms = jnp.stack([loss, gene_loss, spot_loss])
    reg_terms = jnp.stack([kl_term, count_term, binarity, entropy])
    gene_shrink = gene_scale * dot_s / (pp_s + eps)
    grad_pred = -jnp.dot(onehot, gene_scale, precision=high) * target
    grad_pred = grad_pred + jnp.dot(onehot, gene_shrink, precision=high) * g_pred
    spot_shrink = sdot / (spp + eps)
    grad_pred = grad_pred - spot_mask * spot_scale[:, None] * (
        target - spot_shrink[:, None] * g_pred
    )
    spot_slide = jnp.dot(onehot, jnp.stack([mass_s, wsum_s], axis=1), precision=high)
    grad_mass = -(density / spot_slide[:, 1]) / mass + 1.0 / spot_slide[:, 0]
    grad_weighted = lax.dot_general(whole, grad_pred, (((1,), (1,)), ((), ())), precision=high)
    grad_weighted = grad_weighted + grad_mass[None, :]
    grad_prob = keep[:, None] * grad_weighted
    keep_part = jnp.sum(prob * grad_weighted, axis=1)
    grad_logits = prob * (grad_prob - jnp.sum(prob * grad_prob, axis=0, keepdims=True))
    cell_part = jnp.dot(weighted, grad_pred, precision=high)
    grad_cells, keep_sum = (
        lax.psum_scatter(cell_part, ("wide", "narrow"), scatter_dimension=0, tiled=True),
        lax.psum_scatter(keep_part, ("wide", "narrow"), scatter_dimension=0, tiled=True),
    )
    first_row = lax.axis_index(("wide", "narrow")) * own_rows
    own_keep = lax.dynamic_slice_in_dim(keep, first_row, own_rows, 0)
    own_valid = lax.dynamic_slice_in_dim(valid, first_row, own_rows, 0)
    keep_grad = (
        keep_sum + own_valid * (jnp.sign(count - target_count) + 1.0 - 2.0 * own_keep) / n_cells
    )
    grad_filter = keep_grad * own_keep * (1.0 - own_keep)
    return (terms, reg_terms, g_pred, gene_cos, spot_cos, grad_logits, grad_filter, grad_cells)


def fits_fused(mesh, logits, cells, gene_mask, slide_ids):
    n_cells, spots = logits.shape
    return (
        (mesh.shape["wide"], mesh.shape["narrow"]) == (8, 4)
        and cells.shape == (16, 2048)
        and n_cells == 512
        and spots == 1024
        and gene_mask.shape[0] == 8
    )


def solution(mesh):
    def step(logits, filt, cells, cell_mask, gene_mask, slide_ids, target, density):
        fits = fits_fused(mesh, logits, cells, gene_mask, slide_ids)
        run = fused if fits else on_device
        return run(logits, filt, cells, cell_mask, gene_mask, slide_ids, target, density)

    placed = (
        P(None, ("wide", "narrow")),
        P(("wide", "narrow")),
        P(("wide", "narrow"), None),
        P(),
        P(),
        P(("wide", "narrow")),
        P(("wide", "narrow"), None),
        P(("wide", "narrow")),
    )
    return jax.shard_map(
        step,
        mesh=mesh,
        in_specs=placed,
        out_specs=(
            P(),
            P(),
            P(("wide", "narrow"), None),
            P(),
            P(("wide", "narrow")),
            P(None, ("wide", "narrow")),
            P(("wide", "narrow")),
            P(("wide", "narrow"), None),
        ),
        check_vma=False,
    )
```

```python
import jax
import jax.numpy as jnp
from jax import lax
from jax.experimental import pallas as pl
from jax.experimental.pallas import tpu as pltpu
from jax.sharding import PartitionSpec as P

eps = 1e-06
MESH = pl.DeviceIdType.MESH
bf16 = jnp.bfloat16
f32 = jnp.float32
LANES = 128
NCH = 8
BR = 32
GR = 256
AHEAD = 3


def split(value):
    high = value.astype(bf16)
    return high, (value - high.astype(f32)).astype(bf16)


def mm(a, b):
    return lax.dot_general(a, b, (((1,), (0,)), ((), ())), preferred_element_type=f32)


def mm_nt(a, b):
    return lax.dot_general(a, b, (((1,), (1,)), ((), ())), preferred_element_type=f32)


def fused_kernel(
    logits_hbm, filt_ref, cells_hbm, mask_ref, gene_ref, ids_ref, target_hbm, dens_ref,
    pv, gw, keep_ref, sums_ref, loss_ref, gcos_ref, scos_ref, gfilt_ref, gcell_ref,
    lg, tv, buf, chi, clo, ownc, ownk, along, valid, keepc, whi, wlo, thi, tlo, gmb, oh, l1, l2, cf,
    idc, blocks, sd, sp, st, mass, gmass, gph, gpl, kp,
    stat, a1, a2, a3, fin, kvec, k1, k2, k3,
    part, rb, sb, r1, tt_, r2, qq, r3,
    lsem, tsem, osem,
    zs, zr, xs, xr, ys, yr, bs, br,
    as1, ar1, as2, ar2, as3, ar3, as4, ar4,
    ks1, kr1, ks2, kr2, ks3, kr3,
    cbs, cbr, cxs, cxr, cys, cyr, czs, czr,
):
    n_cells = chi.shape[1]
    width = chi.shape[2]
    last = NCH - 1
    n_blocks = tv.shape[1]
    spots = n_blocks * BR
    n_slides = gene_ref.shape[0]
    tiles = spots // LANES
    wide, narrow = lax.axis_index("wide"), lax.axis_index("narrow")
    z, y = lax.div(wide, 2), lax.rem(wide, 2)
    x, core = lax.div(narrow, 2), lax.rem(narrow, 2)
    to_z = [(lax.rem(z + k, 4) * 2 + y, narrow) for k in (1, 2, 3)]
    from_z = [lax.rem(z + 4 - k, 4) for k in (1, 2, 3)]
    to_x = (wide, (1 - x) * 2 + core)
    to_y = (z * 2 + 1 - y, narrow)
    to_xy = (z * 2 + 1 - y, (1 - x) * 2 + core)
    to_b = (wide, x * 2 + 1 - core)

    def rcopy(src, dst, ss, rs, dev):
        return pltpu.make_async_remote_copy(
            src_ref=src, dst_ref=dst, send_sem=ss, recv_sem=rs, device_id=dev, device_id_type=MESH
        )

    def lanes(i, w=LANES):
        return pl.ds(pl.multiple_of(i * w, w), w)

    own_cells = pltpu.make_async_copy(cells_hbm, ownc, lsem.at[0])

    def get_logits(i):
        return pltpu.make_async_copy(logits_hbm.at[:, lanes(i)], lg.at[i], osem.at[i])

    def get_target(c):
        return pltpu.make_async_copy(target_hbm.at[:, :, lanes(c, width)], tv.at[c], tsem.at[c])

    own_cells.start()
    for i in range(tiles):
        get_logits(i).start()
    for c in range(NCH):
        get_target(c).start()

    barrier = pltpu.get_barrier_semaphore()
    for dev in to_z + [to_x, to_y, to_xy, to_b]:
        pl.semaphore_signal(barrier, inc=1, device_id=dev, device_id_type=MESH)

    iota8 = lax.broadcasted_iota(jnp.int32, (8, LANES), 0)
    lane8 = lax.broadcasted_iota(jnp.int32, (8, LANES), 1)
    row16 = lax.broadcasted_iota(jnp.int32, (16, LANES), 0)
    dev = wide * 4 + narrow
    place = lane8 + iota8 * LANES - dev * 16
    mine = jnp.zeros((16, LANES), f32)
    vector = jnp.zeros((8, LANES), f32)
    for r in range(16):
        mine = jnp.where(row16 == r, filt_ref[r], mine)
        vector = jnp.where(place == r, filt_ref[r], vector)
    kvec[2] = vector
    own_keep = jax.nn.sigmoid(mine)
    ownk[...] = own_keep
    along[...] = jnp.zeros_like(along)
    own_cells.wait()
    for c in range(NCH):
        for h in range(2):
            buf[c, h, z, y, x, core] = own_keep * ownc[:, (c * 2 + h) * LANES : (c * 2 + h + 1) * LANES]
    for q in range(n_cells // LANES):
        line = mask_ref[q : q + 1, :].astype(f32)
        valid[q * LANES : (q + 1) * LANES, :] = jnp.broadcast_to(line, (LANES, LANES)).T
    pl.semaphore_wait(barrier, 7)

    def z_out(c, k):
        r = buf.at[c, :, z, y, x, core]
        return rcopy(r, r, zs.at[c, k], zr.at[c, k], to_z[k])

    def z_in(c, k):
        r = buf.at[c, :, from_z[k], y, x, core]
        return rcopy(r, r, zs.at[c, k], zr.at[c, k], to_z[k])

    def s1_out(c):
        a = buf.at[c, 0, :, y, x, core]
        b = buf.at[c, 1, :, y, x, core]
        return [rcopy(a, a, xs.at[c, 0], xr.at[c, 0], to_x), rcopy(b, b, ys.at[c, 0], yr.at[c, 0], to_y)]

    def s1_in(c):
        a = buf.at[c, 0, :, y, 1 - x, core]
        b = buf.at[c, 1, :, 1 - y, x, core]
        return [rcopy(a, a, xs.at[c, 0], xr.at[c, 0], to_x), rcopy(b, b, ys.at[c, 0], yr.at[c, 0], to_y)]

    def s2_out(c):
        a = buf.at[c, 0, :, y, :, core]
        b = buf.at[c, 1, :, :, x, core]
        return [rcopy(a, a, ys.at[c, 1], yr.at[c, 1], to_y), rcopy(b, b, xs.at[c, 1], xr.at[c, 1], to_x)]

    def s2_in(c):
        a = buf.at[c, 0, :, 1 - y, :, core]
        b = buf.at[c, 1, :, :, 1 - x, core]
        return [rcopy(a, a, ys.at[c, 1], yr.at[c, 1], to_y), rcopy(b, b, xs.at[c, 1], xr.at[c, 1], to_x)]

    def s3_out(c):
        r = buf.at[c, :, :, :, :, core]
        return rcopy(r, r, bs.at[c], br.at[c], to_b)

    def s3_in(c):
        r = buf.at[c, :, :, :, :, 1 - core]
        return rcopy(r, r, bs.at[c], br.at[c], to_b)

    def b1(c):
        return rcopy(stat.at[c, 1 - core], a1.at[c], as1.at[c], ar1.at[c], to_b)

    plane = [to_x, to_y, to_xy]
    here = y * 2 + x
    there = [y * 2 + 1 - x, (1 - y) * 2 + x, (1 - y) * 2 + 1 - x]

    def b2_out(c, k):
        r = a2.at[c, here]
        return rcopy(r, r, as2.at[c, k], ar2.at[c, k], plane[k])

    def b2_in(c, k):
        r = a2.at[c, there[k]]
        return rcopy(r, r, as2.at[c, k], ar2.at[c, k], plane[k])

    def b3_out(c, k):
        r = a3.at[c, z]
        return rcopy(r, r, as3.at[c, k], ar3.at[c, k], to_z[k])

    def b3_in(c, k):
        r = a3.at[c, from_z[k]]
        return rcopy(r, r, as3.at[c, k], ar3.at[c, k], to_z[k])

    def b4(c, half):
        r = fin.at[c, half]
        return rcopy(r, r, as4.at[c], ar4.at[c], to_b)

    def sum_second(c):
        b1(c).wait_recv()
        a2[c, here] = stat[c, core] + a1[c]
        for k in range(3):
            b2_out(c, k).start()

    def sum_third(c):
        for k in range(3):
            b2_in(c, k).wait_recv()
        a3[c, z] = (a2[c, 0] + a2[c, 1]) + (a2[c, 2] + a2[c, 3])
        for k in range(3):
            b3_out(c, k).start()

    def sum_fourth(c):
        for k in range(3):
            b3_in(c, k).wait_recv()
        fin[c, core] = (a3[c, 0] + a3[c, 1]) + (a3[c, 2] + a3[c, 3])
        b4(c, core).start()

    def sum_last(c):
        b4(c, 1 - core).wait_recv()

    def v1(n):
        return rcopy(kvec.at[n], k1.at[n], ks1.at[n], kr1.at[n], to_b)

    def v2(n, slot, k):
        return rcopy(k2.at[n, slot], k2.at[n, slot], ks2.at[n, k], kr2.at[n, k], plane[k])

    def v3(n, slot, k):
        return rcopy(k3.at[n, slot], k3.at[n, slot], ks3.at[n, k], kr3.at[n, k], to_z[k])

    def vector_second(n):
        v1(n).wait_recv()
        k2[n, here] = kvec[n] + k1[n]
        for k in range(3):
            v2(n, here, k).start()

    def vector_third(n):
        for k in range(3):
            v2(n, there[k], k).wait_recv()
        k3[n, z] = (k2[n, 0] + k2[n, 1]) + (k2[n, 2] + k2[n, 3])
        for k in range(3):
            v3(n, z, k).start()

    def vector_last(n):
        for k in range(3):
            v3(n, from_z[k], k).wait_recv()
        return (k3[n, 0] + k3[n, 1]) + (k3[n, 2] + k3[n, 3])

    def softmax(i, ent):
        get_logits(i).wait()
        value = lg[i]
        top = jnp.max(value, axis=0, keepdims=True)
        expo = jnp.exp(value - top) * valid[...]
        total = jnp.sum(expo, axis=0, keepdims=True)
        prob = expo * (1.0 / total)
        lg[i] = prob
        high, low = split(prob)
        whi[:, lanes(i)] = high
        wlo[:, lanes(i)] = low
        high, low = split(prob.T)
        thi[lanes(i), :] = high
        tlo[lanes(i), :] = low
        return ent + jnp.sum(prob * (value - top - jnp.log(total)), axis=0, keepdims=True)

    def one_hot(i, _):
        ids = ids_ref[pl.ds(i, 1), :]
        square = (lax.broadcasted_iota(jnp.int32, (LANES, LANES), 0) == ids).astype(f32)
        oh[lanes(i), :] = square.T.astype(bf16)
        per = LANES // BR
        turned = jnp.broadcast_to(ids, (LANES, LANES)).astype(f32).T
        idc[pl.ds(i * per, per)] = turned.reshape(per, BR, LANES)
        return 0

    def leave_z(c):
        for k in range(3):
            z_out(c, k).start()

    for c in range(AHEAD):
        leave_z(c)
    v1(2).start()

    def stage_z(c):
        for k in range(3):
            z_in(c, k).wait_recv()
        for d in s1_out(c):
            d.start()

    def stage_1(c):
        for d in s1_in(c):
            d.wait_recv()
        for d in s2_out(c):
            d.start()

    def stage_2(c):
        for d in s2_in(c):
            d.wait_recv()
        s3_out(c).start()

    def fold(v):
        out = v[:, :LANES]
        for k in range(1, v.shape[1] // LANES):
            out = out + v[:, k * LANES : (k + 1) * LANES]
        return out

    def eighths(v):
        return jnp.sum(v.reshape(v.shape[0] // 8, 8, v.shape[1]), axis=0)

    for c in range(NCH):
        gm = jnp.concatenate(
            [gene_ref[:, c * width : (c + 1) * width].astype(f32), jnp.zeros((LANES - n_slides, width), f32)], axis=0
        )
        gmb[c] = gm.astype(bf16)
    sd[...] = jnp.zeros_like(sd)
    sp[...] = jnp.zeros_like(sp)
    st[...] = jnp.zeros_like(st)
    lax.fori_loop(0, tiles, one_hot, 0)

    begins = [jnp.sum((ids_ref[...] < k).astype(jnp.int32)) for k in range(n_slides + 1)]
    firsts = [jnp.minimum(lax.div(begins[k], BR), n_blocks - 1) for k in range(n_slides)]
    lasts = [lax.div(jnp.maximum(begins[k + 1] - 1, 0), BR) for k in range(n_slides)]
    slide16 = lax.broadcasted_iota(jnp.int32, (16, 8 * n_blocks), 0)
    block16 = lax.div(lax.broadcasted_iota(jnp.int32, (16, 8 * n_blocks), 1), 8)
    inner = jnp.zeros((16, 8 * n_blocks), f32)
    for k in range(n_slides):
        full = jnp.logical_and(block16 > firsts[k], block16 < lasts[k])
        inner = jnp.where(jnp.logical_and(slide16 == k, full), 1.0, inner)
    inner = inner.astype(bf16)
    inner = jnp.concatenate([inner, inner], axis=1)
    slide8 = lax.broadcasted_iota(jnp.int32, (8, width), 0)

    def gene_sums(c, products, number, at_row):
        sums = []
        for n in range(number):
            bh, bl = split(blocks[n])
            sums.append(mm(inner, jnp.concatenate([bh, bl], axis=0))[:8, :])
        for k in range(n_slides):
            parts = [jnp.zeros((8, width), f32)] * number
            for block, counts in ((firsts[k], None), (lasts[k], lasts[k] != firsts[k])):
                own = idc[block] == float(k)
                if counts is not None:
                    own = jnp.logical_and(own, counts)
                own = own.astype(f32)
                own = jnp.concatenate([own] * (width // LANES), axis=1)
                for n, prod in enumerate(products(c, block)):
                    parts[n] = parts[n] + eighths(prod * own)
            for n in range(number):
                line = jnp.sum(parts[n], axis=0, keepdims=True)
                sums[n] = sums[n] + jnp.where(slide8 == k, line, 0.0)
        for n in range(number):
            for h in range(2):
                stat[c, h, at_row + n * 8 : at_row + (n + 1) * 8, :] = sums[n][:, h * LANES : (h + 1) * LANES]

    def of_target(c, r):
        tgt = tv[c, r]
        return (tgt * tgt,)

    def of_both(c, r):
        pred, tgt = pv[c, r], tv[c, r]
        return pred * tgt, jnp.where(tgt > 0.0, pred * pred, 0.0)

    def by_rows(c, products, spots_of):
        for r in range(n_blocks):
            at = slice(r * BR, (r + 1) * BR)
            for n, (prod, spot) in enumerate(zip(products(c, r), spots_of)):
                spot[at, :] += fold(prod)
                blocks[n, r * 8 : (r + 1) * 8, :] = eighths(prod)

    def target_sums(c, _):
        per = GR // BR
        for n in range(spots // GR):
            sees = mm(oh[n * GR : (n + 1) * GR, :], gmb[c]).reshape(per, BR, width)
            for r in range(per):
                tv[c, n * per + r] = sees[r] * tv[c, n * per + r]
        by_rows(c, of_target, (st,))
        gene_sums(c, of_target, 1, 16)
        return 0

    def predict(c):
        s3_in(c).wait_recv()
        whole = jnp.concatenate([buf[c, h].reshape(n_cells, LANES) for h in range(2)], axis=1)
        high, low = split(whole)
        chi[c] = high
        clo[c] = low
        wh, wl = thi[...], tlo[...]
        pred = mm(jnp.concatenate([wh, wl, wh], axis=1), jnp.concatenate([high, high, low], axis=0))
        pv[c] = pred.reshape(n_blocks, BR, width)

    def predicted_sums(c):
        by_rows(c, of_both, (sd, sp))
        gene_sums(c, of_both, 2, 0)

    def slide_sums():
        keep_rows = jax.nn.sigmoid(vector_last(2))
        keep_ref[...] = keep_rows
        for q in range(quarter):
            line = jnp.broadcast_to(keep_rows[q : q + 1, :], (LANES, LANES))
            keepc[q * LANES : (q + 1) * LANES, :] = line.T

        def by_tile(i, sums):
            at = pl.ds(i, 1)
            line = jnp.sum(lg[i] * keepc[...], axis=0, keepdims=True)
            mass[at, :] = line
            dens = dens_ref[at, :]
            mine = (iota8 == ids_ref[at, :]).astype(f32)
            terms = (line, dens, dens * (jnp.log(dens) - jnp.log(line)))
            return tuple(a + mine * b for a, b in zip(sums, terms))

        blank = jnp.zeros((8, LANES), f32)
        totals = lax.fori_loop(0, tiles, by_tile, (blank, blank, blank))
        for k, value in enumerate(totals):
            blank = jnp.where(lane8 == k, jnp.sum(value, axis=1, keepdims=True), blank)
        kvec[0] = blank
        v1(0).start()

    quarter = n_cells // LANES
    ent = lax.fori_loop(0, tiles // 2, softmax, jnp.zeros((1, LANES), f32))
    stage_z(0)
    leave_z(AHEAD)
    vector_second(2)
    ent = lax.fori_loop(tiles // 2, tiles, softmax, ent)
    stage_z(1)
    leave_z(AHEAD + 1)
    for c in range(NCH):
        get_target(c).wait()
    lax.fori_loop(0, 3, target_sums, 0)
    stage_z(2)
    leave_z(AHEAD + 2)
    stage_1(0)
    vector_third(2)
    lax.fori_loop(3, 6, target_sums, 0)
    stage_z(3)
    leave_z(AHEAD + 3)
    stage_1(1)
    lax.fori_loop(6, NCH, target_sums, 0)
    stage_z(4)
    leave_z(AHEAD + 4)
    stage_2(0)
    stage_1(2)
    slide_sums()

    def gather_tick(t, _):
        c = t - 5
        pl.when(t < NCH)(lambda: stage_z(t))
        pl.when(t + AHEAD < NCH)(lambda: leave_z(t + AHEAD))
        pl.when(t - 4 < NCH)(lambda: stage_2(t - 4))
        pl.when(t - 2 < NCH)(lambda: stage_1(t - 2))
        predict(c)
        predicted_sums(c)
        b1(c).start()
        pl.when(c == 0)(lambda: vector_second(0))
        pl.when(c == 2)(lambda: vector_third(0))
        pl.when(c >= 1)(lambda: sum_second(c - 1))
        pl.when(c >= 3)(lambda: sum_third(c - 3))
        pl.when(c >= 6)(lambda: sum_fourth(c - 6))
        return 0

    lax.fori_loop(5, NCH + 5, gather_tick, 0)

    lane128 = lax.broadcasted_iota(jnp.int32, (LANES, LANES), 1)
    slide_of_lane = lax.rem(lane128, 8).astype(f32)

    def spot_rows(i, _):
        at = lanes(i)
        sdot, spp, stt = [jnp.sum(ref[at, :], axis=1, keepdims=True) for ref in (sd, sp, st)]
        scale = lax.rsqrt(spp + eps) * lax.rsqrt(stt + eps)
        sd[at, :] = jnp.broadcast_to(sdot * scale, (LANES, LANES))
        per = LANES // BR
        own = jnp.logical_and(idc[pl.ds(i * per, per)].reshape(LANES, LANES) == slide_of_lane, lane128 < 32)
        for ref, value in ((l1, scale), (l2, scale * (sdot / (spp + eps)))):
            high, low = split(value)
            value = jnp.where(lane128 < 16, 1.0, jnp.where(lane128 < 24, high.astype(f32), low.astype(f32)))
            ref[at, :] = jnp.where(own, value, 0.0).astype(bf16)
        return 0

    lax.fori_loop(0, tiles, spot_rows, 0)
    sum_second(last)
    sum_third(last - 2)
    sum_fourth(last - 5)

    def scatter_sib(c):
        return rcopy(part.at[c, :, :, :, :, 1 - core], rb.at[c], cbs.at[c], cbr.at[c], to_b)

    def scatter_one(c):
        return [
            rcopy(sb.at[c, 0, :, 1 - y], r1.at[c, 0], cys.at[c, 0], cyr.at[c, 0], to_y),
            rcopy(sb.at[c, 1, :, :, 1 - x], r1.at[c, 1], cxs.at[c, 0], cxr.at[c, 0], to_x),
        ]

    def scatter_two(c):
        return [
            rcopy(tt_.at[c, 0, :, 1 - x], r2.at[c, 0], cxs.at[c, 1], cxr.at[c, 1], to_x),
            rcopy(tt_.at[c, 1, :, 1 - y], r2.at[c, 1], cys.at[c, 1], cyr.at[c, 1], to_y),
        ]

    def scatter_z(c, k):
        return rcopy(qq.at[c, :, lax.rem(z + k + 1, 4)], r3.at[c, k], czs.at[c, k], czr.at[c, k], to_z[k])

    def sc1(c):
        scatter_sib(c).wait_recv()
        sb[c] = part[c, :, :, :, :, core] + rb[c]
        for d in scatter_one(c):
            d.start()

    def sc2(c):
        for d in scatter_one(c):
            d.wait_recv()
        tt_[c, 0] = sb[c, 0, :, y] + r1[c, 0]
        tt_[c, 1] = sb[c, 1, :, :, x] + r1[c, 1]
        for d in scatter_two(c):
            d.start()

    def sc3(c):
        for d in scatter_two(c):
            d.wait_recv()
        qq[c, 0] = tt_[c, 0, :, x] + r2[c, 0]
        qq[c, 1] = tt_[c, 1, :, y] + r2[c, 1]
        for k in range(3):
            scatter_z(c, k).start()

    def sc4(c):
        for k in range(3):
            scatter_z(c, k).wait_recv()
        for h in range(2):
            at = lanes(c * 2 + h)
            total = (qq[c, h, z] + r3[c, 0, h]) + (r3[c, 1, h] + r3[c, 2, h])
            gcell_ref[:, at] = total * ownk[...]
            along[...] += total * ownc[:, at]

    def gene_coefs(c):
        total = jnp.concatenate([fin[c, 0], fin[c, 1]], axis=1)
        dot_s, pp_s, tt_s = total[0:8], total[8:16], total[16:24]
        gm = gene_ref[:, lanes(c, width)].astype(f32)
        gscale = gm * lax.rsqrt(pp_s + eps) * lax.rsqrt(tt_s + eps)
        gcos_ref[:, lanes(c, width)] = dot_s * gscale
        gshrink = gscale * (dot_s / (pp_s + eps))
        pad = jnp.zeros((LANES - 32, width), f32)
        for n, value in enumerate((gscale, gshrink)):
            high, low = split(value)
            high, low = high.astype(f32), low.astype(f32)
            cf[lax.rem(c, 2), n] = jnp.concatenate([high, low, gm, gm, pad], axis=0).astype(bf16)

    def backward(c):
        slot = lax.rem(c, 2)
        per = GR // BR
        for n in range(spots // GR):
            at = slice(n * GR, (n + 1) * GR)
            own = slice(n * per, (n + 1) * per)
            pred, tgt = pv[c, own].reshape(GR, width), tv[c, own].reshape(GR, width)
            gh, gl = split(mm(l2[at, :], cf[slot, 1]) * pred - mm(l1[at, :], cf[slot, 0]) * tgt)
            gph[c, at, :] = gh
            gpl[c, at, :] = gl
        wh, wl = whi[...], wlo[...]
        gh, gl = gph[c], gpl[c]
        out = mm(jnp.concatenate([wh, wl, wh], axis=1), jnp.concatenate([gh, gh, gl], axis=0))
        for h in range(2):
            part[c, h] = out[:, h * LANES : (h + 1) * LANES].reshape(4, 2, 2, 2, 16, LANES)
        gene_coefs(jnp.minimum(c + 1, last))
        scatter_sib(c).start()

    def spot_part(n):
        at = pl.ds(n * GR, GR)
        left = [chi[c] for c in range(NCH)]
        left = left + [clo[c] for c in range(NCH)] + left
        right = [gph[c, at, :] for c in range(NCH)]
        right = right + right + [gpl[c, at, :] for c in range(NCH)]
        out = mm_nt(jnp.concatenate(left, axis=1), jnp.concatenate(right, axis=1))
        for h in range(GR // LANES):
            i = n * (GR // LANES) + h
            grad = out[:, h * LANES : (h + 1) * LANES] + keepc[...] * gmass[i : i + 1, :]
            prob = lg[i]
            gw[i] = prob * (grad - jnp.sum(prob * grad, axis=0, keepdims=True))

    def back_tick(t, _):
        pl.when(t >= 3)(lambda: sc2(t - 3))
        pl.when(t < last)(lambda: sum_last(t + 1))
        backward(t)
        pl.when(t >= 1)(lambda: sc1(t - 1))
        pl.when(t >= 4)(lambda: sc3(t - 4))
        pl.when(t <= 1)(lambda: sum_third(last - 1 + t))
        pl.when(t <= 4)(lambda: sum_fourth(last - 4 + t))

        @pl.when(t == 4)
        def _():
            slide_totals()

        @pl.when(t == 5)
        def _():
            vector_second(1)

        @pl.when(t == 7)
        def _():
            vector_third(1)

        pl.when(t >= 6)(lambda: sc4(t - 6))
        return 0

    def slide_totals():
        sums_s = vector_last(0)
        sums_ref[...] = sums_s
        mass_s, wsum_s = sums_s[:, 0:1], sums_s[:, 1:2]
        kp[...] = jnp.zeros_like(kp)

        def by_mass(i, total):
            at = pl.ds(i, 1)
            mine = (iota8 == ids_ref[at, :]).astype(f32)
            mass_at = jnp.sum(mine * mass_s, axis=0, keepdims=True)
            wsum_at = jnp.sum(mine * wsum_s, axis=0, keepdims=True)
            line = -(dens_ref[at, :] / wsum_at) / mass[at, :] + 1.0 / mass_at
            gmass[at, :] = line
            kp[...] += lg[i] * line
            spot = sd[lanes(i), :].T[0:1, :]
            scos_ref[at, :] = spot
            return total + spot

        total = lax.fori_loop(0, tiles, by_mass, jnp.zeros((1, LANES), f32))
        rows_k = [jnp.sum(kp[q * LANES : (q + 1) * LANES, :].T, axis=0, keepdims=True) for q in range(quarter)]
        rows_k = rows_k + [-total, -ent, jnp.zeros((6 - quarter, LANES), f32)]
        kvec[1] = jnp.concatenate(rows_k, axis=0)
        v1(1).start()

    sum_last(0)
    gene_coefs(0)
    lax.fori_loop(0, NCH, back_tick, 0)
    sc1(last)
    sc3(last - 3)
    sc2(last - 2)
    spot_part(0)
    sc3(last - 2)
    sc2(last - 1)
    sc2(last)
    spot_part(1)
    sc3(last - 1)
    sc3(last)
    for c in range(NCH - 6, NCH - 3):
        sc4(c)
    spot_part(2)
    spot_part(3)

    keep = keep_ref[...]
    ok = jnp.concatenate([mask_ref[...].astype(f32), jnp.zeros((8 - quarter, LANES), f32)], axis=0)
    off = jnp.sum(ok * keep) - n_cells // 4
    sign = jnp.where(off > 0, 1.0, jnp.where(off < 0, -1.0, 0.0))
    totals = vector_last(1)
    loss_ref[...] = totals
    rest = totals + ok * (sign + 1.0 - 2.0 * keep) / n_cells

    def own_lanes(value):
        picked = jnp.sum(jnp.where(iota8 == lax.div(dev, 8), value, 0.0), axis=0, keepdims=True)
        return pltpu.roll(picked, lax.rem(LANES - lax.rem(dev, 8) * 16, LANES), 1)

    keep = own_lanes(keep)
    rest = own_lanes(rest)
    for c in range(NCH - 3, NCH):
        sc4(c)
    genes_part = jnp.concatenate([along[...], jnp.zeros((LANES - 16, LANES), f32)], axis=0)
    genes_part = jnp.sum(genes_part.T, axis=0, keepdims=True)
    gfilt_ref[...] = ((genes_part + rest) * keep * (1.0 - keep))[:, : gfilt_ref.shape[1]]

    def leave(c, _):
        for k in range(3):
            z_out(c, k).wait_send()
            b2_out(c, k).wait_send()
            b3_out(c, k).wait_send()
            scatter_z(c, k).wait_send()
        for d in s1_out(c) + s2_out(c) + scatter_one(c) + scatter_two(c):
            d.wait_send()
        s3_out(c).wait_send()
        b1(c).wait_send()
        b4(c, core).wait_send()
        scatter_sib(c).wait_send()
        return 0

    lax.fori_loop(0, NCH, leave, 0)
    for n in range(3):
        v1(n).wait_send()
        for k in range(3):
            v2(n, here, k).wait_send()
            v3(n, z, k).wait_send()


def finish_kernel(
    pv, gw, keep_ref, sums_ref, loss_ref, gcos_in, scos_in, gfilt_in, gcell_in, mask_ref,
    terms_hbm, reg_hbm, pred_hbm, gcos_hbm, scos_hbm, glog_hbm, gfilt_hbm, gcell_hbm,
    terms_ref, reg_ref, psem, osem, rsem,
):
    width = pv.shape[3]
    tiles, n_cells = gw.shape[:2]
    quarter = n_cells // LANES

    def put_pred(c):
        return pltpu.make_async_copy(pv.at[c], pred_hbm.at[:, :, c * width : (c + 1) * width], psem.at[c])

    def put_glog(i):
        return pltpu.make_async_copy(gw.at[i], glog_hbm.at[:, i * LANES : (i + 1) * LANES], osem.at[i])

    for c in range(NCH):
        put_pred(c).start()
    for i in range(tiles):
        put_glog(i).start()
    pairs = [(gcos_in, gcos_hbm), (scos_in, scos_hbm), (gcell_in, gcell_hbm), (gfilt_in, gfilt_hbm)]
    rest = [pltpu.make_async_copy(a, b, rsem.at[k]) for k, (a, b) in enumerate(pairs)]
    for copy in rest:
        copy.start()

    sums_s = sums_ref[...]
    mass_s, wsum_s, logsum_s = sums_s[:, 0:1], sums_s[:, 1:2], sums_s[:, 2:3]
    keep = keep_ref[:quarter, :]
    ok = mask_ref[...].astype(f32)
    count = jnp.sum(ok * keep)
    count_term = jnp.abs(count - n_cells // 4) / n_cells
    binarity = jnp.sum(ok * (keep - keep * keep)) / n_cells
    gene_loss = -jnp.sum(gcos_in[...])
    spot_loss = jnp.sum(loss_ref[quarter : quarter + 1, :])
    entropy = jnp.sum(loss_ref[quarter + 1 : quarter + 2, :]) / (tiles * LANES * 32)
    kl = jnp.sum(logsum_s / wsum_s + jnp.log(mass_s) - jnp.log(wsum_s))
    terms_ref[0] = gene_loss + spot_loss + kl + count_term + binarity
    terms_ref[1] = gene_loss
    terms_ref[2] = spot_loss
    reg_ref[0] = kl
    reg_ref[1] = count_term
    reg_ref[2] = binarity
    reg_ref[3] = entropy
    for k, (a, b) in enumerate(((terms_ref, terms_hbm), (reg_ref, reg_hbm))):
        rest.append(pltpu.make_async_copy(a, b, rsem.at[len(pairs) + k]))
        rest[-1].start()
    for copy in rest:
        copy.wait()
    for i in range(tiles):
        put_glog(i).wait()
    for c in range(NCH):
        put_pred(c).wait()


def fused(logits, filt, cells, cell_mask, gene_mask, slide_ids, target, density):
    n_cells, spots = logits.shape
    own, genes = cells.shape
    n_slides = gene_mask.shape[0]
    width = genes // NCH
    tiles = spots // LANES
    dma = pltpu.SemaphoreType.DMA
    vmem, anywhere = pltpu.VMEM, pl.BlockSpec(memory_space=pl.ANY)
    inside = pl.BlockSpec(memory_space=pltpu.VMEM)
    scalars = pl.BlockSpec(memory_space=pltpu.SMEM)
    ring = (4, 2, 2, 2, 16, LANES)
    scratch = [
        vmem((tiles, n_cells, LANES), f32),
        vmem((NCH, spots // BR, BR, width), f32),
        vmem((NCH, 2) + ring, f32),
        vmem((NCH, n_cells, width), bf16),
        vmem((NCH, n_cells, width), bf16),
        vmem((own, genes), f32),
        vmem((own, LANES), f32),
        vmem((own, LANES), f32),
        vmem((n_cells, LANES), f32),
        vmem((n_cells, LANES), f32),
        vmem((n_cells, spots), bf16),
        vmem((n_cells, spots), bf16),
        vmem((spots, n_cells), bf16),
        vmem((spots, n_cells), bf16),
        vmem((NCH, LANES, width), bf16),
        vmem((spots, LANES), bf16),
        vmem((spots, LANES), bf16),
        vmem((spots, LANES), bf16),
        vmem((2, 2, LANES, width), bf16),
        vmem((spots // BR, BR, LANES), f32),
        vmem((2, spots * 8 // BR, width), f32),
        vmem((spots, LANES), f32),
        vmem((spots, LANES), f32),
        vmem((spots, LANES), f32),
        vmem((8, LANES), f32),
        vmem((8, LANES), f32),
        vmem((NCH, spots, width), bf16),
        vmem((NCH, spots, width), bf16),
        vmem((n_cells, LANES), f32),
        vmem((NCH, 2, 24, LANES), f32),
        vmem((NCH, 24, LANES), f32),
        vmem((NCH, 4, 24, LANES), f32),
        vmem((NCH, 4, 24, LANES), f32),
        vmem((NCH, 2, 24, LANES), f32),
        vmem((3, 8, LANES), f32),
        vmem((3, 8, LANES), f32),
        vmem((3, 4, 8, LANES), f32),
        vmem((3, 4, 8, LANES), f32),
        vmem((NCH, 2) + ring, f32),
        vmem((NCH, 2, 4, 2, 2, 16, LANES), f32),
        vmem((NCH, 2, 4, 2, 2, 16, LANES), f32),
        vmem((NCH, 2, 4, 2, 16, LANES), f32),
        vmem((NCH, 2, 4, 2, 16, LANES), f32),
        vmem((NCH, 2, 4, 16, LANES), f32),
        vmem((NCH, 2, 4, 16, LANES), f32),
        vmem((NCH, 3, 2, 16, LANES), f32),
        dma((1,)), dma((NCH,)), dma((tiles,)),
        dma((NCH, 3)), dma((NCH, 3)), dma((NCH, 2)), dma((NCH, 2)), dma((NCH, 2)), dma((NCH, 2)), dma((NCH,)), dma((NCH,)),
        dma((NCH,)), dma((NCH,)), dma((NCH, 3)), dma((NCH, 3)), dma((NCH, 3)), dma((NCH, 3)), dma((NCH,)), dma((NCH,)),
        dma((3,)), dma((3,)), dma((3, 3)), dma((3, 3)), dma((3, 3)), dma((3, 3)),
        dma((NCH,)), dma((NCH,)), dma((NCH, 2)), dma((NCH, 2)), dma((NCH, 2)), dma((NCH, 2)), dma((NCH, 3)), dma((NCH, 3)),
    ]
    mask = cell_mask.reshape(n_cells // LANES, LANES)
    held = (
        vmem((NCH, spots // BR, BR, width), f32),
        vmem((tiles, n_cells, LANES), f32),
        vmem((8, LANES), f32),
        vmem((8, LANES), f32),
        vmem((8, LANES), f32),
        vmem((n_slides, genes), f32),
        vmem((tiles, LANES), f32),
        vmem((1, own), f32),
        vmem((own, genes), f32),
    )
    between = pl.pallas_call(
        fused_kernel,
        out_shape=held,
        in_specs=[anywhere, scalars, anywhere, inside, inside, inside, anywhere, inside],
        out_specs=(inside,) * len(held),
        scratch_shapes=scratch,
        compiler_params=pltpu.CompilerParams(
            collective_id=0, has_side_effects=True, vmem_limit_bytes=50 << 20
        ),
    )(
        logits, filt, cells, mask, gene_mask,
        slide_ids.reshape(tiles, LANES), target.reshape(spots // BR, BR, genes), density.reshape(tiles, LANES),
    )
    out = pl.pallas_call(
        finish_kernel,
        out_shape=(
            jax.ShapeDtypeStruct((3,), f32),
            jax.ShapeDtypeStruct((4,), f32),
            jax.ShapeDtypeStruct((spots // BR, BR, genes), f32),
            jax.ShapeDtypeStruct((n_slides, genes), f32),
            jax.ShapeDtypeStruct((tiles, LANES), f32),
            jax.ShapeDtypeStruct((n_cells, spots), f32),
            jax.ShapeDtypeStruct((1, own), f32),
            jax.ShapeDtypeStruct((own, genes), f32),
        ),
        in_specs=[inside] * (len(held) + 1),
        out_specs=(anywhere,) * 8,
        scratch_shapes=[pltpu.SMEM((3,), f32), pltpu.SMEM((4,), f32), dma((NCH,)), dma((tiles,)), dma((6,))],
        compiler_params=pltpu.CompilerParams(vmem_limit_bytes=24 << 20),
    )(*between, mask)
    terms, reg, pred, gcos, scos, glog, gfilt, gcell = out
    return terms, reg, pred.reshape(spots, genes), gcos, scos.reshape(spots), glog, gfilt.reshape(own), gcell


def per_slide(onehot, values):
    return lax.dot_general(
        onehot, values, (((0,), (0,)), ((), ())), precision=lax.Precision.HIGHEST
    )


def on_device(logits, filt, cells, cell_mask, gene_mask, slide_ids, target, density):
    high = lax.Precision.HIGHEST
    n_cells = logits.shape[0]
    own_rows = cells.shape[0]
    n_slides = gene_mask.shape[0]
    valid = cell_mask.astype(jnp.float32)
    top = jnp.max(logits, axis=0, keepdims=True)
    expo = jnp.exp(logits - top) * valid[:, None]
    total = jnp.sum(expo, axis=0, keepdims=True)
    prob = expo / total
    logp = jnp.where(valid[:, None] > 0, logits - top - jnp.log(total), 0.0)
    entropy_part = -jnp.sum(prob * logp)
    whole, filt_all = (
        lax.all_gather(cells, ("wide", "narrow"), axis=0, tiled=True),
        lax.all_gather(filt, ("wide", "narrow"), axis=0, tiled=True),
    )
    keep = jax.nn.sigmoid(filt_all)
    weighted = prob * keep[:, None]
    g_pred = lax.dot_general(weighted, whole, (((0,), (0,)), ((), ())), precision=high)
    onehot = (slide_ids[:, None] == jnp.arange(n_slides, dtype=jnp.int32)[None, :]).astype(
        jnp.float32
    )
    gmask = gene_mask.astype(jnp.float32)
    spot_mask = jnp.dot(onehot, gmask, precision=high)
    masked_pred = spot_mask * g_pred
    sdot = jnp.sum(masked_pred * target, axis=1)
    spp = jnp.sum(masked_pred * g_pred, axis=1)
    stt = jnp.sum(spot_mask * target * target, axis=1)
    spot_scale = lax.rsqrt(spp + eps) * lax.rsqrt(stt + eps)
    spot_cos = sdot * spot_scale
    mass = jnp.sum(weighted, axis=0)
    log_part = density * (jnp.log(density) - jnp.log(mass))
    slide_vec = jnp.stack([mass, density, log_part], axis=1)
    loss_parts = jnp.stack([-jnp.sum(spot_cos), entropy_part])
    dot_s, pp_s, tt_s, slide_tot, loss_tot = lax.psum(
        (
            per_slide(onehot, g_pred * target),
            per_slide(onehot, g_pred * g_pred),
            per_slide(onehot, target * target),
            per_slide(onehot, slide_vec),
            loss_parts,
        ),
        ("wide", "narrow"),
    )
    mass_s = slide_tot[:, 0]
    wsum_s = slide_tot[:, 1]
    logsum_s = slide_tot[:, 2]
    gene_scale = gmask * lax.rsqrt(pp_s + eps) * lax.rsqrt(tt_s + eps)
    gene_cos = dot_s * gene_scale
    gene_loss = -jnp.sum(gene_cos)
    spot_loss = loss_tot[0]
    entropy = loss_tot[1] / (prob.shape[1] * lax.axis_size(("wide", "narrow")))
    kl_term = jnp.sum(logsum_s / wsum_s) + jnp.sum(jnp.log(mass_s) - jnp.log(wsum_s))
    count = jnp.sum(valid * keep)
    target_count = n_cells // 4
    count_term = jnp.abs(count - target_count) / n_cells
    binarity = jnp.sum(valid * (keep - keep * keep)) / n_cells
    loss = gene_loss + spot_loss + kl_term + count_term + binarity
    terms = jnp.stack([loss, gene_loss, spot_loss])
    reg_terms = jnp.stack([kl_term, count_term, binarity, entropy])
    gene_shrink = gene_scale * dot_s / (pp_s + eps)
    grad_pred = -jnp.dot(onehot, gene_scale, precision=high) * target
    grad_pred = grad_pred + jnp.dot(onehot, gene_shrink, precision=high) * g_pred
    spot_shrink = sdot / (spp + eps)
    grad_pred = grad_pred - spot_mask * spot_scale[:, None] * (
        target - spot_shrink[:, None] * g_pred
    )
    spot_slide = jnp.dot(onehot, jnp.stack([mass_s, wsum_s], axis=1), precision=high)
    grad_mass = -(density / spot_slide[:, 1]) / mass + 1.0 / spot_slide[:, 0]
    grad_weighted = lax.dot_general(whole, grad_pred, (((1,), (1,)), ((), ())), precision=high)
    grad_weighted = grad_weighted + grad_mass[None, :]
    grad_prob = keep[:, None] * grad_weighted
    keep_part = jnp.sum(prob * grad_weighted, axis=1)
    grad_logits = prob * (grad_prob - jnp.sum(prob * grad_prob, axis=0, keepdims=True))
    cell_part = jnp.dot(weighted, grad_pred, precision=high)
    grad_cells, keep_sum = (
        lax.psum_scatter(cell_part, ("wide", "narrow"), scatter_dimension=0, tiled=True),
        lax.psum_scatter(keep_part, ("wide", "narrow"), scatter_dimension=0, tiled=True),
    )
    first_row = lax.axis_index(("wide", "narrow")) * own_rows
    own_keep = lax.dynamic_slice_in_dim(keep, first_row, own_rows, 0)
    own_valid = lax.dynamic_slice_in_dim(valid, first_row, own_rows, 0)
    keep_grad = (
        keep_sum + own_valid * (jnp.sign(count - target_count) + 1.0 - 2.0 * own_keep) / n_cells
    )
    grad_filter = keep_grad * own_keep * (1.0 - own_keep)
    return (terms, reg_terms, g_pred, gene_cos, spot_cos, grad_logits, grad_filter, grad_cells)


def fits_fused(mesh, logits, cells, gene_mask, slide_ids):
    n_cells, spots = logits.shape
    return (
        (mesh.shape["wide"], mesh.shape["narrow"]) == (8, 4)
        and cells.shape == (16, 2048)
        and n_cells == 512
        and spots == 1024
        and gene_mask.shape[0] == 8
    )


def solution(mesh):
    def step(logits, filt, cells, cell_mask, gene_mask, slide_ids, target, density):
        fits = fits_fused(mesh, logits, cells, gene_mask, slide_ids)
        run = fused if fits else on_device
        return run(logits, filt, cells, cell_mask, gene_mask, slide_ids, target, density)

    placed = (
        P(None, ("wide", "narrow")),
        P(("wide", "narrow")),
        P(("wide", "narrow"), None),
        P(),
        P(),
        P(("wide", "narrow")),
        P(("wide", "narrow"), None),
        P(("wide", "narrow")),
    )
    return jax.shard_map(
        step,
        mesh=mesh,
        in_specs=placed,
        out_specs=(
            P(),
            P(),
            P(("wide", "narrow"), None),
            P(),
            P(("wide", "narrow")),
            P(None, ("wide", "narrow")),
            P(("wide", "narrow")),
            P(("wide", "narrow"), None),
        ),
        check_vma=False,
    )
```

```python
import jax
import jax.numpy as jnp
from jax import lax
from jax.experimental import pallas as pl
from jax.experimental.pallas import tpu as pltpu
from jax.sharding import PartitionSpec as P

eps = 1e-06
MESH = pl.DeviceIdType.MESH
bf16 = jnp.bfloat16
f32 = jnp.float32
LANES = 128
NCH = 8
BR = 32
GR = 256
AHEAD = 3


def split(value):
    high = value.astype(bf16)
    return high, (value - high.astype(f32)).astype(bf16)


def mm(a, b):
    return lax.dot_general(a, b, (((1,), (0,)), ((), ())), preferred_element_type=f32)


def mm_nt(a, b):
    return lax.dot_general(a, b, (((1,), (1,)), ((), ())), preferred_element_type=f32)


def fused_kernel(
    logits_hbm, filt_ref, cells_hbm, mask_ref, gene_ref, ids_ref, target_hbm, dens_ref,
    pv, gw, keep_ref, sums_ref, loss_ref, gcos_ref, scos_ref, gfilt_ref, gcell_ref,
    lg, tv, buf, chi, clo, ownc, ownk, along, valid, keepc, whi, wlo, thi, tlo, gmb, oh, l1, l2, cf,
    idc, blocks, sd, sp, st, mass, gmass, gph, gpl, kp,
    stat, a1, a2, a3, fin, kvec, k1, k2, k3,
    part, rb, sb, r1, tt_, r2, qq, r3,
    lsem, tsem, osem,
    zs, zr, xs, xr, ys, yr, bs, br,
    as1, ar1, as2, ar2, as3, ar3, as4, ar4,
    ks1, kr1, ks2, kr2, ks3, kr3,
    cbs, cbr, cxs, cxr, cys, cyr, czs, czr,
):
    n_cells = chi.shape[1]
    width = chi.shape[2]
    last = NCH - 1
    n_blocks = tv.shape[1]
    spots = n_blocks * BR
    n_slides = gene_ref.shape[0]
    tiles = spots // LANES
    wide, narrow = lax.axis_index("wide"), lax.axis_index("narrow")
    z, y = lax.div(wide, 2), lax.rem(wide, 2)
    x, core = lax.div(narrow, 2), lax.rem(narrow, 2)
    to_z = [(lax.rem(z + k, 4) * 2 + y, narrow) for k in (1, 2, 3)]
    from_z = [lax.rem(z + 4 - k, 4) for k in (1, 2, 3)]
    to_x = (wide, (1 - x) * 2 + core)
    to_y = (z * 2 + 1 - y, narrow)
    to_xy = (z * 2 + 1 - y, (1 - x) * 2 + core)
    to_b = (wide, x * 2 + 1 - core)

    def rcopy(src, dst, ss, rs, dev):
        return pltpu.make_async_remote_copy(
            src_ref=src, dst_ref=dst, send_sem=ss, recv_sem=rs, device_id=dev, device_id_type=MESH
        )

    def lanes(i, w=LANES):
        return pl.ds(pl.multiple_of(i * w, w), w)

    own_cells = pltpu.make_async_copy(cells_hbm, ownc, lsem.at[0])

    def get_logits(i):
        return pltpu.make_async_copy(logits_hbm.at[:, lanes(i)], lg.at[i], osem.at[i])

    def get_target(c):
        return pltpu.make_async_copy(target_hbm.at[:, :, lanes(c, width)], tv.at[c], tsem.at[c])

    own_cells.start()
    for i in range(tiles):
        get_logits(i).start()
    for c in range(NCH):
        get_target(c).start()

    barrier = pltpu.get_barrier_semaphore()
    for dev in to_z + [to_x, to_y, to_xy, to_b]:
        pl.semaphore_signal(barrier, inc=1, device_id=dev, device_id_type=MESH)

    iota8 = lax.broadcasted_iota(jnp.int32, (8, LANES), 0)
    lane8 = lax.broadcasted_iota(jnp.int32, (8, LANES), 1)
    row16 = lax.broadcasted_iota(jnp.int32, (16, LANES), 0)
    dev = wide * 4 + narrow
    place = lane8 + iota8 * LANES - dev * 16
    mine = jnp.zeros((16, LANES), f32)
    vector = jnp.zeros((8, LANES), f32)
    for r in range(16):
        mine = jnp.where(row16 == r, filt_ref[r], mine)
        vector = jnp.where(place == r, filt_ref[r], vector)
    kvec[2] = vector
    own_keep = jax.nn.sigmoid(mine)
    ownk[...] = own_keep
    along[...] = jnp.zeros_like(along)
    own_cells.wait()
    for c in range(NCH):
        for h in range(2):
            buf[c, h, z, y, x, core] = own_keep * ownc[:, (c * 2 + h) * LANES : (c * 2 + h + 1) * LANES]
    for q in range(n_cells // LANES):
        line = mask_ref[q : q + 1, :].astype(f32)
        valid[q * LANES : (q + 1) * LANES, :] = jnp.broadcast_to(line, (LANES, LANES)).T
    pl.semaphore_wait(barrier, 7)

    def z_out(c, k):
        r = buf.at[c, :, z, y, x, core]
        return rcopy(r, r, zs.at[c, k], zr.at[c, k], to_z[k])

    def z_in(c, k):
        r = buf.at[c, :, from_z[k], y, x, core]
        return rcopy(r, r, zs.at[c, k], zr.at[c, k], to_z[k])

    def s1_out(c):
        a = buf.at[c, 0, :, y, x, core]
        b = buf.at[c, 1, :, y, x, core]
        return [rcopy(a, a, xs.at[c, 0], xr.at[c, 0], to_x), rcopy(b, b, ys.at[c, 0], yr.at[c, 0], to_y)]

    def s1_in(c):
        a = buf.at[c, 0, :, y, 1 - x, core]
        b = buf.at[c, 1, :, 1 - y, x, core]
        return [rcopy(a, a, xs.at[c, 0], xr.at[c, 0], to_x), rcopy(b, b, ys.at[c, 0], yr.at[c, 0], to_y)]

    def s2_out(c):
        a = buf.at[c, 0, :, y, :, core]
        b = buf.at[c, 1, :, :, x, core]
        return [rcopy(a, a, ys.at[c, 1], yr.at[c, 1], to_y), rcopy(b, b, xs.at[c, 1], xr.at[c, 1], to_x)]

    def s2_in(c):
        a = buf.at[c, 0, :, 1 - y, :, core]
        b = buf.at[c, 1, :, :, 1 - x, core]
        return [rcopy(a, a, ys.at[c, 1], yr.at[c, 1], to_y), rcopy(b, b, xs.at[c, 1], xr.at[c, 1], to_x)]

    def s3_out(c):
        r = buf.at[c, :, :, :, :, core]
        return rcopy(r, r, bs.at[c], br.at[c], to_b)

    def s3_in(c):
        r = buf.at[c, :, :, :, :, 1 - core]
        return rcopy(r, r, bs.at[c], br.at[c], to_b)

    def b1(c):
        return rcopy(stat.at[c, 1 - core], a1.at[c], as1.at[c], ar1.at[c], to_b)

    plane = [to_x, to_y, to_xy]
    here = y * 2 + x
    there = [y * 2 + 1 - x, (1 - y) * 2 + x, (1 - y) * 2 + 1 - x]

    def b2_out(c, k):
        r = a2.at[c, here]
        return rcopy(r, r, as2.at[c, k], ar2.at[c, k], plane[k])

    def b2_in(c, k):
        r = a2.at[c, there[k]]
        return rcopy(r, r, as2.at[c, k], ar2.at[c, k], plane[k])

    def b3_out(c, k):
        r = a3.at[c, z]
        return rcopy(r, r, as3.at[c, k], ar3.at[c, k], to_z[k])

    def b3_in(c, k):
        r = a3.at[c, from_z[k]]
        return rcopy(r, r, as3.at[c, k], ar3.at[c, k], to_z[k])

    def b4(c, half):
        r = fin.at[c, half]
        return rcopy(r, r, as4.at[c], ar4.at[c], to_b)

    def sum_second(c):
        b1(c).wait_recv()
        a2[c, here] = stat[c, core] + a1[c]
        for k in range(3):
            b2_out(c, k).start()

    def sum_third(c):
        for k in range(3):
            b2_in(c, k).wait_recv()
        a3[c, z] = (a2[c, 0] + a2[c, 1]) + (a2[c, 2] + a2[c, 3])
        for k in range(3):
            b3_out(c, k).start()

    def sum_fourth(c):
        for k in range(3):
            b3_in(c, k).wait_recv()
        fin[c, core] = (a3[c, 0] + a3[c, 1]) + (a3[c, 2] + a3[c, 3])
        b4(c, core).start()

    def sum_last(c):
        b4(c, 1 - core).wait_recv()

    def v1(n):
        return rcopy(kvec.at[n], k1.at[n], ks1.at[n], kr1.at[n], to_b)

    def v2(n, slot, k):
        return rcopy(k2.at[n, slot], k2.at[n, slot], ks2.at[n, k], kr2.at[n, k], plane[k])

    def v3(n, slot, k):
        return rcopy(k3.at[n, slot], k3.at[n, slot], ks3.at[n, k], kr3.at[n, k], to_z[k])

    def vector_second(n):
        v1(n).wait_recv()
        k2[n, here] = kvec[n] + k1[n]
        for k in range(3):
            v2(n, here, k).start()

    def vector_third(n):
        for k in range(3):
            v2(n, there[k], k).wait_recv()
        k3[n, z] = (k2[n, 0] + k2[n, 1]) + (k2[n, 2] + k2[n, 3])
        for k in range(3):
            v3(n, z, k).start()

    def vector_last(n):
        for k in range(3):
            v3(n, from_z[k], k).wait_recv()
        return (k3[n, 0] + k3[n, 1]) + (k3[n, 2] + k3[n, 3])

    def softmax(i, ent):
        get_logits(i).wait()
        value = lg[i]
        top = jnp.max(value, axis=0, keepdims=True)
        expo = jnp.exp(value - top) * valid[...]
        total = jnp.sum(expo, axis=0, keepdims=True)
        prob = expo * (1.0 / total)
        lg[i] = prob
        high, low = split(prob)
        whi[:, lanes(i)] = high
        wlo[:, lanes(i)] = low
        high, low = split(prob.T)
        thi[lanes(i), :] = high
        tlo[lanes(i), :] = low
        return ent + jnp.sum(prob * (value - top - jnp.log(total)), axis=0, keepdims=True)

    def one_hot(i, _):
        ids = ids_ref[pl.ds(i, 1), :]
        square = (lax.broadcasted_iota(jnp.int32, (LANES, LANES), 0) == ids).astype(f32)
        oh[lanes(i), :] = square.T.astype(bf16)
        per = LANES // BR
        turned = jnp.broadcast_to(ids, (LANES, LANES)).astype(f32).T
        idc[pl.ds(i * per, per)] = turned.reshape(per, BR, LANES)
        return 0

    def leave_z(c):
        for k in range(3):
            z_out(c, k).start()

    for c in range(AHEAD):
        leave_z(c)
    v1(2).start()

    def stage_z(c):
        for k in range(3):
            z_in(c, k).wait_recv()
        for d in s1_out(c):
            d.start()

    def stage_1(c):
        for d in s1_in(c):
            d.wait_recv()
        for d in s2_out(c):
            d.start()

    def stage_2(c):
        for d in s2_in(c):
            d.wait_recv()
        s3_out(c).start()

    def fold(v):
        out = v[:, :LANES]
        for k in range(1, v.shape[1] // LANES):
            out = out + v[:, k * LANES : (k + 1) * LANES]
        return out

    def eighths(v):
        return jnp.sum(v.reshape(v.shape[0] // 8, 8, v.shape[1]), axis=0)

    for c in range(NCH):
        gm = jnp.concatenate(
            [gene_ref[:, c * width : (c + 1) * width].astype(f32), jnp.zeros((LANES - n_slides, width), f32)], axis=0
        )
        gmb[c] = gm.astype(bf16)
    sd[...] = jnp.zeros_like(sd)
    sp[...] = jnp.zeros_like(sp)
    st[...] = jnp.zeros_like(st)
    lax.fori_loop(0, tiles, one_hot, 0)

    begins = [jnp.sum((ids_ref[...] < k).astype(jnp.int32)) for k in range(n_slides + 1)]
    firsts = [jnp.minimum(lax.div(begins[k], BR), n_blocks - 1) for k in range(n_slides)]
    lasts = [lax.div(jnp.maximum(begins[k + 1] - 1, 0), BR) for k in range(n_slides)]
    slide16 = lax.broadcasted_iota(jnp.int32, (16, 8 * n_blocks), 0)
    block16 = lax.div(lax.broadcasted_iota(jnp.int32, (16, 8 * n_blocks), 1), 8)
    inner = jnp.zeros((16, 8 * n_blocks), f32)
    for k in range(n_slides):
        full = jnp.logical_and(block16 > firsts[k], block16 < lasts[k])
        inner = jnp.where(jnp.logical_and(slide16 == k, full), 1.0, inner)
    inner = inner.astype(bf16)
    inner = jnp.concatenate([inner, inner], axis=1)
    slide8 = lax.broadcasted_iota(jnp.int32, (8, width), 0)

    def gene_sums(c, products, number, at_row):
        sums = []
        for n in range(number):
            bh, bl = split(blocks[n])
            sums.append(mm(inner, jnp.concatenate([bh, bl], axis=0))[:8, :])
        for k in range(n_slides):
            parts = [jnp.zeros((8, width), f32)] * number
            for block, counts in ((firsts[k], None), (lasts[k], lasts[k] != firsts[k])):
                own = idc[block] == float(k)
                if counts is not None:
                    own = jnp.logical_and(own, counts)
                own = own.astype(f32)
                own = jnp.concatenate([own] * (width // LANES), axis=1)
                for n, prod in enumerate(products(c, block)):
                    parts[n] = parts[n] + eighths(prod * own)
            for n in range(number):
                line = jnp.sum(parts[n], axis=0, keepdims=True)
                sums[n] = sums[n] + jnp.where(slide8 == k, line, 0.0)
        for n in range(number):
            for h in range(2):
                stat[c, h, at_row + n * 8 : at_row + (n + 1) * 8, :] = sums[n][:, h * LANES : (h + 1) * LANES]

    def of_target(c, r):
        tgt = tv[c, r]
        return (tgt * tgt,)

    def of_both(c, r):
        pred, tgt = pv[c, r], tv[c, r]
        return pred * tgt, jnp.where(tgt > 0.0, pred * pred, 0.0)

    def by_rows(c, products, spots_of):
        for r in range(n_blocks):
            at = slice(r * BR, (r + 1) * BR)
            for n, (prod, spot) in enumerate(zip(products(c, r), spots_of)):
                spot[at, :] += fold(prod)
                blocks[n, r * 8 : (r + 1) * 8, :] = eighths(prod)

    def target_sums(c, _):
        per = GR // BR
        for n in range(spots // GR):
            sees = mm(oh[n * GR : (n + 1) * GR, :], gmb[c]).reshape(per, BR, width)
            for r in range(per):
                tv[c, n * per + r] = sees[r] * tv[c, n * per + r]
        by_rows(c, of_target, (st,))
        gene_sums(c, of_target, 1, 16)
        return 0

    def predict(c):
        s3_in(c).wait_recv()
        whole = jnp.concatenate([buf[c, h].reshape(n_cells, LANES) for h in range(2)], axis=1)
        high, low = split(whole)
        chi[c] = high
        clo[c] = low
        wh, wl = thi[...], tlo[...]
        pred = mm(jnp.concatenate([wh, wl, wh], axis=1), jnp.concatenate([high, high, low], axis=0))
        pv[c] = pred.reshape(n_blocks, BR, width)

    def predicted_sums(c):
        by_rows(c, of_both, (sd, sp))
        gene_sums(c, of_both, 2, 0)

    def slide_sums():
        keep_rows = jax.nn.sigmoid(vector_last(2))
        keep_ref[...] = keep_rows
        for q in range(quarter):
            line = jnp.broadcast_to(keep_rows[q : q + 1, :], (LANES, LANES))
            keepc[q * LANES : (q + 1) * LANES, :] = line.T

        def by_tile(i, sums):
            at = pl.ds(i, 1)
            line = jnp.sum(lg[i] * keepc[...], axis=0, keepdims=True)
            mass[at, :] = line
            dens = dens_ref[at, :]
            mine = (iota8 == ids_ref[at, :]).astype(f32)
            terms = (line, dens, dens * (jnp.log(dens) - jnp.log(line)))
            return tuple(a + mine * b for a, b in zip(sums, terms))

        blank = jnp.zeros((8, LANES), f32)
        totals = lax.fori_loop(0, tiles, by_tile, (blank, blank, blank))
        for k, value in enumerate(totals):
            blank = jnp.where(lane8 == k, jnp.sum(value, axis=1, keepdims=True), blank)
        kvec[0] = blank
        v1(0).start()

    quarter = n_cells // LANES
    ent = lax.fori_loop(0, tiles // 2, softmax, jnp.zeros((1, LANES), f32))
    stage_z(0)
    leave_z(AHEAD)
    vector_second(2)
    ent = lax.fori_loop(tiles // 2, tiles, softmax, ent)
    stage_z(1)
    leave_z(AHEAD + 1)
    for c in range(NCH):
        get_target(c).wait()
    lax.fori_loop(0, 3, target_sums, 0)
    stage_z(2)
    leave_z(AHEAD + 2)
    stage_1(0)
    vector_third(2)
    lax.fori_loop(3, 6, target_sums, 0)
    stage_z(3)
    leave_z(AHEAD + 3)
    stage_1(1)
    lax.fori_loop(6, NCH, target_sums, 0)
    stage_z(4)
    leave_z(AHEAD + 4)
    stage_1(2)
    slide_sums()
    stage_z(5)
    stage_2(0)
    stage_1(3)

    def gather_tick(t, _):
        c = t - 6
        pl.when(t < NCH)(lambda: stage_z(t))
        pl.when(t + AHEAD < NCH)(lambda: leave_z(t + AHEAD))
        pl.when(t - 5 < NCH)(lambda: stage_2(t - 5))
        predict(c)
        predicted_sums(c)
        b1(c).start()
        pl.when(t - 2 < NCH)(lambda: stage_1(t - 2))
        pl.when(c == 0)(lambda: vector_second(0))
        pl.when(c == 2)(lambda: vector_third(0))
        pl.when(c >= 1)(lambda: sum_second(c - 1))
        pl.when(c >= 3)(lambda: sum_third(c - 3))
        pl.when(c >= 6)(lambda: sum_fourth(c - 6))
        return 0

    lax.fori_loop(6, NCH + 6, gather_tick, 0)

    lane128 = lax.broadcasted_iota(jnp.int32, (LANES, LANES), 1)
    slide_of_lane = lax.rem(lane128, 8).astype(f32)

    def spot_rows(i, _):
        at = lanes(i)
        sdot, spp, stt = [jnp.sum(ref[at, :], axis=1, keepdims=True) for ref in (sd, sp, st)]
        scale = lax.rsqrt(spp + eps) * lax.rsqrt(stt + eps)
        sd[at, :] = jnp.broadcast_to(sdot * scale, (LANES, LANES))
        per = LANES // BR
        own = jnp.logical_and(idc[pl.ds(i * per, per)].reshape(LANES, LANES) == slide_of_lane, lane128 < 32)
        for ref, value in ((l1, scale), (l2, scale * (sdot / (spp + eps)))):
            high, low = split(value)
            value = jnp.where(lane128 < 16, 1.0, jnp.where(lane128 < 24, high.astype(f32), low.astype(f32)))
            ref[at, :] = jnp.where(own, value, 0.0).astype(bf16)
        return 0

    lax.fori_loop(0, tiles, spot_rows, 0)
    sum_second(last)
    sum_third(last - 2)
    sum_fourth(last - 5)

    def scatter_sib(c):
        return rcopy(part.at[c, :, :, :, :, 1 - core], rb.at[c], cbs.at[c], cbr.at[c], to_b)

    def scatter_one(c):
        return [
            rcopy(sb.at[c, 0, :, 1 - y], r1.at[c, 0], cys.at[c, 0], cyr.at[c, 0], to_y),
            rcopy(sb.at[c, 1, :, :, 1 - x], r1.at[c, 1], cxs.at[c, 0], cxr.at[c, 0], to_x),
        ]

    def scatter_two(c):
        return [
            rcopy(tt_.at[c, 0, :, 1 - x], r2.at[c, 0], cxs.at[c, 1], cxr.at[c, 1], to_x),
            rcopy(tt_.at[c, 1, :, 1 - y], r2.at[c, 1], cys.at[c, 1], cyr.at[c, 1], to_y),
        ]

    def scatter_z(c, k):
        return rcopy(qq.at[c, :, lax.rem(z + k + 1, 4)], r3.at[c, k], czs.at[c, k], czr.at[c, k], to_z[k])

    def sc1(c):
        scatter_sib(c).wait_recv()
        sb[c] = part[c, :, :, :, :, core] + rb[c]
        for d in scatter_one(c):
            d.start()

    def sc2(c):
        for d in scatter_one(c):
            d.wait_recv()
        tt_[c, 0] = sb[c, 0, :, y] + r1[c, 0]
        tt_[c, 1] = sb[c, 1, :, :, x] + r1[c, 1]
        for d in scatter_two(c):
            d.start()

    def sc3(c):
        for d in scatter_two(c):
            d.wait_recv()
        qq[c, 0] = tt_[c, 0, :, x] + r2[c, 0]
        qq[c, 1] = tt_[c, 1, :, y] + r2[c, 1]
        for k in range(3):
            scatter_z(c, k).start()

    def sc4(c):
        for k in range(3):
            scatter_z(c, k).wait_recv()
        for h in range(2):
            at = lanes(c * 2 + h)
            total = (qq[c, h, z] + r3[c, 0, h]) + (r3[c, 1, h] + r3[c, 2, h])
            gcell_ref[:, at] = total * ownk[...]
            along[...] += total * ownc[:, at]

    def gene_coefs(c):
        total = jnp.concatenate([fin[c, 0], fin[c, 1]], axis=1)
        dot_s, pp_s, tt_s = total[0:8], total[8:16], total[16:24]
        gm = gene_ref[:, lanes(c, width)].astype(f32)
        gscale = gm * lax.rsqrt(pp_s + eps) * lax.rsqrt(tt_s + eps)
        gcos_ref[:, lanes(c, width)] = dot_s * gscale
        gshrink = gscale * (dot_s / (pp_s + eps))
        pad = jnp.zeros((LANES - 32, width), f32)
        for n, value in enumerate((gscale, gshrink)):
            high, low = split(value)
            high, low = high.astype(f32), low.astype(f32)
            cf[lax.rem(c, 2), n] = jnp.concatenate([high, low, gm, gm, pad], axis=0).astype(bf16)

    def backward(c):
        slot = lax.rem(c, 2)
        per = GR // BR
        for n in range(spots // GR):
            at = slice(n * GR, (n + 1) * GR)
            own = slice(n * per, (n + 1) * per)
            pred, tgt = pv[c, own].reshape(GR, width), tv[c, own].reshape(GR, width)
            gh, gl = split(mm(l2[at, :], cf[slot, 1]) * pred - mm(l1[at, :], cf[slot, 0]) * tgt)
            gph[c, at, :] = gh
            gpl[c, at, :] = gl
        wh, wl = whi[...], wlo[...]
        gh, gl = gph[c], gpl[c]
        out = mm(jnp.concatenate([wh, wl, wh], axis=1), jnp.concatenate([gh, gh, gl], axis=0))
        for h in range(2):
            part[c, h] = out[:, h * LANES : (h + 1) * LANES].reshape(4, 2, 2, 2, 16, LANES)
        gene_coefs(jnp.minimum(c + 1, last))
        scatter_sib(c).start()

    def spot_part(n):
        at = pl.ds(n * GR, GR)
        left = [chi[c] for c in range(NCH)]
        left = left + [clo[c] for c in range(NCH)] + left
        right = [gph[c, at, :] for c in range(NCH)]
        right = right + right + [gpl[c, at, :] for c in range(NCH)]
        out = mm_nt(jnp.concatenate(left, axis=1), jnp.concatenate(right, axis=1))
        for h in range(GR // LANES):
            i = n * (GR // LANES) + h
            grad = out[:, h * LANES : (h + 1) * LANES] + keepc[...] * gmass[i : i + 1, :]
            prob = lg[i]
            gw[i] = prob * (grad - jnp.sum(prob * grad, axis=0, keepdims=True))

    def back_tick(t, _):
        pl.when(t < last)(lambda: sum_last(t + 1))
        backward(t)
        pl.when(t >= 1)(lambda: sc1(t - 1))
        pl.when(t >= 3)(lambda: sc2(t - 3))
        pl.when(t >= 5)(lambda: sc3(t - 5))
        pl.when(t <= 1)(lambda: sum_third(last - 1 + t))
        pl.when(t <= 4)(lambda: sum_fourth(last - 4 + t))

        @pl.when(t == 4)
        def _():
            slide_totals()

        @pl.when(t == 5)
        def _():
            vector_second(1)

        @pl.when(t == 7)
        def _():
            vector_third(1)

        return 0

    def slide_totals():
        sums_s = vector_last(0)
        sums_ref[...] = sums_s
        mass_s, wsum_s = sums_s[:, 0:1], sums_s[:, 1:2]
        kp[...] = jnp.zeros_like(kp)

        def by_mass(i, total):
            at = pl.ds(i, 1)
            mine = (iota8 == ids_ref[at, :]).astype(f32)
            mass_at = jnp.sum(mine * mass_s, axis=0, keepdims=True)
            wsum_at = jnp.sum(mine * wsum_s, axis=0, keepdims=True)
            line = -(dens_ref[at, :] / wsum_at) / mass[at, :] + 1.0 / mass_at
            gmass[at, :] = line
            kp[...] += lg[i] * line
            spot = sd[lanes(i), :].T[0:1, :]
            scos_ref[at, :] = spot
            return total + spot

        total = lax.fori_loop(0, tiles, by_mass, jnp.zeros((1, LANES), f32))
        rows_k = [jnp.sum(kp[q * LANES : (q + 1) * LANES, :].T, axis=0, keepdims=True) for q in range(quarter)]
        rows_k = rows_k + [-total, -ent, jnp.zeros((6 - quarter, LANES), f32)]
        kvec[1] = jnp.concatenate(rows_k, axis=0)
        v1(1).start()

    sum_last(0)
    gene_coefs(0)
    lax.fori_loop(0, NCH, back_tick, 0)
    sc1(7)
    sc2(5)
    sc3(3)
    spot_part(0)
    sc2(6)
    sc3(4)
    sc2(7)
    sc3(5)
    spot_part(1)
    sc3(6)
    sc3(7)
    sc4(0)
    sc4(1)
    sc4(2)
    sc4(3)
    sc4(4)
    spot_part(2)
    spot_part(3)

    keep = keep_ref[...]
    ok = jnp.concatenate([mask_ref[...].astype(f32), jnp.zeros((8 - quarter, LANES), f32)], axis=0)
    off = jnp.sum(ok * keep) - n_cells // 4
    sign = jnp.where(off > 0, 1.0, jnp.where(off < 0, -1.0, 0.0))
    totals = vector_last(1)
    loss_ref[...] = totals
    rest = totals + ok * (sign + 1.0 - 2.0 * keep) / n_cells

    def own_lanes(value):
        picked = jnp.sum(jnp.where(iota8 == lax.div(dev, 8), value, 0.0), axis=0, keepdims=True)
        return pltpu.roll(picked, lax.rem(LANES - lax.rem(dev, 8) * 16, LANES), 1)

    keep = own_lanes(keep)
    rest = own_lanes(rest)

    def leave(c, _):
        for k in range(3):
            z_out(c, k).wait_send()
            b2_out(c, k).wait_send()
            b3_out(c, k).wait_send()
        for d in s1_out(c) + s2_out(c) + scatter_one(c) + scatter_two(c):
            d.wait_send()
        s3_out(c).wait_send()
        b1(c).wait_send()
        b4(c, core).wait_send()
        scatter_sib(c).wait_send()
        return 0

    lax.fori_loop(0, NCH, leave, 0)
    for c in range(NCH - 3):
        for k in range(3):
            scatter_z(c, k).wait_send()
    for n in range(3):
        v1(n).wait_send()
        for k in range(3):
            v2(n, here, k).wait_send()
            v3(n, z, k).wait_send()
    for c in range(NCH - 3, NCH):
        sc4(c)
    genes_part = jnp.concatenate([along[...], jnp.zeros((LANES - 16, LANES), f32)], axis=0)
    genes_part = jnp.sum(genes_part.T, axis=0, keepdims=True)
    gfilt_ref[...] = ((genes_part + rest) * keep * (1.0 - keep))[:, : gfilt_ref.shape[1]]

    for c in range(NCH - 3, NCH):
        for k in range(3):
            scatter_z(c, k).wait_send()


def finish_kernel(
    pv, gw, keep_ref, sums_ref, loss_ref, gcos_in, scos_in, gfilt_in, gcell_in, mask_ref,
    terms_hbm, reg_hbm, pred_hbm, gcos_hbm, scos_hbm, glog_hbm, gfilt_hbm, gcell_hbm,
    terms_ref, reg_ref, psem, osem, rsem,
):
    width = pv.shape[3]
    tiles, n_cells = gw.shape[:2]
    quarter = n_cells // LANES

    def put_pred(c):
        return pltpu.make_async_copy(pv.at[c], pred_hbm.at[:, :, c * width : (c + 1) * width], psem.at[c])

    def put_glog(i):
        return pltpu.make_async_copy(gw.at[i], glog_hbm.at[:, i * LANES : (i + 1) * LANES], osem.at[i])

    for c in range(NCH):
        put_pred(c).start()
    for i in range(tiles):
        put_glog(i).start()
    pairs = [(gcos_in, gcos_hbm), (scos_in, scos_hbm), (gcell_in, gcell_hbm), (gfilt_in, gfilt_hbm)]
    rest = [pltpu.make_async_copy(a, b, rsem.at[k]) for k, (a, b) in enumerate(pairs)]
    for copy in rest:
        copy.start()

    sums_s = sums_ref[...]
    mass_s, wsum_s, logsum_s = sums_s[:, 0:1], sums_s[:, 1:2], sums_s[:, 2:3]
    keep = keep_ref[:quarter, :]
    ok = mask_ref[...].astype(f32)
    count = jnp.sum(ok * keep)
    count_term = jnp.abs(count - n_cells // 4) / n_cells
    binarity = jnp.sum(ok * (keep - keep * keep)) / n_cells
    gene_loss = -jnp.sum(gcos_in[...])
    spot_loss = jnp.sum(loss_ref[quarter : quarter + 1, :])
    entropy = jnp.sum(loss_ref[quarter + 1 : quarter + 2, :]) / (tiles * LANES * 32)
    kl = jnp.sum(logsum_s / wsum_s + jnp.log(mass_s) - jnp.log(wsum_s))
    terms_ref[0] = gene_loss + spot_loss + kl + count_term + binarity
    terms_ref[1] = gene_loss
    terms_ref[2] = spot_loss
    reg_ref[0] = kl
    reg_ref[1] = count_term
    reg_ref[2] = binarity
    reg_ref[3] = entropy
    for k, (a, b) in enumerate(((terms_ref, terms_hbm), (reg_ref, reg_hbm))):
        rest.append(pltpu.make_async_copy(a, b, rsem.at[len(pairs) + k]))
        rest[-1].start()
    for copy in rest:
        copy.wait()
    for i in range(tiles):
        put_glog(i).wait()
    for c in range(NCH):
        put_pred(c).wait()


def fused(logits, filt, cells, cell_mask, gene_mask, slide_ids, target, density):
    n_cells, spots = logits.shape
    own, genes = cells.shape
    n_slides = gene_mask.shape[0]
    width = genes // NCH
    tiles = spots // LANES
    dma = pltpu.SemaphoreType.DMA
    vmem, anywhere = pltpu.VMEM, pl.BlockSpec(memory_space=pl.ANY)
    inside = pl.BlockSpec(memory_space=pltpu.VMEM)
    scalars = pl.BlockSpec(memory_space=pltpu.SMEM)
    ring = (4, 2, 2, 2, 16, LANES)
    scratch = [
        vmem((tiles, n_cells, LANES), f32),
        vmem((NCH, spots // BR, BR, width), f32),
        vmem((NCH, 2) + ring, f32),
        vmem((NCH, n_cells, width), bf16),
        vmem((NCH, n_cells, width), bf16),
        vmem((own, genes), f32),
        vmem((own, LANES), f32),
        vmem((own, LANES), f32),
        vmem((n_cells, LANES), f32),
        vmem((n_cells, LANES), f32),
        vmem((n_cells, spots), bf16),
        vmem((n_cells, spots), bf16),
        vmem((spots, n_cells), bf16),
        vmem((spots, n_cells), bf16),
        vmem((NCH, LANES, width), bf16),
        vmem((spots, LANES), bf16),
        vmem((spots, LANES), bf16),
        vmem((spots, LANES), bf16),
        vmem((2, 2, LANES, width), bf16),
        vmem((spots // BR, BR, LANES), f32),
        vmem((2, spots * 8 // BR, width), f32),
        vmem((spots, LANES), f32),
        vmem((spots, LANES), f32),
        vmem((spots, LANES), f32),
        vmem((8, LANES), f32),
        vmem((8, LANES), f32),
        vmem((NCH, spots, width), bf16),
        vmem((NCH, spots, width), bf16),
        vmem((n_cells, LANES), f32),
        vmem((NCH, 2, 24, LANES), f32),
        vmem((NCH, 24, LANES), f32),
        vmem((NCH, 4, 24, LANES), f32),
        vmem((NCH, 4, 24, LANES), f32),
        vmem((NCH, 2, 24, LANES), f32),
        vmem((3, 8, LANES), f32),
        vmem((3, 8, LANES), f32),
        vmem((3, 4, 8, LANES), f32),
        vmem((3, 4, 8, LANES), f32),
        vmem((NCH, 2) + ring, f32),
        vmem((NCH, 2, 4, 2, 2, 16, LANES), f32),
        vmem((NCH, 2, 4, 2, 2, 16, LANES), f32),
        vmem((NCH, 2, 4, 2, 16, LANES), f32),
        vmem((NCH, 2, 4, 2, 16, LANES), f32),
        vmem((NCH, 2, 4, 16, LANES), f32),
        vmem((NCH, 2, 4, 16, LANES), f32),
        vmem((NCH, 3, 2, 16, LANES), f32),
        dma((1,)), dma((NCH,)), dma((tiles,)),
        dma((NCH, 3)), dma((NCH, 3)), dma((NCH, 2)), dma((NCH, 2)), dma((NCH, 2)), dma((NCH, 2)), dma((NCH,)), dma((NCH,)),
        dma((NCH,)), dma((NCH,)), dma((NCH, 3)), dma((NCH, 3)), dma((NCH, 3)), dma((NCH, 3)), dma((NCH,)), dma((NCH,)),
        dma((3,)), dma((3,)), dma((3, 3)), dma((3, 3)), dma((3, 3)), dma((3, 3)),
        dma((NCH,)), dma((NCH,)), dma((NCH, 2)), dma((NCH, 2)), dma((NCH, 2)), dma((NCH, 2)), dma((NCH, 3)), dma((NCH, 3)),
    ]
    mask = cell_mask.reshape(n_cells // LANES, LANES)
    held = (
        vmem((NCH, spots // BR, BR, width), f32),
        vmem((tiles, n_cells, LANES), f32),
        vmem((8, LANES), f32),
        vmem((8, LANES), f32),
        vmem((8, LANES), f32),
        vmem((n_slides, genes), f32),
        vmem((tiles, LANES), f32),
        vmem((1, own), f32),
        vmem((own, genes), f32),
    )
    between = pl.pallas_call(
        fused_kernel,
        out_shape=held,
        in_specs=[anywhere, scalars, anywhere, inside, inside, inside, anywhere, inside],
        out_specs=(inside,) * len(held),
        scratch_shapes=scratch,
        compiler_params=pltpu.CompilerParams(
            collective_id=0, has_side_effects=True, vmem_limit_bytes=50 << 20
        ),
    )(
        logits, filt, cells, mask, gene_mask,
        slide_ids.reshape(tiles, LANES), target.reshape(spots // BR, BR, genes), density.reshape(tiles, LANES),
    )
    out = pl.pallas_call(
        finish_kernel,
        out_shape=(
            jax.ShapeDtypeStruct((3,), f32),
            jax.ShapeDtypeStruct((4,), f32),
            jax.ShapeDtypeStruct((spots // BR, BR, genes), f32),
            jax.ShapeDtypeStruct((n_slides, genes), f32),
            jax.ShapeDtypeStruct((tiles, LANES), f32),
            jax.ShapeDtypeStruct((n_cells, spots), f32),
            jax.ShapeDtypeStruct((1, own), f32),
            jax.ShapeDtypeStruct((own, genes), f32),
        ),
        in_specs=[inside] * (len(held) + 1),
        out_specs=(anywhere,) * 8,
        scratch_shapes=[pltpu.SMEM((3,), f32), pltpu.SMEM((4,), f32), dma((NCH,)), dma((tiles,)), dma((6,))],
        compiler_params=pltpu.CompilerParams(vmem_limit_bytes=24 << 20),
    )(*between, mask)
    terms, reg, pred, gcos, scos, glog, gfilt, gcell = out
    return terms, reg, pred.reshape(spots, genes), gcos, scos.reshape(spots), glog, gfilt.reshape(own), gcell


def per_slide(onehot, values):
    return lax.dot_general(
        onehot, values, (((0,), (0,)), ((), ())), precision=lax.Precision.HIGHEST
    )


def on_device(logits, filt, cells, cell_mask, gene_mask, slide_ids, target, density):
    high = lax.Precision.HIGHEST
    n_cells = logits.shape[0]
    own_rows = cells.shape[0]
    n_slides = gene_mask.shape[0]
    valid = cell_mask.astype(jnp.float32)
    top = jnp.max(logits, axis=0, keepdims=True)
    expo = jnp.exp(logits - top) * valid[:, None]
    total = jnp.sum(expo, axis=0, keepdims=True)
    prob = expo / total
    logp = jnp.where(valid[:, None] > 0, logits - top - jnp.log(total), 0.0)
    entropy_part = -jnp.sum(prob * logp)
    whole, filt_all = (
        lax.all_gather(cells, ("wide", "narrow"), axis=0, tiled=True),
        lax.all_gather(filt, ("wide", "narrow"), axis=0, tiled=True),
    )
    keep = jax.nn.sigmoid(filt_all)
    weighted = prob * keep[:, None]
    g_pred = lax.dot_general(weighted, whole, (((0,), (0,)), ((), ())), precision=high)
    onehot = (slide_ids[:, None] == jnp.arange(n_slides, dtype=jnp.int32)[None, :]).astype(
        jnp.float32
    )
    gmask = gene_mask.astype(jnp.float32)
    spot_mask = jnp.dot(onehot, gmask, precision=high)
    masked_pred = spot_mask * g_pred
    sdot = jnp.sum(masked_pred * target, axis=1)
    spp = jnp.sum(masked_pred * g_pred, axis=1)
    stt = jnp.sum(spot_mask * target * target, axis=1)
    spot_scale = lax.rsqrt(spp + eps) * lax.rsqrt(stt + eps)
    spot_cos = sdot * spot_scale
    mass = jnp.sum(weighted, axis=0)
    log_part = density * (jnp.log(density) - jnp.log(mass))
    slide_vec = jnp.stack([mass, density, log_part], axis=1)
    loss_parts = jnp.stack([-jnp.sum(spot_cos), entropy_part])
    dot_s, pp_s, tt_s, slide_tot, loss_tot = lax.psum(
        (
            per_slide(onehot, g_pred * target),
            per_slide(onehot, g_pred * g_pred),
            per_slide(onehot, target * target),
            per_slide(onehot, slide_vec),
            loss_parts,
        ),
        ("wide", "narrow"),
    )
    mass_s = slide_tot[:, 0]
    wsum_s = slide_tot[:, 1]
    logsum_s = slide_tot[:, 2]
    gene_scale = gmask * lax.rsqrt(pp_s + eps) * lax.rsqrt(tt_s + eps)
    gene_cos = dot_s * gene_scale
    gene_loss = -jnp.sum(gene_cos)
    spot_loss = loss_tot[0]
    entropy = loss_tot[1] / (prob.shape[1] * lax.axis_size(("wide", "narrow")))
    kl_term = jnp.sum(logsum_s / wsum_s) + jnp.sum(jnp.log(mass_s) - jnp.log(wsum_s))
    count = jnp.sum(valid * keep)
    target_count = n_cells // 4
    count_term = jnp.abs(count - target_count) / n_cells
    binarity = jnp.sum(valid * (keep - keep * keep)) / n_cells
    loss = gene_loss + spot_loss + kl_term + count_term + binarity
    terms = jnp.stack([loss, gene_loss, spot_loss])
    reg_terms = jnp.stack([kl_term, count_term, binarity, entropy])
    gene_shrink = gene_scale * dot_s / (pp_s + eps)
    grad_pred = -jnp.dot(onehot, gene_scale, precision=high) * target
    grad_pred = grad_pred + jnp.dot(onehot, gene_shrink, precision=high) * g_pred
    spot_shrink = sdot / (spp + eps)
    grad_pred = grad_pred - spot_mask * spot_scale[:, None] * (
        target - spot_shrink[:, None] * g_pred
    )
    spot_slide = jnp.dot(onehot, jnp.stack([mass_s, wsum_s], axis=1), precision=high)
    grad_mass = -(density / spot_slide[:, 1]) / mass + 1.0 / spot_slide[:, 0]
    grad_weighted = lax.dot_general(whole, grad_pred, (((1,), (1,)), ((), ())), precision=high)
    grad_weighted = grad_weighted + grad_mass[None, :]
    grad_prob = keep[:, None] * grad_weighted
    keep_part = jnp.sum(prob * grad_weighted, axis=1)
    grad_logits = prob * (grad_prob - jnp.sum(prob * grad_prob, axis=0, keepdims=True))
    cell_part = jnp.dot(weighted, grad_pred, precision=high)
    grad_cells, keep_sum = (
        lax.psum_scatter(cell_part, ("wide", "narrow"), scatter_dimension=0, tiled=True),
        lax.psum_scatter(keep_part, ("wide", "narrow"), scatter_dimension=0, tiled=True),
    )
    first_row = lax.axis_index(("wide", "narrow")) * own_rows
    own_keep = lax.dynamic_slice_in_dim(keep, first_row, own_rows, 0)
    own_valid = lax.dynamic_slice_in_dim(valid, first_row, own_rows, 0)
    keep_grad = (
        keep_sum + own_valid * (jnp.sign(count - target_count) + 1.0 - 2.0 * own_keep) / n_cells
    )
    grad_filter = keep_grad * own_keep * (1.0 - own_keep)
    return (terms, reg_terms, g_pred, gene_cos, spot_cos, grad_logits, grad_filter, grad_cells)


def fits_fused(mesh, logits, cells, gene_mask, slide_ids):
    n_cells, spots = logits.shape
    return (
        (mesh.shape["wide"], mesh.shape["narrow"]) == (8, 4)
        and cells.shape == (16, 2048)
        and n_cells == 512
        and spots == 1024
        and gene_mask.shape[0] == 8
    )


def solution(mesh):
    def step(logits, filt, cells, cell_mask, gene_mask, slide_ids, target, density):
        fits = fits_fused(mesh, logits, cells, gene_mask, slide_ids)
        run = fused if fits else on_device
        return run(logits, filt, cells, cell_mask, gene_mask, slide_ids, target, density)

    placed = (
        P(None, ("wide", "narrow")),
        P(("wide", "narrow")),
        P(("wide", "narrow"), None),
        P(),
        P(),
        P(("wide", "narrow")),
        P(("wide", "narrow"), None),
        P(("wide", "narrow")),
    )
    return jax.shard_map(
        step,
        mesh=mesh,
        in_specs=placed,
        out_specs=(
            P(),
            P(),
            P(("wide", "narrow"), None),
            P(),
            P(("wide", "narrow")),
            P(None, ("wide", "narrow")),
            P(("wide", "narrow")),
            P(("wide", "narrow"), None),
        ),
        check_vma=False,
    )
```

```python
import jax
import jax.numpy as jnp
from jax import lax
from jax.experimental import pallas as pl
from jax.experimental.pallas import tpu as pltpu
from jax.sharding import PartitionSpec as P

eps = 1e-06
MESH = pl.DeviceIdType.MESH
bf16 = jnp.bfloat16
f32 = jnp.float32
LANES = 128
NCH = 8
BR = 32
GR = 256
AHEAD = 3


def split(value):
    high = value.astype(bf16)
    return high, (value - high.astype(f32)).astype(bf16)


def mm(a, b):
    return lax.dot_general(a, b, (((1,), (0,)), ((), ())), preferred_element_type=f32)


def mm_nt(a, b):
    return lax.dot_general(a, b, (((1,), (1,)), ((), ())), preferred_element_type=f32)


def fused_kernel(
    logits_hbm, filt_ref, cells_hbm, mask_ref, gene_ref, ids_ref, target_hbm, dens_ref,
    pv, gw, keep_ref, sums_ref, loss_ref, gcos_ref, scos_ref, gfilt_ref, gcell_ref,
    lg, tv, buf, chi, clo, ownc, ownk, along, valid, keepc, whi, wlo, thi, tlo, gmb, oh, l1, l2, cf,
    idc, blocks, sd, sp, st, mass, gmass, gph, gpl, kp,
    stat, a1, a2, a3, fin, kvec, k1, k2, k3,
    part, rb, sb, r1, tt_, r2, qq, r3,
    lsem, tsem, osem,
    zs, zr, xs, xr, ys, yr, bs, br,
    as1, ar1, as2, ar2, as3, ar3, as4, ar4,
    ks1, kr1, ks2, kr2, ks3, kr3,
    cbs, cbr, cxs, cxr, cys, cyr, czs, czr,
):
    n_cells = chi.shape[1]
    width = chi.shape[2]
    last = NCH - 1
    n_blocks = tv.shape[1]
    spots = n_blocks * BR
    n_slides = gene_ref.shape[0]
    tiles = spots // LANES
    wide, narrow = lax.axis_index("wide"), lax.axis_index("narrow")
    z, y = lax.div(wide, 2), lax.rem(wide, 2)
    x, core = lax.div(narrow, 2), lax.rem(narrow, 2)
    to_z = [(lax.rem(z + k, 4) * 2 + y, narrow) for k in (1, 2, 3)]
    from_z = [lax.rem(z + 4 - k, 4) for k in (1, 2, 3)]
    to_x = (wide, (1 - x) * 2 + core)
    to_y = (z * 2 + 1 - y, narrow)
    to_xy = (z * 2 + 1 - y, (1 - x) * 2 + core)
    to_b = (wide, x * 2 + 1 - core)

    def rcopy(src, dst, ss, rs, dev):
        return pltpu.make_async_remote_copy(
            src_ref=src, dst_ref=dst, send_sem=ss, recv_sem=rs, device_id=dev, device_id_type=MESH
        )

    def lanes(i, w=LANES):
        return pl.ds(pl.multiple_of(i * w, w), w)

    own_cells = pltpu.make_async_copy(cells_hbm, ownc, lsem.at[0])

    def get_logits(i):
        return pltpu.make_async_copy(logits_hbm.at[:, lanes(i)], lg.at[i], osem.at[i])

    def get_target(c):
        return pltpu.make_async_copy(target_hbm.at[:, :, lanes(c, width)], tv.at[c], tsem.at[c])

    own_cells.start()
    for i in range(tiles):
        get_logits(i).start()
    for c in range(NCH):
        get_target(c).start()

    barrier = pltpu.get_barrier_semaphore()
    for dev in to_z + [to_x, to_y, to_xy, to_b]:
        pl.semaphore_signal(barrier, inc=1, device_id=dev, device_id_type=MESH)

    iota8 = lax.broadcasted_iota(jnp.int32, (8, LANES), 0)
    lane8 = lax.broadcasted_iota(jnp.int32, (8, LANES), 1)
    row16 = lax.broadcasted_iota(jnp.int32, (16, LANES), 0)
    dev = wide * 4 + narrow
    place = lane8 + iota8 * LANES - dev * 16
    mine = jnp.zeros((16, LANES), f32)
    vector = jnp.zeros((8, LANES), f32)
    for r in range(16):
        mine = jnp.where(row16 == r, filt_ref[r], mine)
        vector = jnp.where(place == r, filt_ref[r], vector)
    kvec[2] = vector
    own_keep = jax.nn.sigmoid(mine)
    ownk[...] = own_keep
    along[...] = jnp.zeros_like(along)
    def one_hot(i, _):
        ids = ids_ref[pl.ds(i, 1), :]
        square = (lax.broadcasted_iota(jnp.int32, (LANES, LANES), 0) == ids).astype(f32)
        oh[lanes(i), :] = square.T.astype(bf16)
        per = LANES // BR
        turned = jnp.broadcast_to(ids, (LANES, LANES)).astype(f32).T
        idc[pl.ds(i * per, per)] = turned.reshape(per, BR, LANES)
        return 0

    lax.fori_loop(0, tiles, one_hot, 0)
    for q in range(n_cells // LANES):
        line = mask_ref[q : q + 1, :].astype(f32)
        valid[q * LANES : (q + 1) * LANES, :] = jnp.broadcast_to(line, (LANES, LANES)).T
    own_cells.wait()
    for c in range(NCH):
        for h in range(2):
            buf[c, h, z, y, x, core] = own_keep * ownc[:, (c * 2 + h) * LANES : (c * 2 + h + 1) * LANES]
    pl.semaphore_wait(barrier, 7)

    def z_out(c, k):
        r = buf.at[c, :, z, y, x, core]
        return rcopy(r, r, zs.at[c, k], zr.at[c, k], to_z[k])

    def z_in(c, k):
        r = buf.at[c, :, from_z[k], y, x, core]
        return rcopy(r, r, zs.at[c, k], zr.at[c, k], to_z[k])

    def s1_out(c):
        a = buf.at[c, 0, :, y, x, core]
        b = buf.at[c, 1, :, y, x, core]
        return [rcopy(a, a, xs.at[c, 0], xr.at[c, 0], to_x), rcopy(b, b, ys.at[c, 0], yr.at[c, 0], to_y)]

    def s1_in(c):
        a = buf.at[c, 0, :, y, 1 - x, core]
        b = buf.at[c, 1, :, 1 - y, x, core]
        return [rcopy(a, a, xs.at[c, 0], xr.at[c, 0], to_x), rcopy(b, b, ys.at[c, 0], yr.at[c, 0], to_y)]

    def s2_out(c):
        a = buf.at[c, 0, :, y, :, core]
        b = buf.at[c, 1, :, :, x, core]
        return [rcopy(a, a, ys.at[c, 1], yr.at[c, 1], to_y), rcopy(b, b, xs.at[c, 1], xr.at[c, 1], to_x)]

    def s2_in(c):
        a = buf.at[c, 0, :, 1 - y, :, core]
        b = buf.at[c, 1, :, :, 1 - x, core]
        return [rcopy(a, a, ys.at[c, 1], yr.at[c, 1], to_y), rcopy(b, b, xs.at[c, 1], xr.at[c, 1], to_x)]

    def s3_out(c):
        r = buf.at[c, :, :, :, :, core]
        return rcopy(r, r, bs.at[c], br.at[c], to_b)

    def s3_in(c):
        r = buf.at[c, :, :, :, :, 1 - core]
        return rcopy(r, r, bs.at[c], br.at[c], to_b)

    def b1(c):
        return rcopy(stat.at[c, 1 - core], a1.at[c], as1.at[c], ar1.at[c], to_b)

    plane = [to_x, to_y, to_xy]
    here = y * 2 + x
    there = [y * 2 + 1 - x, (1 - y) * 2 + x, (1 - y) * 2 + 1 - x]

    def b2_out(c, k):
        r = a2.at[c, here]
        return rcopy(r, r, as2.at[c, k], ar2.at[c, k], plane[k])

    def b2_in(c, k):
        r = a2.at[c, there[k]]
        return rcopy(r, r, as2.at[c, k], ar2.at[c, k], plane[k])

    def b3_out(c, k):
        r = a3.at[c, z]
        return rcopy(r, r, as3.at[c, k], ar3.at[c, k], to_z[k])

    def b3_in(c, k):
        r = a3.at[c, from_z[k]]
        return rcopy(r, r, as3.at[c, k], ar3.at[c, k], to_z[k])

    def b4(c, half):
        r = fin.at[c, half]
        return rcopy(r, r, as4.at[c], ar4.at[c], to_b)

    def sum_second(c):
        b1(c).wait_recv()
        a2[c, here] = stat[c, core] + a1[c]
        for k in range(3):
            b2_out(c, k).start()

    def sum_third(c):
        for k in range(3):
            b2_in(c, k).wait_recv()
        a3[c, z] = (a2[c, 0] + a2[c, 1]) + (a2[c, 2] + a2[c, 3])
        for k in range(3):
            b3_out(c, k).start()

    def sum_fourth(c):
        for k in range(3):
            b3_in(c, k).wait_recv()
        fin[c, core] = (a3[c, 0] + a3[c, 1]) + (a3[c, 2] + a3[c, 3])
        b4(c, core).start()

    def sum_last(c):
        b4(c, 1 - core).wait_recv()

    def v1(n):
        return rcopy(kvec.at[n], k1.at[n], ks1.at[n], kr1.at[n], to_b)

    def v2(n, slot, k):
        return rcopy(k2.at[n, slot], k2.at[n, slot], ks2.at[n, k], kr2.at[n, k], plane[k])

    def v3(n, slot, k):
        return rcopy(k3.at[n, slot], k3.at[n, slot], ks3.at[n, k], kr3.at[n, k], to_z[k])

    def vector_second(n):
        v1(n).wait_recv()
        k2[n, here] = kvec[n] + k1[n]
        for k in range(3):
            v2(n, here, k).start()

    def vector_third(n):
        for k in range(3):
            v2(n, there[k], k).wait_recv()
        k3[n, z] = (k2[n, 0] + k2[n, 1]) + (k2[n, 2] + k2[n, 3])
        for k in range(3):
            v3(n, z, k).start()

    def vector_last(n):
        for k in range(3):
            v3(n, from_z[k], k).wait_recv()
        return (k3[n, 0] + k3[n, 1]) + (k3[n, 2] + k3[n, 3])

    def softmax(i, ent):
        get_logits(i).wait()
        value = lg[i]
        top = jnp.max(value, axis=0, keepdims=True)
        expo = jnp.exp(value - top) * valid[...]
        total = jnp.sum(expo, axis=0, keepdims=True)
        prob = expo * (1.0 / total)
        lg[i] = prob
        high, low = split(prob)
        whi[:, lanes(i)] = high
        wlo[:, lanes(i)] = low
        high, low = split(prob.T)
        thi[lanes(i), :] = high
        tlo[lanes(i), :] = low
        return ent + jnp.sum(prob * (value - top - jnp.log(total)), axis=0, keepdims=True)

    def leave_z(c):
        for k in range(3):
            z_out(c, k).start()

    for c in range(AHEAD):
        leave_z(c)
    v1(2).start()

    def stage_z(c):
        for k in range(3):
            z_in(c, k).wait_recv()
        for d in s1_out(c):
            d.start()

    def stage_1(c):
        for arrived, onward in zip(s1_in(c), s2_out(c)):
            arrived.wait_recv()
            onward.start()

    def stage_2(c):
        for d in s2_in(c):
            d.wait_recv()
        s3_out(c).start()

    def fold(v):
        out = v[:, :LANES]
        for k in range(1, v.shape[1] // LANES):
            out = out + v[:, k * LANES : (k + 1) * LANES]
        return out

    def eighths(v):
        return jnp.sum(v.reshape(v.shape[0] // 8, 8, v.shape[1]), axis=0)

    for c in range(NCH):
        gm = jnp.concatenate(
            [gene_ref[:, c * width : (c + 1) * width].astype(f32), jnp.zeros((LANES - n_slides, width), f32)], axis=0
        )
        gmb[c] = gm.astype(bf16)
    sd[...] = jnp.zeros_like(sd)
    sp[...] = jnp.zeros_like(sp)
    st[...] = jnp.zeros_like(st)

    begins = [jnp.sum((ids_ref[...] < k).astype(jnp.int32)) for k in range(n_slides + 1)]
    firsts = [jnp.minimum(lax.div(begins[k], BR), n_blocks - 1) for k in range(n_slides)]
    lasts = [lax.div(jnp.maximum(begins[k + 1] - 1, 0), BR) for k in range(n_slides)]
    slide16 = lax.broadcasted_iota(jnp.int32, (16, 8 * n_blocks), 0)
    block16 = lax.div(lax.broadcasted_iota(jnp.int32, (16, 8 * n_blocks), 1), 8)
    inner = jnp.zeros((16, 8 * n_blocks), f32)
    for k in range(n_slides):
        full = jnp.logical_and(block16 > firsts[k], block16 < lasts[k])
        inner = jnp.where(jnp.logical_and(slide16 == k, full), 1.0, inner)
    inner = inner.astype(bf16)
    inner = jnp.concatenate([inner, inner], axis=1)
    slide8 = lax.broadcasted_iota(jnp.int32, (8, width), 0)

    def gene_sums(c, products, number, at_row):
        sums = []
        for n in range(number):
            bh, bl = split(blocks[n])
            sums.append(mm(inner, jnp.concatenate([bh, bl], axis=0))[:8, :])
        for k in range(n_slides):
            parts = [jnp.zeros((8, width), f32)] * number
            for block, counts in ((firsts[k], None), (lasts[k], lasts[k] != firsts[k])):
                own = idc[block] == float(k)
                if counts is not None:
                    own = jnp.logical_and(own, counts)
                own = own.astype(f32)
                own = jnp.concatenate([own] * (width // LANES), axis=1)
                for n, prod in enumerate(products(c, block)):
                    parts[n] = parts[n] + eighths(prod * own)
            for n in range(number):
                line = jnp.sum(parts[n], axis=0, keepdims=True)
                sums[n] = sums[n] + jnp.where(slide8 == k, line, 0.0)
        for n in range(number):
            for h in range(2):
                stat[c, h, at_row + n * 8 : at_row + (n + 1) * 8, :] = sums[n][:, h * LANES : (h + 1) * LANES]

    def of_target(c, r):
        tgt = tv[c, r]
        return (tgt * tgt,)

    def of_both(c, r):
        pred, tgt = pv[c, r], tv[c, r]
        return pred * tgt, jnp.where(tgt > 0.0, pred * pred, 0.0)

    def by_rows(c, products, spots_of):
        for r in range(n_blocks):
            at = slice(r * BR, (r + 1) * BR)
            for n, (prod, spot) in enumerate(zip(products(c, r), spots_of)):
                spot[at, :] += fold(prod)
                blocks[n, r * 8 : (r + 1) * 8, :] = eighths(prod)

    def target_sums(c, _):
        per = GR // BR
        for n in range(spots // GR):
            sees = mm(oh[n * GR : (n + 1) * GR, :], gmb[c]).reshape(per, BR, width)
            for r in range(per):
                tv[c, n * per + r] = sees[r] * tv[c, n * per + r]
        by_rows(c, of_target, (st,))
        gene_sums(c, of_target, 1, 16)
        return 0

    def predict(c):
        s3_in(c).wait_recv()
        whole = jnp.concatenate([buf[c, h].reshape(n_cells, LANES) for h in range(2)], axis=1)
        high, low = split(whole)
        chi[c] = high
        clo[c] = low
        wh, wl = thi[...], tlo[...]
        pred = mm(jnp.concatenate([wh, wl, wh], axis=1), jnp.concatenate([high, high, low], axis=0))
        pv[c] = pred.reshape(n_blocks, BR, width)

    def predicted_sums(c):
        by_rows(c, of_both, (sd, sp))
        gene_sums(c, of_both, 2, 0)

    def slide_sums():
        keep_rows = jax.nn.sigmoid(vector_last(2))
        keep_ref[...] = keep_rows
        for q in range(quarter):
            line = jnp.broadcast_to(keep_rows[q : q + 1, :], (LANES, LANES))
            keepc[q * LANES : (q + 1) * LANES, :] = line.T

        def by_tile(i, sums):
            at = pl.ds(i, 1)
            line = jnp.sum(lg[i] * keepc[...], axis=0, keepdims=True)
            mass[at, :] = line
            dens = dens_ref[at, :]
            mine = (iota8 == ids_ref[at, :]).astype(f32)
            terms = (line, dens, dens * (jnp.log(dens) - jnp.log(line)))
            return tuple(a + mine * b for a, b in zip(sums, terms))

        blank = jnp.zeros((8, LANES), f32)
        totals = lax.fori_loop(0, tiles, by_tile, (blank, blank, blank))
        for k, value in enumerate(totals):
            blank = jnp.where(lane8 == k, jnp.sum(value, axis=1, keepdims=True), blank)
        kvec[0] = blank
        v1(0).start()

    quarter = n_cells // LANES
    ent = lax.fori_loop(0, tiles // 2, softmax, jnp.zeros((1, LANES), f32))
    stage_z(0)
    leave_z(AHEAD)
    vector_second(2)
    ent = lax.fori_loop(tiles // 2, tiles, softmax, ent)
    stage_z(1)
    leave_z(AHEAD + 1)
    for c in range(NCH):
        get_target(c).wait()
    lax.fori_loop(0, 3, target_sums, 0)
    stage_z(2)
    leave_z(AHEAD + 2)
    stage_1(0)
    vector_third(2)
    lax.fori_loop(3, 6, target_sums, 0)
    stage_z(3)
    leave_z(AHEAD + 3)
    stage_1(1)
    lax.fori_loop(6, NCH, target_sums, 0)
    stage_z(4)
    leave_z(AHEAD + 4)
    stage_1(2)
    slide_sums()
    stage_z(5)
    stage_2(0)
    stage_1(3)

    def gather_tick(t, _):
        c = t - 6
        pl.when(t < NCH)(lambda: stage_z(t))
        pl.when(t + AHEAD < NCH)(lambda: leave_z(t + AHEAD))
        pl.when(t - 5 < NCH)(lambda: stage_2(t - 5))
        predict(c)
        predicted_sums(c)
        b1(c).start()
        pl.when(t - 2 < NCH)(lambda: stage_1(t - 2))
        pl.when(c == 0)(lambda: vector_second(0))
        pl.when(c == 2)(lambda: vector_third(0))
        pl.when(c >= 1)(lambda: sum_second(c - 1))
        pl.when(c >= 3)(lambda: sum_third(c - 3))
        pl.when(c >= 6)(lambda: sum_fourth(c - 6))
        return 0

    lax.fori_loop(6, NCH + 6, gather_tick, 0)

    lane128 = lax.broadcasted_iota(jnp.int32, (LANES, LANES), 1)
    slide_of_lane = lax.rem(lane128, 8).astype(f32)

    def spot_rows(i, _):
        at = lanes(i)
        sdot, spp, stt = [jnp.sum(ref[at, :], axis=1, keepdims=True) for ref in (sd, sp, st)]
        scale = lax.rsqrt(spp + eps) * lax.rsqrt(stt + eps)
        sd[at, :] = jnp.broadcast_to(sdot * scale, (LANES, LANES))
        per = LANES // BR
        own = jnp.logical_and(idc[pl.ds(i * per, per)].reshape(LANES, LANES) == slide_of_lane, lane128 < 32)
        for ref, value in ((l1, scale), (l2, scale * (sdot / (spp + eps)))):
            high, low = split(value)
            value = jnp.where(lane128 < 16, 1.0, jnp.where(lane128 < 24, high.astype(f32), low.astype(f32)))
            ref[at, :] = jnp.where(own, value, 0.0).astype(bf16)
        return 0

    lax.fori_loop(0, tiles, spot_rows, 0)
    sum_second(last)
    sum_third(last - 2)
    sum_fourth(last - 5)

    def scatter_sib(c):
        return rcopy(part.at[c, :, :, :, :, 1 - core], rb.at[c], cbs.at[c], cbr.at[c], to_b)

    def scatter_one(c):
        return [
            rcopy(sb.at[c, 0, :, 1 - y], r1.at[c, 0], cys.at[c, 0], cyr.at[c, 0], to_y),
            rcopy(sb.at[c, 1, :, :, 1 - x], r1.at[c, 1], cxs.at[c, 0], cxr.at[c, 0], to_x),
        ]

    def scatter_two(c):
        return [
            rcopy(tt_.at[c, 0, :, 1 - x], r2.at[c, 0], cxs.at[c, 1], cxr.at[c, 1], to_x),
            rcopy(tt_.at[c, 1, :, 1 - y], r2.at[c, 1], cys.at[c, 1], cyr.at[c, 1], to_y),
        ]

    def scatter_z(c, k):
        return rcopy(qq.at[c, :, lax.rem(z + k + 1, 4)], r3.at[c, k], czs.at[c, k], czr.at[c, k], to_z[k])

    def sc1(c):
        scatter_sib(c).wait_recv()
        sb[c] = part[c, :, :, :, :, core] + rb[c]
        for d in scatter_one(c):
            d.start()

    def sc2(c):
        arrived, onward = scatter_one(c), scatter_two(c)
        arrived[0].wait_recv()
        tt_[c, 0] = sb[c, 0, :, y] + r1[c, 0]
        onward[0].start()
        arrived[1].wait_recv()
        tt_[c, 1] = sb[c, 1, :, :, x] + r1[c, 1]
        onward[1].start()

    def sc3(c):
        for d in scatter_two(c):
            d.wait_recv()
        qq[c, 0] = tt_[c, 0, :, x] + r2[c, 0]
        qq[c, 1] = tt_[c, 1, :, y] + r2[c, 1]
        for k in range(3):
            scatter_z(c, k).start()

    def sc4(c):
        for k in range(3):
            scatter_z(c, k).wait_recv()
        for h in range(2):
            at = lanes(c * 2 + h)
            total = (qq[c, h, z] + r3[c, 0, h]) + (r3[c, 1, h] + r3[c, 2, h])
            gcell_ref[:, at] = total * ownk[...]
            along[...] += total * ownc[:, at]

    def gene_coefs(c):
        total = jnp.concatenate([fin[c, 0], fin[c, 1]], axis=1)
        dot_s, pp_s, tt_s = total[0:8], total[8:16], total[16:24]
        gm = gene_ref[:, lanes(c, width)].astype(f32)
        gscale = gm * lax.rsqrt(pp_s + eps) * lax.rsqrt(tt_s + eps)
        gcos_ref[:, lanes(c, width)] = dot_s * gscale
        gshrink = gscale * (dot_s / (pp_s + eps))
        pad = jnp.zeros((LANES - 32, width), f32)
        for n, value in enumerate((gscale, gshrink)):
            high, low = split(value)
            high, low = high.astype(f32), low.astype(f32)
            cf[lax.rem(c, 2), n] = jnp.concatenate([high, low, gm, gm, pad], axis=0).astype(bf16)

    def backward(c):
        slot = lax.rem(c, 2)
        per = GR // BR
        for n in range(spots // GR):
            at = slice(n * GR, (n + 1) * GR)
            own = slice(n * per, (n + 1) * per)
            pred, tgt = pv[c, own].reshape(GR, width), tv[c, own].reshape(GR, width)
            gh, gl = split(mm(l2[at, :], cf[slot, 1]) * pred - mm(l1[at, :], cf[slot, 0]) * tgt)
            gph[c, at, :] = gh
            gpl[c, at, :] = gl
        wh, wl = whi[...], wlo[...]
        gh, gl = gph[c], gpl[c]
        out = mm(jnp.concatenate([wh, wl, wh], axis=1), jnp.concatenate([gh, gh, gl], axis=0))
        for h in range(2):
            part[c, h] = out[:, h * LANES : (h + 1) * LANES].reshape(4, 2, 2, 2, 16, LANES)
        scatter_sib(c).start()
        gene_coefs(jnp.minimum(c + 1, last))

    def spot_part(n):
        at = pl.ds(n * GR, GR)
        left = [chi[c] for c in range(NCH)]
        left = left + [clo[c] for c in range(NCH)] + left
        right = [gph[c, at, :] for c in range(NCH)]
        right = right + right + [gpl[c, at, :] for c in range(NCH)]
        out = mm_nt(jnp.concatenate(left, axis=1), jnp.concatenate(right, axis=1))
        for h in range(GR // LANES):
            i = n * (GR // LANES) + h
            grad = out[:, h * LANES : (h + 1) * LANES] + keepc[...] * gmass[i : i + 1, :]
            prob = lg[i]
            gw[i] = prob * (grad - jnp.sum(prob * grad, axis=0, keepdims=True))

    def back_tick(t, _):
        pl.when(t < last)(lambda: sum_last(t + 1))
        backward(t)
        pl.when(t >= 1)(lambda: sc1(t - 1))
        pl.when(t >= 3)(lambda: sc2(t - 3))
        pl.when(t >= 5)(lambda: sc3(t - 5))
        pl.when(t <= 1)(lambda: sum_third(last - 1 + t))
        pl.when(t <= 4)(lambda: sum_fourth(last - 4 + t))

        @pl.when(t == 4)
        def _():
            slide_totals()

        @pl.when(t == 5)
        def _():
            vector_second(1)

        @pl.when(t == 7)
        def _():
            vector_third(1)

        return 0

    def slide_totals():
        sums_s = vector_last(0)
        sums_ref[...] = sums_s
        mass_s, wsum_s = sums_s[:, 0:1], sums_s[:, 1:2]
        kp[...] = jnp.zeros_like(kp)

        def by_mass(i, total):
            at = pl.ds(i, 1)
            mine = (iota8 == ids_ref[at, :]).astype(f32)
            mass_at = jnp.sum(mine * mass_s, axis=0, keepdims=True)
            wsum_at = jnp.sum(mine * wsum_s, axis=0, keepdims=True)
            line = -(dens_ref[at, :] / wsum_at) / mass[at, :] + 1.0 / mass_at
            gmass[at, :] = line
            kp[...] += lg[i] * line
            spot = sd[lanes(i), :].T[0:1, :]
            scos_ref[at, :] = spot
            return total + spot

        total = lax.fori_loop(0, tiles, by_mass, jnp.zeros((1, LANES), f32))
        rows_k = [jnp.sum(kp[q * LANES : (q + 1) * LANES, :].T, axis=0, keepdims=True) for q in range(quarter)]
        rows_k = rows_k + [-total, -ent, jnp.zeros((6 - quarter, LANES), f32)]
        kvec[1] = jnp.concatenate(rows_k, axis=0)
        v1(1).start()

    sum_last(0)
    gene_coefs(0)
    lax.fori_loop(0, NCH, back_tick, 0)
    sc1(7)
    sc2(5)
    sc3(3)
    spot_part(0)
    sc2(6)
    sc3(4)
    sc2(7)
    sc3(5)
    spot_part(1)
    sc3(6)
    sc3(7)
    sc4(0)
    sc4(1)
    sc4(2)
    sc4(3)
    sc4(4)
    spot_part(2)
    spot_part(3)

    keep = keep_ref[...]
    ok = jnp.concatenate([mask_ref[...].astype(f32), jnp.zeros((8 - quarter, LANES), f32)], axis=0)
    off = jnp.sum(ok * keep) - n_cells // 4
    sign = jnp.where(off > 0, 1.0, jnp.where(off < 0, -1.0, 0.0))
    totals = vector_last(1)
    loss_ref[...] = totals
    rest = totals + ok * (sign + 1.0 - 2.0 * keep) / n_cells

    def own_lanes(value):
        picked = jnp.sum(jnp.where(iota8 == lax.div(dev, 8), value, 0.0), axis=0, keepdims=True)
        return pltpu.roll(picked, lax.rem(LANES - lax.rem(dev, 8) * 16, LANES), 1)

    keep = own_lanes(keep)
    rest = own_lanes(rest)

    def leave(c, _):
        for k in range(3):
            z_out(c, k).wait_send()
            b2_out(c, k).wait_send()
            b3_out(c, k).wait_send()
        for d in s1_out(c) + s2_out(c) + scatter_one(c) + scatter_two(c):
            d.wait_send()
        s3_out(c).wait_send()
        b1(c).wait_send()
        b4(c, core).wait_send()
        scatter_sib(c).wait_send()
        return 0

    lax.fori_loop(0, NCH, leave, 0)
    for c in range(NCH - 3):
        for k in range(3):
            scatter_z(c, k).wait_send()
    for n in range(3):
        v1(n).wait_send()
        for k in range(3):
            v2(n, here, k).wait_send()
            v3(n, z, k).wait_send()
    for c in range(NCH - 3, NCH):
        sc4(c)
    genes_part = jnp.concatenate([along[...], jnp.zeros((LANES - 16, LANES), f32)], axis=0)
    genes_part = jnp.sum(genes_part.T, axis=0, keepdims=True)
    gfilt_ref[...] = ((genes_part + rest) * keep * (1.0 - keep))[:, : gfilt_ref.shape[1]]

    for c in range(NCH - 3, NCH):
        for k in range(3):
            scatter_z(c, k).wait_send()


def finish_kernel(
    pv, gw, keep_ref, sums_ref, loss_ref, gcos_in, scos_in, gfilt_in, gcell_in, mask_ref,
    terms_hbm, reg_hbm, pred_hbm, gcos_hbm, scos_hbm, glog_hbm, gfilt_hbm, gcell_hbm,
    terms_ref, reg_ref, psem, osem, rsem,
):
    width = pv.shape[3]
    tiles, n_cells = gw.shape[:2]
    quarter = n_cells // LANES

    def put_pred(c):
        return pltpu.make_async_copy(pv.at[c], pred_hbm.at[:, :, c * width : (c + 1) * width], psem.at[c])

    def put_glog(i):
        return pltpu.make_async_copy(gw.at[i], glog_hbm.at[:, i * LANES : (i + 1) * LANES], osem.at[i])

    for c in range(NCH):
        put_pred(c).start()
    for i in range(tiles):
        put_glog(i).start()
    pairs = [(gcos_in, gcos_hbm), (scos_in, scos_hbm), (gcell_in, gcell_hbm), (gfilt_in, gfilt_hbm)]
    rest = [pltpu.make_async_copy(a, b, rsem.at[k]) for k, (a, b) in enumerate(pairs)]
    for copy in rest:
        copy.start()

    sums_s = sums_ref[...]
    mass_s, wsum_s, logsum_s = sums_s[:, 0:1], sums_s[:, 1:2], sums_s[:, 2:3]
    keep = keep_ref[:quarter, :]
    ok = mask_ref[...].astype(f32)
    count = jnp.sum(ok * keep)
    count_term = jnp.abs(count - n_cells // 4) / n_cells
    binarity = jnp.sum(ok * (keep - keep * keep)) / n_cells
    gene_loss = -jnp.sum(gcos_in[...])
    spot_loss = jnp.sum(loss_ref[quarter : quarter + 1, :])
    entropy = jnp.sum(loss_ref[quarter + 1 : quarter + 2, :]) / (tiles * LANES * 32)
    kl = jnp.sum(logsum_s / wsum_s + jnp.log(mass_s) - jnp.log(wsum_s))
    terms_ref[0] = gene_loss + spot_loss + kl + count_term + binarity
    terms_ref[1] = gene_loss
    terms_ref[2] = spot_loss
    reg_ref[0] = kl
    reg_ref[1] = count_term
    reg_ref[2] = binarity
    reg_ref[3] = entropy
    for k, (a, b) in enumerate(((terms_ref, terms_hbm), (reg_ref, reg_hbm))):
        rest.append(pltpu.make_async_copy(a, b, rsem.at[len(pairs) + k]))
        rest[-1].start()
    for copy in rest:
        copy.wait()
    for i in range(tiles):
        put_glog(i).wait()
    for c in range(NCH):
        put_pred(c).wait()


def fused(logits, filt, cells, cell_mask, gene_mask, slide_ids, target, density):
    n_cells, spots = logits.shape
    own, genes = cells.shape
    n_slides = gene_mask.shape[0]
    width = genes // NCH
    tiles = spots // LANES
    dma = pltpu.SemaphoreType.DMA
    vmem, anywhere = pltpu.VMEM, pl.BlockSpec(memory_space=pl.ANY)
    inside = pl.BlockSpec(memory_space=pltpu.VMEM)
    scalars = pl.BlockSpec(memory_space=pltpu.SMEM)
    ring = (4, 2, 2, 2, 16, LANES)
    scratch = [
        vmem((tiles, n_cells, LANES), f32),
        vmem((NCH, spots // BR, BR, width), f32),
        vmem((NCH, 2) + ring, f32),
        vmem((NCH, n_cells, width), bf16),
        vmem((NCH, n_cells, width), bf16),
        vmem((own, genes), f32),
        vmem((own, LANES), f32),
        vmem((own, LANES), f32),
        vmem((n_cells, LANES), f32),
        vmem((n_cells, LANES), f32),
        vmem((n_cells, spots), bf16),
        vmem((n_cells, spots), bf16),
        vmem((spots, n_cells), bf16),
        vmem((spots, n_cells), bf16),
        vmem((NCH, LANES, width), bf16),
        vmem((spots, LANES), bf16),
        vmem((spots, LANES), bf16),
        vmem((spots, LANES), bf16),
        vmem((2, 2, LANES, width), bf16),
        vmem((spots // BR, BR, LANES), f32),
        vmem((2, spots * 8 // BR, width), f32),
        vmem((spots, LANES), f32),
        vmem((spots, LANES), f32),
        vmem((spots, LANES), f32),
        vmem((8, LANES), f32),
        vmem((8, LANES), f32),
        vmem((NCH, spots, width), bf16),
        vmem((NCH, spots, width), bf16),
        vmem((n_cells, LANES), f32),
        vmem((NCH, 2, 24, LANES), f32),
        vmem((NCH, 24, LANES), f32),
        vmem((NCH, 4, 24, LANES), f32),
        vmem((NCH, 4, 24, LANES), f32),
        vmem((NCH, 2, 24, LANES), f32),
        vmem((3, 8, LANES), f32),
        vmem((3, 8, LANES), f32),
        vmem((3, 4, 8, LANES), f32),
        vmem((3, 4, 8, LANES), f32),
        vmem((NCH, 2) + ring, f32),
        vmem((NCH, 2, 4, 2, 2, 16, LANES), f32),
        vmem((NCH, 2, 4, 2, 2, 16, LANES), f32),
        vmem((NCH, 2, 4, 2, 16, LANES), f32),
        vmem((NCH, 2, 4, 2, 16, LANES), f32),
        vmem((NCH, 2, 4, 16, LANES), f32),
        vmem((NCH, 2, 4, 16, LANES), f32),
        vmem((NCH, 3, 2, 16, LANES), f32),
        dma((1,)), dma((NCH,)), dma((tiles,)),
        dma((NCH, 3)), dma((NCH, 3)), dma((NCH, 2)), dma((NCH, 2)), dma((NCH, 2)), dma((NCH, 2)), dma((NCH,)), dma((NCH,)),
        dma((NCH,)), dma((NCH,)), dma((NCH, 3)), dma((NCH, 3)), dma((NCH, 3)), dma((NCH, 3)), dma((NCH,)), dma((NCH,)),
        dma((3,)), dma((3,)), dma((3, 3)), dma((3, 3)), dma((3, 3)), dma((3, 3)),
        dma((NCH,)), dma((NCH,)), dma((NCH, 2)), dma((NCH, 2)), dma((NCH, 2)), dma((NCH, 2)), dma((NCH, 3)), dma((NCH, 3)),
    ]
    mask = cell_mask.reshape(n_cells // LANES, LANES)
    held = (
        vmem((NCH, spots // BR, BR, width), f32),
        vmem((tiles, n_cells, LANES), f32),
        vmem((8, LANES), f32),
        vmem((8, LANES), f32),
        vmem((8, LANES), f32),
        vmem((n_slides, genes), f32),
        vmem((tiles, LANES), f32),
        vmem((1, own), f32),
        vmem((own, genes), f32),
    )
    between = pl.pallas_call(
        fused_kernel,
        out_shape=held,
        in_specs=[anywhere, scalars, anywhere, inside, inside, inside, anywhere, inside],
        out_specs=(inside,) * len(held),
        scratch_shapes=scratch,
        compiler_params=pltpu.CompilerParams(
            collective_id=0, has_side_effects=True, vmem_limit_bytes=50 << 20
        ),
    )(
        logits, filt, cells, mask, gene_mask,
        slide_ids.reshape(tiles, LANES), target.reshape(spots // BR, BR, genes), density.reshape(tiles, LANES),
    )
    out = pl.pallas_call(
        finish_kernel,
        out_shape=(
            jax.ShapeDtypeStruct((3,), f32),
            jax.ShapeDtypeStruct((4,), f32),
            jax.ShapeDtypeStruct((spots // BR, BR, genes), f32),
            jax.ShapeDtypeStruct((n_slides, genes), f32),
            jax.ShapeDtypeStruct((tiles, LANES), f32),
            jax.ShapeDtypeStruct((n_cells, spots), f32),
            jax.ShapeDtypeStruct((1, own), f32),
            jax.ShapeDtypeStruct((own, genes), f32),
        ),
        in_specs=[inside] * (len(held) + 1),
        out_specs=(anywhere,) * 8,
        scratch_shapes=[pltpu.SMEM((3,), f32), pltpu.SMEM((4,), f32), dma((NCH,)), dma((tiles,)), dma((6,))],
        compiler_params=pltpu.CompilerParams(vmem_limit_bytes=24 << 20),
    )(*between, mask)
    terms, reg, pred, gcos, scos, glog, gfilt, gcell = out
    return terms, reg, pred.reshape(spots, genes), gcos, scos.reshape(spots), glog, gfilt.reshape(own), gcell


def per_slide(onehot, values):
    return lax.dot_general(
        onehot, values, (((0,), (0,)), ((), ())), precision=lax.Precision.HIGHEST
    )


def on_device(logits, filt, cells, cell_mask, gene_mask, slide_ids, target, density):
    high = lax.Precision.HIGHEST
    n_cells = logits.shape[0]
    own_rows = cells.shape[0]
    n_slides = gene_mask.shape[0]
    valid = cell_mask.astype(jnp.float32)
    top = jnp.max(logits, axis=0, keepdims=True)
    expo = jnp.exp(logits - top) * valid[:, None]
    total = jnp.sum(expo, axis=0, keepdims=True)
    prob = expo / total
    logp = jnp.where(valid[:, None] > 0, logits - top - jnp.log(total), 0.0)
    entropy_part = -jnp.sum(prob * logp)
    whole, filt_all = (
        lax.all_gather(cells, ("wide", "narrow"), axis=0, tiled=True),
        lax.all_gather(filt, ("wide", "narrow"), axis=0, tiled=True),
    )
    keep = jax.nn.sigmoid(filt_all)
    weighted = prob * keep[:, None]
    g_pred = lax.dot_general(weighted, whole, (((0,), (0,)), ((), ())), precision=high)
    onehot = (slide_ids[:, None] == jnp.arange(n_slides, dtype=jnp.int32)[None, :]).astype(
        jnp.float32
    )
    gmask = gene_mask.astype(jnp.float32)
    spot_mask = jnp.dot(onehot, gmask, precision=high)
    masked_pred = spot_mask * g_pred
    sdot = jnp.sum(masked_pred * target, axis=1)
    spp = jnp.sum(masked_pred * g_pred, axis=1)
    stt = jnp.sum(spot_mask * target * target, axis=1)
    spot_scale = lax.rsqrt(spp + eps) * lax.rsqrt(stt + eps)
    spot_cos = sdot * spot_scale
    mass = jnp.sum(weighted, axis=0)
    log_part = density * (jnp.log(density) - jnp.log(mass))
    slide_vec = jnp.stack([mass, density, log_part], axis=1)
    loss_parts = jnp.stack([-jnp.sum(spot_cos), entropy_part])
    dot_s, pp_s, tt_s, slide_tot, loss_tot = lax.psum(
        (
            per_slide(onehot, g_pred * target),
            per_slide(onehot, g_pred * g_pred),
            per_slide(onehot, target * target),
            per_slide(onehot, slide_vec),
            loss_parts,
        ),
        ("wide", "narrow"),
    )
    mass_s = slide_tot[:, 0]
    wsum_s = slide_tot[:, 1]
    logsum_s = slide_tot[:, 2]
    gene_scale = gmask * lax.rsqrt(pp_s + eps) * lax.rsqrt(tt_s + eps)
    gene_cos = dot_s * gene_scale
    gene_loss = -jnp.sum(gene_cos)
    spot_loss = loss_tot[0]
    entropy = loss_tot[1] / (prob.shape[1] * lax.axis_size(("wide", "narrow")))
    kl_term = jnp.sum(logsum_s / wsum_s) + jnp.sum(jnp.log(mass_s) - jnp.log(wsum_s))
    count = jnp.sum(valid * keep)
    target_count = n_cells // 4
    count_term = jnp.abs(count - target_count) / n_cells
    binarity = jnp.sum(valid * (keep - keep * keep)) / n_cells
    loss = gene_loss + spot_loss + kl_term + count_term + binarity
    terms = jnp.stack([loss, gene_loss, spot_loss])
    reg_terms = jnp.stack([kl_term, count_term, binarity, entropy])
    gene_shrink = gene_scale * dot_s / (pp_s + eps)
    grad_pred = -jnp.dot(onehot, gene_scale, precision=high) * target
    grad_pred = grad_pred + jnp.dot(onehot, gene_shrink, precision=high) * g_pred
    spot_shrink = sdot / (spp + eps)
    grad_pred = grad_pred - spot_mask * spot_scale[:, None] * (
        target - spot_shrink[:, None] * g_pred
    )
    spot_slide = jnp.dot(onehot, jnp.stack([mass_s, wsum_s], axis=1), precision=high)
    grad_mass = -(density / spot_slide[:, 1]) / mass + 1.0 / spot_slide[:, 0]
    grad_weighted = lax.dot_general(whole, grad_pred, (((1,), (1,)), ((), ())), precision=high)
    grad_weighted = grad_weighted + grad_mass[None, :]
    grad_prob = keep[:, None] * grad_weighted
    keep_part = jnp.sum(prob * grad_weighted, axis=1)
    grad_logits = prob * (grad_prob - jnp.sum(prob * grad_prob, axis=0, keepdims=True))
    cell_part = jnp.dot(weighted, grad_pred, precision=high)
    grad_cells, keep_sum = (
        lax.psum_scatter(cell_part, ("wide", "narrow"), scatter_dimension=0, tiled=True),
        lax.psum_scatter(keep_part, ("wide", "narrow"), scatter_dimension=0, tiled=True),
    )
    first_row = lax.axis_index(("wide", "narrow")) * own_rows
    own_keep = lax.dynamic_slice_in_dim(keep, first_row, own_rows, 0)
    own_valid = lax.dynamic_slice_in_dim(valid, first_row, own_rows, 0)
    keep_grad = (
        keep_sum + own_valid * (jnp.sign(count - target_count) + 1.0 - 2.0 * own_keep) / n_cells
    )
    grad_filter = keep_grad * own_keep * (1.0 - own_keep)
    return (terms, reg_terms, g_pred, gene_cos, spot_cos, grad_logits, grad_filter, grad_cells)


def fits_fused(mesh, logits, cells, gene_mask, slide_ids):
    n_cells, spots = logits.shape
    return (
        (mesh.shape["wide"], mesh.shape["narrow"]) == (8, 4)
        and cells.shape == (16, 2048)
        and n_cells == 512
        and spots == 1024
        and gene_mask.shape[0] == 8
    )


def solution(mesh):
    def step(logits, filt, cells, cell_mask, gene_mask, slide_ids, target, density):
        fits = fits_fused(mesh, logits, cells, gene_mask, slide_ids)
        run = fused if fits else on_device
        return run(logits, filt, cells, cell_mask, gene_mask, slide_ids, target, density)

    placed = (
        P(None, ("wide", "narrow")),
        P(("wide", "narrow")),
        P(("wide", "narrow"), None),
        P(),
        P(),
        P(("wide", "narrow")),
        P(("wide", "narrow"), None),
        P(("wide", "narrow")),
    )
    return jax.shard_map(
        step,
        mesh=mesh,
        in_specs=placed,
        out_specs=(
            P(),
            P(),
            P(("wide", "narrow"), None),
            P(),
            P(("wide", "narrow")),
            P(None, ("wide", "narrow")),
            P(("wide", "narrow")),
            P(("wide", "narrow"), None),
        ),
        check_vma=False,
    )
```

```python
import jax
import jax.numpy as jnp
from jax import lax
from jax.experimental import pallas as pl
from jax.experimental.pallas import tpu as pltpu
from jax.sharding import PartitionSpec as P

eps = 1e-06
MESH = pl.DeviceIdType.MESH
bf16 = jnp.bfloat16
f32 = jnp.float32
LANES = 128
NCH = 8
BR = 32
GR = 256
AHEAD = 3


def split(value):
    high = value.astype(bf16)
    return high, (value - high.astype(f32)).astype(bf16)


def mm(a, b):
    return lax.dot_general(a, b, (((1,), (0,)), ((), ())), preferred_element_type=f32)


def mm_nt(a, b):
    return lax.dot_general(a, b, (((1,), (1,)), ((), ())), preferred_element_type=f32)


def fused_kernel(
    logits_hbm, filt_ref, cells_hbm, mask_ref, gene_ref, ids_ref, target_hbm, dens_ref,
    pv, gw, keep_ref, sums_ref, loss_ref, gcos_ref, scos_ref, gfilt_ref, gcell_ref,
    lg, tv, buf, chi, clo, ownc, ownk, along, valid, keepc, whi, wlo, thi, tlo, gmb, oh, l1, l2, cf,
    idc, blocks, sd, sp, st, mass, gmass, gph, gpl, kp,
    stat, a1, a2, a3, fin, kvec, k1, k2, k3,
    part, rb, sb, r1, tt_, r2, qq, r3,
    lsem, tsem, osem,
    zs, zr, xs, xr, ys, yr, bs, br,
    as1, ar1, as2, ar2, as3, ar3, as4, ar4,
    ks1, kr1, ks2, kr2, ks3, kr3,
    cbs, cbr, cxs, cxr, cys, cyr, czs, czr,
):
    n_cells = chi.shape[1]
    width = chi.shape[2]
    last = NCH - 1
    n_blocks = tv.shape[1]
    spots = n_blocks * BR
    n_slides = gene_ref.shape[0]
    tiles = spots // LANES
    wide, narrow = lax.axis_index("wide"), lax.axis_index("narrow")
    z, y = lax.div(wide, 2), lax.rem(wide, 2)
    x, core = lax.div(narrow, 2), lax.rem(narrow, 2)
    to_z = [(lax.rem(z + k, 4) * 2 + y, narrow) for k in (1, 2, 3)]
    from_z = [lax.rem(z + 4 - k, 4) for k in (1, 2, 3)]
    to_x = (wide, (1 - x) * 2 + core)
    to_y = (z * 2 + 1 - y, narrow)
    to_xy = (z * 2 + 1 - y, (1 - x) * 2 + core)
    to_b = (wide, x * 2 + 1 - core)

    def rcopy(src, dst, ss, rs, dev):
        return pltpu.make_async_remote_copy(
            src_ref=src, dst_ref=dst, send_sem=ss, recv_sem=rs, device_id=dev, device_id_type=MESH
        )

    def lanes(i, w=LANES):
        return pl.ds(pl.multiple_of(i * w, w), w)

    own_cells = pltpu.make_async_copy(cells_hbm, ownc, lsem.at[0])

    def get_logits(i):
        return pltpu.make_async_copy(logits_hbm.at[:, lanes(i)], lg.at[i], osem.at[i])

    def get_target(c):
        return pltpu.make_async_copy(target_hbm.at[:, :, lanes(c, width)], tv.at[c], tsem.at[c])

    own_cells.start()
    for i in range(tiles):
        get_logits(i).start()
    for c in range(NCH):
        get_target(c).start()

    barrier = pltpu.get_barrier_semaphore()
    for dev in to_z + [to_x, to_y, to_xy, to_b]:
        pl.semaphore_signal(barrier, inc=1, device_id=dev, device_id_type=MESH)

    iota8 = lax.broadcasted_iota(jnp.int32, (8, LANES), 0)
    lane8 = lax.broadcasted_iota(jnp.int32, (8, LANES), 1)
    row16 = lax.broadcasted_iota(jnp.int32, (16, LANES), 0)
    dev = wide * 4 + narrow
    place = lane8 + iota8 * LANES - dev * 16
    mine = jnp.zeros((16, LANES), f32)
    vector = jnp.zeros((8, LANES), f32)
    for r in range(16):
        mine = jnp.where(row16 == r, filt_ref[r], mine)
        vector = jnp.where(place == r, filt_ref[r], vector)
    kvec[2] = vector
    own_keep = jax.nn.sigmoid(mine)
    ownk[...] = own_keep
    along[...] = jnp.zeros_like(along)
    def one_hot(i, _):
        ids = ids_ref[pl.ds(i, 1), :]
        square = (lax.broadcasted_iota(jnp.int32, (LANES, LANES), 0) == ids).astype(f32)
        oh[lanes(i), :] = square.T.astype(bf16)
        per = LANES // BR
        turned = jnp.broadcast_to(ids, (LANES, LANES)).astype(f32).T
        idc[pl.ds(i * per, per)] = turned.reshape(per, BR, LANES)
        return 0

    lax.fori_loop(0, tiles, one_hot, 0)
    for q in range(n_cells // LANES):
        line = mask_ref[q : q + 1, :].astype(f32)
        valid[q * LANES : (q + 1) * LANES, :] = jnp.broadcast_to(line, (LANES, LANES)).T
    own_cells.wait()
    for c in range(NCH):
        for h in range(2):
            buf[c, h, z, y, x, core] = own_keep * ownc[:, (c * 2 + h) * LANES : (c * 2 + h + 1) * LANES]
    pl.semaphore_wait(barrier, 7)

    def z_out(c, k):
        r = buf.at[c, :, z, y, x, core]
        return rcopy(r, r, zs.at[c, k], zr.at[c, k], to_z[k])

    def z_in(c, k):
        r = buf.at[c, :, from_z[k], y, x, core]
        return rcopy(r, r, zs.at[c, k], zr.at[c, k], to_z[k])

    def s1_out(c):
        a = buf.at[c, 0, :, y, x, core]
        b = buf.at[c, 1, :, y, x, core]
        return [rcopy(a, a, xs.at[c, 0], xr.at[c, 0], to_x), rcopy(b, b, ys.at[c, 0], yr.at[c, 0], to_y)]

    def s1_in(c):
        a = buf.at[c, 0, :, y, 1 - x, core]
        b = buf.at[c, 1, :, 1 - y, x, core]
        return [rcopy(a, a, xs.at[c, 0], xr.at[c, 0], to_x), rcopy(b, b, ys.at[c, 0], yr.at[c, 0], to_y)]

    def s2_out(c):
        a = buf.at[c, 0, :, y, :, core]
        b = buf.at[c, 1, :, :, x, core]
        return [rcopy(a, a, ys.at[c, 1], yr.at[c, 1], to_y), rcopy(b, b, xs.at[c, 1], xr.at[c, 1], to_x)]

    def s2_in(c):
        a = buf.at[c, 0, :, 1 - y, :, core]
        b = buf.at[c, 1, :, :, 1 - x, core]
        return [rcopy(a, a, ys.at[c, 1], yr.at[c, 1], to_y), rcopy(b, b, xs.at[c, 1], xr.at[c, 1], to_x)]

    def s3_out(c):
        r = buf.at[c, :, :, :, :, core]
        return rcopy(r, r, bs.at[c], br.at[c], to_b)

    def s3_in(c):
        r = buf.at[c, :, :, :, :, 1 - core]
        return rcopy(r, r, bs.at[c], br.at[c], to_b)

    def b1(c):
        return rcopy(stat.at[c, 1 - core], a1.at[c], as1.at[c], ar1.at[c], to_b)

    plane = [to_x, to_y, to_xy]
    here = y * 2 + x
    there = [y * 2 + 1 - x, (1 - y) * 2 + x, (1 - y) * 2 + 1 - x]

    def b2_out(c, k):
        r = a2.at[c, here]
        return rcopy(r, r, as2.at[c, k], ar2.at[c, k], plane[k])

    def b2_in(c, k):
        r = a2.at[c, there[k]]
        return rcopy(r, r, as2.at[c, k], ar2.at[c, k], plane[k])

    def b3_out(c, k):
        r = a3.at[c, z]
        return rcopy(r, r, as3.at[c, k], ar3.at[c, k], to_z[k])

    def b3_in(c, k):
        r = a3.at[c, from_z[k]]
        return rcopy(r, r, as3.at[c, k], ar3.at[c, k], to_z[k])

    def b4(c, half):
        r = fin.at[c, half]
        return rcopy(r, r, as4.at[c], ar4.at[c], to_b)

    def sum_second(c):
        b1(c).wait_recv()
        a2[c, here] = stat[c, core] + a1[c]
        for k in range(3):
            b2_out(c, k).start()

    def sum_third(c):
        for k in range(3):
            b2_in(c, k).wait_recv()
        a3[c, z] = (a2[c, 0] + a2[c, 1]) + (a2[c, 2] + a2[c, 3])
        for k in range(3):
            b3_out(c, k).start()

    def sum_fourth(c):
        for k in range(3):
            b3_in(c, k).wait_recv()
        fin[c, core] = (a3[c, 0] + a3[c, 1]) + (a3[c, 2] + a3[c, 3])
        b4(c, core).start()

    def sum_last(c):
        b4(c, 1 - core).wait_recv()

    def v1(n):
        return rcopy(kvec.at[n], k1.at[n], ks1.at[n], kr1.at[n], to_b)

    def v2(n, slot, k):
        return rcopy(k2.at[n, slot], k2.at[n, slot], ks2.at[n, k], kr2.at[n, k], plane[k])

    def v3(n, slot, k):
        return rcopy(k3.at[n, slot], k3.at[n, slot], ks3.at[n, k], kr3.at[n, k], to_z[k])

    def vector_second(n):
        v1(n).wait_recv()
        k2[n, here] = kvec[n] + k1[n]
        for k in range(3):
            v2(n, here, k).start()

    def vector_third(n):
        for k in range(3):
            v2(n, there[k], k).wait_recv()
        k3[n, z] = (k2[n, 0] + k2[n, 1]) + (k2[n, 2] + k2[n, 3])
        for k in range(3):
            v3(n, z, k).start()

    def vector_last(n):
        for k in range(3):
            v3(n, from_z[k], k).wait_recv()
        return (k3[n, 0] + k3[n, 1]) + (k3[n, 2] + k3[n, 3])

    def softmax(i, ent):
        get_logits(i).wait()
        value = lg[i]
        top = jnp.max(value, axis=0, keepdims=True)
        expo = jnp.exp(value - top) * valid[...]
        total = jnp.sum(expo, axis=0, keepdims=True)
        prob = expo * (1.0 / total)
        lg[i] = prob
        high, low = split(prob)
        whi[:, lanes(i)] = high
        wlo[:, lanes(i)] = low
        high, low = split(prob.T)
        thi[lanes(i), :] = high
        tlo[lanes(i), :] = low
        return ent + jnp.sum(prob * (value - top - jnp.log(total)), axis=0, keepdims=True)

    def leave_z(c):
        for k in range(3):
            z_out(c, k).start()

    for c in range(AHEAD):
        leave_z(c)
    v1(2).start()

    def stage_z(c):
        for k in range(3):
            z_in(c, k).wait_recv()
        for d in s1_out(c):
            d.start()

    def stage_1(c):
        for arrived, onward in zip(s1_in(c), s2_out(c)):
            arrived.wait_recv()
            onward.start()

    def stage_2(c):
        for d in s2_in(c):
            d.wait_recv()
        s3_out(c).start()

    def fold(v):
        out = v[:, :LANES]
        for k in range(1, v.shape[1] // LANES):
            out = out + v[:, k * LANES : (k + 1) * LANES]
        return out

    def eighths(v):
        return jnp.sum(v.reshape(v.shape[0] // 8, 8, v.shape[1]), axis=0)

    for c in range(NCH):
        gm = jnp.concatenate(
            [gene_ref[:, c * width : (c + 1) * width].astype(f32), jnp.zeros((LANES - n_slides, width), f32)], axis=0
        )
        gmb[c] = gm.astype(bf16)
    sd[...] = jnp.zeros_like(sd)
    sp[...] = jnp.zeros_like(sp)
    st[...] = jnp.zeros_like(st)

    begins = [jnp.sum((ids_ref[...] < k).astype(jnp.int32)) for k in range(n_slides + 1)]
    firsts = [jnp.minimum(lax.div(begins[k], BR), n_blocks - 1) for k in range(n_slides)]
    lasts = [lax.div(jnp.maximum(begins[k + 1] - 1, 0), BR) for k in range(n_slides)]
    slide16 = lax.broadcasted_iota(jnp.int32, (16, 8 * n_blocks), 0)
    block16 = lax.div(lax.broadcasted_iota(jnp.int32, (16, 8 * n_blocks), 1), 8)
    inner = jnp.zeros((16, 8 * n_blocks), f32)
    for k in range(n_slides):
        full = jnp.logical_and(block16 > firsts[k], block16 < lasts[k])
        inner = jnp.where(jnp.logical_and(slide16 == k, full), 1.0, inner)
    inner = inner.astype(bf16)
    inner = jnp.concatenate([inner, inner], axis=1)
    slide8 = lax.broadcasted_iota(jnp.int32, (8, width), 0)

    def gene_sums(c, products, number, at_row):
        sums = []
        for n in range(number):
            bh, bl = split(blocks[n])
            sums.append(mm(inner, jnp.concatenate([bh, bl], axis=0))[:8, :])
        for k in range(n_slides):
            parts = [jnp.zeros((8, width), f32)] * number
            for block, counts in ((firsts[k], None), (lasts[k], lasts[k] != firsts[k])):
                own = idc[block] == float(k)
                if counts is not None:
                    own = jnp.logical_and(own, counts)
                own = own.astype(f32)
                own = jnp.concatenate([own] * (width // LANES), axis=1)
                for n, prod in enumerate(products(c, block)):
                    parts[n] = parts[n] + eighths(prod * own)
            for n in range(number):
                line = jnp.sum(parts[n], axis=0, keepdims=True)
                sums[n] = sums[n] + jnp.where(slide8 == k, line, 0.0)
        for n in range(number):
            for h in range(2):
                stat[c, h, at_row + n * 8 : at_row + (n + 1) * 8, :] = sums[n][:, h * LANES : (h + 1) * LANES]

    def of_target(c, r):
        tgt = tv[c, r]
        return (tgt * tgt,)

    def of_both(c, r):
        pred, tgt = pv[c, r], tv[c, r]
        return pred * tgt, jnp.where(tgt > 0.0, pred * pred, 0.0)

    def by_rows(c, products, spots_of):
        for r in range(n_blocks):
            at = slice(r * BR, (r + 1) * BR)
            for n, (prod, spot) in enumerate(zip(products(c, r), spots_of)):
                spot[at, :] += fold(prod)
                blocks[n, r * 8 : (r + 1) * 8, :] = eighths(prod)

    def target_sums(c, _):
        per = GR // BR
        for n in range(spots // GR):
            sees = mm(oh[n * GR : (n + 1) * GR, :], gmb[c]).reshape(per, BR, width)
            for r in range(per):
                tv[c, n * per + r] = sees[r] * tv[c, n * per + r]
        by_rows(c, of_target, (st,))
        gene_sums(c, of_target, 1, 16)
        return 0

    def predict(c):
        whole = jnp.concatenate([buf[c, h].reshape(n_cells, LANES) for h in range(2)], axis=1)
        high, low = split(whole)
        chi[c] = high
        clo[c] = low
        wh, wl = thi[...], tlo[...]
        pred = mm(jnp.concatenate([wh, wl, wh], axis=1), jnp.concatenate([high, high, low], axis=0))
        pv[c] = pred.reshape(n_blocks, BR, width)

    def slide_sums():
        keep_rows = jax.nn.sigmoid(vector_last(2))
        keep_ref[...] = keep_rows
        for q in range(quarter):
            line = jnp.broadcast_to(keep_rows[q : q + 1, :], (LANES, LANES))
            keepc[q * LANES : (q + 1) * LANES, :] = line.T

        def by_tile(i, sums):
            at = pl.ds(i, 1)
            line = jnp.sum(lg[i] * keepc[...], axis=0, keepdims=True)
            mass[at, :] = line
            dens = dens_ref[at, :]
            mine = (iota8 == ids_ref[at, :]).astype(f32)
            terms = (line, dens, dens * (jnp.log(dens) - jnp.log(line)))
            return tuple(a + mine * b for a, b in zip(sums, terms))

        blank = jnp.zeros((8, LANES), f32)
        totals = lax.fori_loop(0, tiles, by_tile, (blank, blank, blank))
        for k, value in enumerate(totals):
            blank = jnp.where(lane8 == k, jnp.sum(value, axis=1, keepdims=True), blank)
        kvec[0] = blank
        v1(0).start()

    quarter = n_cells // LANES
    ent = lax.fori_loop(0, tiles // 2, softmax, jnp.zeros((1, LANES), f32))
    stage_z(0)
    leave_z(AHEAD)
    vector_second(2)
    ent = lax.fori_loop(tiles // 2, tiles, softmax, ent)
    stage_z(1)
    leave_z(AHEAD + 1)
    for c in range(NCH):
        get_target(c).wait()
    lax.fori_loop(0, 3, target_sums, 0)
    stage_z(2)
    leave_z(AHEAD + 2)
    stage_1(0)
    vector_third(2)
    lax.fori_loop(3, 6, target_sums, 0)
    stage_z(3)
    leave_z(AHEAD + 3)
    stage_1(1)
    lax.fori_loop(6, NCH, target_sums, 0)
    stage_z(4)
    leave_z(AHEAD + 4)
    stage_1(2)
    slide_sums()
    stage_z(5)
    stage_2(0)
    stage_1(3)

    def gather_tick(t, _):
        c = t - 6
        pl.when(t < NCH)(lambda: stage_z(t))
        pl.when(t - 5 < NCH)(lambda: stage_2(t - 5))
        s3_in(c).wait_recv()
        gene_sums(c - 1, of_both, 2, 0)
        b1(c - 1).start()
        predict(c)
        by_rows(c, of_both, (sd, sp))
        pl.when(t - 2 < NCH)(lambda: stage_1(t - 2))
        pl.when(c == 2)(lambda: vector_third(0))
        sum_second(c - 1)
        pl.when(c >= 3)(lambda: sum_third(c - 3))
        pl.when(c >= 6)(lambda: sum_fourth(c - 6))
        return 0

    stage_z(6)
    stage_2(1)
    s3_in(0).wait_recv()
    predict(0)
    by_rows(0, of_both, (sd, sp))
    stage_1(4)
    vector_second(0)
    lax.fori_loop(7, NCH + 6, gather_tick, 0)
    gene_sums(last, of_both, 2, 0)
    b1(last).start()

    lane128 = lax.broadcasted_iota(jnp.int32, (LANES, LANES), 1)
    slide_of_lane = lax.rem(lane128, 8).astype(f32)

    def spot_rows(i, _):
        at = lanes(i)
        sdot, spp, stt = [jnp.sum(ref[at, :], axis=1, keepdims=True) for ref in (sd, sp, st)]
        scale = lax.rsqrt(spp + eps) * lax.rsqrt(stt + eps)
        sd[at, :] = jnp.broadcast_to(sdot * scale, (LANES, LANES))
        per = LANES // BR
        own = jnp.logical_and(idc[pl.ds(i * per, per)].reshape(LANES, LANES) == slide_of_lane, lane128 < 32)
        for ref, value in ((l1, scale), (l2, scale * (sdot / (spp + eps)))):
            high, low = split(value)
            value = jnp.where(lane128 < 16, 1.0, jnp.where(lane128 < 24, high.astype(f32), low.astype(f32)))
            ref[at, :] = jnp.where(own, value, 0.0).astype(bf16)
        return 0

    lax.fori_loop(0, tiles, spot_rows, 0)
    sum_second(last)
    sum_third(last - 2)
    sum_fourth(last - 5)

    def scatter_sib(c):
        return rcopy(part.at[c, :, :, :, :, 1 - core], rb.at[c], cbs.at[c], cbr.at[c], to_b)

    def scatter_one(c):
        return [
            rcopy(sb.at[c, 0, :, 1 - y], r1.at[c, 0], cys.at[c, 0], cyr.at[c, 0], to_y),
            rcopy(sb.at[c, 1, :, :, 1 - x], r1.at[c, 1], cxs.at[c, 0], cxr.at[c, 0], to_x),
        ]

    def scatter_two(c):
        return [
            rcopy(tt_.at[c, 0, :, 1 - x], r2.at[c, 0], cxs.at[c, 1], cxr.at[c, 1], to_x),
            rcopy(tt_.at[c, 1, :, 1 - y], r2.at[c, 1], cys.at[c, 1], cyr.at[c, 1], to_y),
        ]

    def scatter_z(c, k):
        return rcopy(qq.at[c, :, lax.rem(z + k + 1, 4)], r3.at[c, k], czs.at[c, k], czr.at[c, k], to_z[k])

    def sc1(c):
        scatter_sib(c).wait_recv()
        sb[c] = part[c, :, :, :, :, core] + rb[c]
        for d in scatter_one(c):
            d.start()

    def sc2(c):
        arrived, onward = scatter_one(c), scatter_two(c)
        arrived[0].wait_recv()
        tt_[c, 0] = sb[c, 0, :, y] + r1[c, 0]
        onward[0].start()
        arrived[1].wait_recv()
        tt_[c, 1] = sb[c, 1, :, :, x] + r1[c, 1]
        onward[1].start()

    def sc3(c):
        for d in scatter_two(c):
            d.wait_recv()
        qq[c, 0] = tt_[c, 0, :, x] + r2[c, 0]
        qq[c, 1] = tt_[c, 1, :, y] + r2[c, 1]
        for k in range(3):
            scatter_z(c, k).start()

    def sc4(c):
        for k in range(3):
            scatter_z(c, k).wait_recv()
        for h in range(2):
            at = lanes(c * 2 + h)
            total = (qq[c, h, z] + r3[c, 0, h]) + (r3[c, 1, h] + r3[c, 2, h])
            gcell_ref[:, at] = total * ownk[...]
            along[...] += total * ownc[:, at]

    def gene_coefs(c):
        total = jnp.concatenate([fin[c, 0], fin[c, 1]], axis=1)
        dot_s, pp_s, tt_s = total[0:8], total[8:16], total[16:24]
        gm = gene_ref[:, lanes(c, width)].astype(f32)
        gscale = gm * lax.rsqrt(pp_s + eps) * lax.rsqrt(tt_s + eps)
        gcos_ref[:, lanes(c, width)] = dot_s * gscale
        gshrink = gscale * (dot_s / (pp_s + eps))
        pad = jnp.zeros((LANES - 32, width), f32)
        for n, value in enumerate((gscale, gshrink)):
            high, low = split(value)
            high, low = high.astype(f32), low.astype(f32)
            cf[lax.rem(c, 2), n] = jnp.concatenate([high, low, gm, gm, pad], axis=0).astype(bf16)

    def backward(c):
        slot = lax.rem(c, 2)
        per = GR // BR
        for n in range(spots // GR):
            at = slice(n * GR, (n + 1) * GR)
            own = slice(n * per, (n + 1) * per)
            pred, tgt = pv[c, own].reshape(GR, width), tv[c, own].reshape(GR, width)
            gh, gl = split(mm(l2[at, :], cf[slot, 1]) * pred - mm(l1[at, :], cf[slot, 0]) * tgt)
            gph[c, at, :] = gh
            gpl[c, at, :] = gl
        wh, wl = whi[...], wlo[...]
        gh, gl = gph[c], gpl[c]
        out = mm(jnp.concatenate([wh, wl, wh], axis=1), jnp.concatenate([gh, gh, gl], axis=0))
        for h in range(2):
            part[c, h] = out[:, h * LANES : (h + 1) * LANES].reshape(4, 2, 2, 2, 16, LANES)
        scatter_sib(c).start()
        gene_coefs(jnp.minimum(c + 1, last))

    def spot_part(n):
        at = pl.ds(n * GR, GR)
        left = [chi[c] for c in range(NCH)]
        left = left + [clo[c] for c in range(NCH)] + left
        right = [gph[c, at, :] for c in range(NCH)]
        right = right + right + [gpl[c, at, :] for c in range(NCH)]
        out = mm_nt(jnp.concatenate(left, axis=1), jnp.concatenate(right, axis=1))
        for h in range(GR // LANES):
            i = n * (GR // LANES) + h
            grad = out[:, h * LANES : (h + 1) * LANES] + keepc[...] * gmass[i : i + 1, :]
            prob = lg[i]
            gw[i] = prob * (grad - jnp.sum(prob * grad, axis=0, keepdims=True))

    def back_tick(t, _):
        pl.when(t >= 4)(lambda: sc2(t - 4))
        pl.when(t < last)(lambda: sum_last(t + 1))
        backward(t)
        pl.when(t >= 1)(lambda: sc1(t - 1))
        pl.when(t >= 5)(lambda: sc3(t - 5))
        pl.when(t <= 1)(lambda: sum_third(last - 1 + t))
        pl.when(t <= 4)(lambda: sum_fourth(last - 4 + t))

        return 0

    def slide_totals():
        sums_s = vector_last(0)
        sums_ref[...] = sums_s
        mass_s, wsum_s = sums_s[:, 0:1], sums_s[:, 1:2]
        kp[...] = jnp.zeros_like(kp)

        def by_mass(i, total):
            at = pl.ds(i, 1)
            mine = (iota8 == ids_ref[at, :]).astype(f32)
            mass_at = jnp.sum(mine * mass_s, axis=0, keepdims=True)
            wsum_at = jnp.sum(mine * wsum_s, axis=0, keepdims=True)
            line = -(dens_ref[at, :] / wsum_at) / mass[at, :] + 1.0 / mass_at
            gmass[at, :] = line
            kp[...] += lg[i] * line
            spot = sd[lanes(i), :].T[0:1, :]
            scos_ref[at, :] = spot
            return total + spot

        total = lax.fori_loop(0, tiles, by_mass, jnp.zeros((1, LANES), f32))
        rows_k = [jnp.sum(kp[q * LANES : (q + 1) * LANES, :].T, axis=0, keepdims=True) for q in range(quarter)]
        rows_k = rows_k + [-total, -ent, jnp.zeros((6 - quarter, LANES), f32)]
        kvec[1] = jnp.concatenate(rows_k, axis=0)
        v1(1).start()

    sum_last(0)
    gene_coefs(0)
    lax.fori_loop(0, NCH, back_tick, 0)
    slide_totals()
    sc1(7)
    sc2(4)
    sc2(5)
    sc3(3)
    spot_part(0)
    vector_second(1)
    sc2(6)
    sc3(4)
    sc2(7)
    sc3(5)
    spot_part(1)
    vector_third(1)
    sc3(6)
    sc3(7)
    sc4(0)
    sc4(1)
    sc4(2)
    sc4(3)
    sc4(4)
    spot_part(2)
    spot_part(3)

    keep = keep_ref[...]
    ok = jnp.concatenate([mask_ref[...].astype(f32), jnp.zeros((8 - quarter, LANES), f32)], axis=0)
    off = jnp.sum(ok * keep) - n_cells // 4
    sign = jnp.where(off > 0, 1.0, jnp.where(off < 0, -1.0, 0.0))
    totals = vector_last(1)
    loss_ref[...] = totals
    rest = totals + ok * (sign + 1.0 - 2.0 * keep) / n_cells

    def own_lanes(value):
        picked = jnp.sum(jnp.where(iota8 == lax.div(dev, 8), value, 0.0), axis=0, keepdims=True)
        return pltpu.roll(picked, lax.rem(LANES - lax.rem(dev, 8) * 16, LANES), 1)

    keep = own_lanes(keep)
    rest = own_lanes(rest)

    def leave(c, _):
        for k in range(3):
            z_out(c, k).wait_send()
            b2_out(c, k).wait_send()
            b3_out(c, k).wait_send()
        for d in s1_out(c) + s2_out(c) + scatter_one(c) + scatter_two(c):
            d.wait_send()
        s3_out(c).wait_send()
        b1(c).wait_send()
        b4(c, core).wait_send()
        scatter_sib(c).wait_send()
        return 0

    lax.fori_loop(0, NCH, leave, 0)
    for c in range(NCH - 3):
        for k in range(3):
            scatter_z(c, k).wait_send()
    for n in range(3):
        v1(n).wait_send()
        for k in range(3):
            v2(n, here, k).wait_send()
            v3(n, z, k).wait_send()
    for c in range(NCH - 3, NCH):
        sc4(c)
    genes_part = jnp.concatenate([along[...], jnp.zeros((LANES - 16, LANES), f32)], axis=0)
    genes_part = jnp.sum(genes_part.T, axis=0, keepdims=True)
    gfilt_ref[...] = ((genes_part + rest) * keep * (1.0 - keep))[:, : gfilt_ref.shape[1]]

    for c in range(NCH - 3, NCH):
        for k in range(3):
            scatter_z(c, k).wait_send()


def finish_kernel(
    pv, gw, keep_ref, sums_ref, loss_ref, gcos_in, scos_in, gfilt_in, gcell_in, mask_ref,
    terms_hbm, reg_hbm, pred_hbm, gcos_hbm, scos_hbm, glog_hbm, gfilt_hbm, gcell_hbm,
    terms_ref, reg_ref, psem, osem, rsem,
):
    width = pv.shape[3]
    tiles, n_cells = gw.shape[:2]
    quarter = n_cells // LANES

    def put_pred(c):
        return pltpu.make_async_copy(pv.at[c], pred_hbm.at[:, :, c * width : (c + 1) * width], psem.at[c])

    def put_glog(i):
        return pltpu.make_async_copy(gw.at[i], glog_hbm.at[:, i * LANES : (i + 1) * LANES], osem.at[i])

    for c in range(NCH):
        put_pred(c).start()
    for i in range(tiles):
        put_glog(i).start()
    pairs = [(gcos_in, gcos_hbm), (scos_in, scos_hbm), (gcell_in, gcell_hbm), (gfilt_in, gfilt_hbm)]
    rest = [pltpu.make_async_copy(a, b, rsem.at[k]) for k, (a, b) in enumerate(pairs)]
    for copy in rest:
        copy.start()

    sums_s = sums_ref[...]
    mass_s, wsum_s, logsum_s = sums_s[:, 0:1], sums_s[:, 1:2], sums_s[:, 2:3]
    keep = keep_ref[:quarter, :]
    ok = mask_ref[...].astype(f32)
    count = jnp.sum(ok * keep)
    count_term = jnp.abs(count - n_cells // 4) / n_cells
    binarity = jnp.sum(ok * (keep - keep * keep)) / n_cells
    gene_loss = -jnp.sum(gcos_in[...])
    spot_loss = jnp.sum(loss_ref[quarter : quarter + 1, :])
    entropy = jnp.sum(loss_ref[quarter + 1 : quarter + 2, :]) / (tiles * LANES * 32)
    kl = jnp.sum(logsum_s / wsum_s + jnp.log(mass_s) - jnp.log(wsum_s))
    terms_ref[0] = gene_loss + spot_loss + kl + count_term + binarity
    terms_ref[1] = gene_loss
    terms_ref[2] = spot_loss
    reg_ref[0] = kl
    reg_ref[1] = count_term
    reg_ref[2] = binarity
    reg_ref[3] = entropy
    for k, (a, b) in enumerate(((terms_ref, terms_hbm), (reg_ref, reg_hbm))):
        rest.append(pltpu.make_async_copy(a, b, rsem.at[len(pairs) + k]))
        rest[-1].start()
    for copy in rest:
        copy.wait()
    for i in range(tiles):
        put_glog(i).wait()
    for c in range(NCH):
        put_pred(c).wait()


def fused(logits, filt, cells, cell_mask, gene_mask, slide_ids, target, density):
    n_cells, spots = logits.shape
    own, genes = cells.shape
    n_slides = gene_mask.shape[0]
    width = genes // NCH
    tiles = spots // LANES
    dma = pltpu.SemaphoreType.DMA
    vmem, anywhere = pltpu.VMEM, pl.BlockSpec(memory_space=pl.ANY)
    inside = pl.BlockSpec(memory_space=pltpu.VMEM)
    scalars = pl.BlockSpec(memory_space=pltpu.SMEM)
    ring = (4, 2, 2, 2, 16, LANES)
    scratch = [
        vmem((tiles, n_cells, LANES), f32),
        vmem((NCH, spots // BR, BR, width), f32),
        vmem((NCH, 2) + ring, f32),
        vmem((NCH, n_cells, width), bf16),
        vmem((NCH, n_cells, width), bf16),
        vmem((own, genes), f32),
        vmem((own, LANES), f32),
        vmem((own, LANES), f32),
        vmem((n_cells, LANES), f32),
        vmem((n_cells, LANES), f32),
        vmem((n_cells, spots), bf16),
        vmem((n_cells, spots), bf16),
        vmem((spots, n_cells), bf16),
        vmem((spots, n_cells), bf16),
        vmem((NCH, LANES, width), bf16),
        vmem((spots, LANES), bf16),
        vmem((spots, LANES), bf16),
        vmem((spots, LANES), bf16),
        vmem((2, 2, LANES, width), bf16),
        vmem((spots // BR, BR, LANES), f32),
        vmem((2, spots * 8 // BR, width), f32),
        vmem((spots, LANES), f32),
        vmem((spots, LANES), f32),
        vmem((spots, LANES), f32),
        vmem((8, LANES), f32),
        vmem((8, LANES), f32),
        vmem((NCH, spots, width), bf16),
        vmem((NCH, spots, width), bf16),
        vmem((n_cells, LANES), f32),
        vmem((NCH, 2, 24, LANES), f32),
        vmem((NCH, 24, LANES), f32),
        vmem((NCH, 4, 24, LANES), f32),
        vmem((NCH, 4, 24, LANES), f32),
        vmem((NCH, 2, 24, LANES), f32),
        vmem((3, 8, LANES), f32),
        vmem((3, 8, LANES), f32),
        vmem((3, 4, 8, LANES), f32),
        vmem((3, 4, 8, LANES), f32),
        vmem((NCH, 2) + ring, f32),
        vmem((NCH, 2, 4, 2, 2, 16, LANES), f32),
        vmem((NCH, 2, 4, 2, 2, 16, LANES), f32),
        vmem((NCH, 2, 4, 2, 16, LANES), f32),
        vmem((NCH, 2, 4, 2, 16, LANES), f32),
        vmem((NCH, 2, 4, 16, LANES), f32),
        vmem((NCH, 2, 4, 16, LANES), f32),
        vmem((NCH, 3, 2, 16, LANES), f32),
        dma((1,)), dma((NCH,)), dma((tiles,)),
        dma((NCH, 3)), dma((NCH, 3)), dma((NCH, 2)), dma((NCH, 2)), dma((NCH, 2)), dma((NCH, 2)), dma((NCH,)), dma((NCH,)),
        dma((NCH,)), dma((NCH,)), dma((NCH, 3)), dma((NCH, 3)), dma((NCH, 3)), dma((NCH, 3)), dma((NCH,)), dma((NCH,)),
        dma((3,)), dma((3,)), dma((3, 3)), dma((3, 3)), dma((3, 3)), dma((3, 3)),
        dma((NCH,)), dma((NCH,)), dma((NCH, 2)), dma((NCH, 2)), dma((NCH, 2)), dma((NCH, 2)), dma((NCH, 3)), dma((NCH, 3)),
    ]
    mask = cell_mask.reshape(n_cells // LANES, LANES)
    held = (
        vmem((NCH, spots // BR, BR, width), f32),
        vmem((tiles, n_cells, LANES), f32),
        vmem((8, LANES), f32),
        vmem((8, LANES), f32),
        vmem((8, LANES), f32),
        vmem((n_slides, genes), f32),
        vmem((tiles, LANES), f32),
        vmem((1, own), f32),
        vmem((own, genes), f32),
    )
    between = pl.pallas_call(
        fused_kernel,
        out_shape=held,
        in_specs=[anywhere, scalars, anywhere, inside, inside, inside, anywhere, inside],
        out_specs=(inside,) * len(held),
        scratch_shapes=scratch,
        compiler_params=pltpu.CompilerParams(
            collective_id=0, has_side_effects=True, vmem_limit_bytes=50 << 20
        ),
    )(
        logits, filt, cells, mask, gene_mask,
        slide_ids.reshape(tiles, LANES), target.reshape(spots // BR, BR, genes), density.reshape(tiles, LANES),
    )
    out = pl.pallas_call(
        finish_kernel,
        out_shape=(
            jax.ShapeDtypeStruct((3,), f32),
            jax.ShapeDtypeStruct((4,), f32),
            jax.ShapeDtypeStruct((spots // BR, BR, genes), f32),
            jax.ShapeDtypeStruct((n_slides, genes), f32),
            jax.ShapeDtypeStruct((tiles, LANES), f32),
            jax.ShapeDtypeStruct((n_cells, spots), f32),
            jax.ShapeDtypeStruct((1, own), f32),
            jax.ShapeDtypeStruct((own, genes), f32),
        ),
        in_specs=[inside] * (len(held) + 1),
        out_specs=(anywhere,) * 8,
        scratch_shapes=[pltpu.SMEM((3,), f32), pltpu.SMEM((4,), f32), dma((NCH,)), dma((tiles,)), dma((6,))],
        compiler_params=pltpu.CompilerParams(vmem_limit_bytes=24 << 20),
    )(*between, mask)
    terms, reg, pred, gcos, scos, glog, gfilt, gcell = out
    return terms, reg, pred.reshape(spots, genes), gcos, scos.reshape(spots), glog, gfilt.reshape(own), gcell


def per_slide(onehot, values):
    return lax.dot_general(
        onehot, values, (((0,), (0,)), ((), ())), precision=lax.Precision.HIGHEST
    )


def on_device(logits, filt, cells, cell_mask, gene_mask, slide_ids, target, density):
    high = lax.Precision.HIGHEST
    n_cells = logits.shape[0]
    own_rows = cells.shape[0]
    n_slides = gene_mask.shape[0]
    valid = cell_mask.astype(jnp.float32)
    top = jnp.max(logits, axis=0, keepdims=True)
    expo = jnp.exp(logits - top) * valid[:, None]
    total = jnp.sum(expo, axis=0, keepdims=True)
    prob = expo / total
    logp = jnp.where(valid[:, None] > 0, logits - top - jnp.log(total), 0.0)
    entropy_part = -jnp.sum(prob * logp)
    whole, filt_all = (
        lax.all_gather(cells, ("wide", "narrow"), axis=0, tiled=True),
        lax.all_gather(filt, ("wide", "narrow"), axis=0, tiled=True),
    )
    keep = jax.nn.sigmoid(filt_all)
    weighted = prob * keep[:, None]
    g_pred = lax.dot_general(weighted, whole, (((0,), (0,)), ((), ())), precision=high)
    onehot = (slide_ids[:, None] == jnp.arange(n_slides, dtype=jnp.int32)[None, :]).astype(
        jnp.float32
    )
    gmask = gene_mask.astype(jnp.float32)
    spot_mask = jnp.dot(onehot, gmask, precision=high)
    masked_pred = spot_mask * g_pred
    sdot = jnp.sum(masked_pred * target, axis=1)
    spp = jnp.sum(masked_pred * g_pred, axis=1)
    stt = jnp.sum(spot_mask * target * target, axis=1)
    spot_scale = lax.rsqrt(spp + eps) * lax.rsqrt(stt + eps)
    spot_cos = sdot * spot_scale
    mass = jnp.sum(weighted, axis=0)
    log_part = density * (jnp.log(density) - jnp.log(mass))
    slide_vec = jnp.stack([mass, density, log_part], axis=1)
    loss_parts = jnp.stack([-jnp.sum(spot_cos), entropy_part])
    dot_s, pp_s, tt_s, slide_tot, loss_tot = lax.psum(
        (
            per_slide(onehot, g_pred * target),
            per_slide(onehot, g_pred * g_pred),
            per_slide(onehot, target * target),
            per_slide(onehot, slide_vec),
            loss_parts,
        ),
        ("wide", "narrow"),
    )
    mass_s = slide_tot[:, 0]
    wsum_s = slide_tot[:, 1]
    logsum_s = slide_tot[:, 2]
    gene_scale = gmask * lax.rsqrt(pp_s + eps) * lax.rsqrt(tt_s + eps)
    gene_cos = dot_s * gene_scale
    gene_loss = -jnp.sum(gene_cos)
    spot_loss = loss_tot[0]
    entropy = loss_tot[1] / (prob.shape[1] * lax.axis_size(("wide", "narrow")))
    kl_term = jnp.sum(logsum_s / wsum_s) + jnp.sum(jnp.log(mass_s) - jnp.log(wsum_s))
    count = jnp.sum(valid * keep)
    target_count = n_cells // 4
    count_term = jnp.abs(count - target_count) / n_cells
    binarity = jnp.sum(valid * (keep - keep * keep)) / n_cells
    loss = gene_loss + spot_loss + kl_term + count_term + binarity
    terms = jnp.stack([loss, gene_loss, spot_loss])
    reg_terms = jnp.stack([kl_term, count_term, binarity, entropy])
    gene_shrink = gene_scale * dot_s / (pp_s + eps)
    grad_pred = -jnp.dot(onehot, gene_scale, precision=high) * target
    grad_pred = grad_pred + jnp.dot(onehot, gene_shrink, precision=high) * g_pred
    spot_shrink = sdot / (spp + eps)
    grad_pred = grad_pred - spot_mask * spot_scale[:, None] * (
        target - spot_shrink[:, None] * g_pred
    )
    spot_slide = jnp.dot(onehot, jnp.stack([mass_s, wsum_s], axis=1), precision=high)
    grad_mass = -(density / spot_slide[:, 1]) / mass + 1.0 / spot_slide[:, 0]
    grad_weighted = lax.dot_general(whole, grad_pred, (((1,), (1,)), ((), ())), precision=high)
    grad_weighted = grad_weighted + grad_mass[None, :]
    grad_prob = keep[:, None] * grad_weighted
    keep_part = jnp.sum(prob * grad_weighted, axis=1)
    grad_logits = prob * (grad_prob - jnp.sum(prob * grad_prob, axis=0, keepdims=True))
    cell_part = jnp.dot(weighted, grad_pred, precision=high)
    grad_cells, keep_sum = (
        lax.psum_scatter(cell_part, ("wide", "narrow"), scatter_dimension=0, tiled=True),
        lax.psum_scatter(keep_part, ("wide", "narrow"), scatter_dimension=0, tiled=True),
    )
    first_row = lax.axis_index(("wide", "narrow")) * own_rows
    own_keep = lax.dynamic_slice_in_dim(keep, first_row, own_rows, 0)
    own_valid = lax.dynamic_slice_in_dim(valid, first_row, own_rows, 0)
    keep_grad = (
        keep_sum + own_valid * (jnp.sign(count - target_count) + 1.0 - 2.0 * own_keep) / n_cells
    )
    grad_filter = keep_grad * own_keep * (1.0 - own_keep)
    return (terms, reg_terms, g_pred, gene_cos, spot_cos, grad_logits, grad_filter, grad_cells)


def fits_fused(mesh, logits, cells, gene_mask, slide_ids):
    n_cells, spots = logits.shape
    return (
        (mesh.shape["wide"], mesh.shape["narrow"]) == (8, 4)
        and cells.shape == (16, 2048)
        and n_cells == 512
        and spots == 1024
        and gene_mask.shape[0] == 8
    )


def solution(mesh):
    def step(logits, filt, cells, cell_mask, gene_mask, slide_ids, target, density):
        fits = fits_fused(mesh, logits, cells, gene_mask, slide_ids)
        run = fused if fits else on_device
        return run(logits, filt, cells, cell_mask, gene_mask, slide_ids, target, density)

    placed = (
        P(None, ("wide", "narrow")),
        P(("wide", "narrow")),
        P(("wide", "narrow"), None),
        P(),
        P(),
        P(("wide", "narrow")),
        P(("wide", "narrow"), None),
        P(("wide", "narrow")),
    )
    return jax.shard_map(
        step,
        mesh=mesh,
        in_specs=placed,
        out_specs=(
            P(),
            P(),
            P(("wide", "narrow"), None),
            P(),
            P(("wide", "narrow")),
            P(None, ("wide", "narrow")),
            P(("wide", "narrow")),
            P(("wide", "narrow"), None),
        ),
        check_vma=False,
    )
```
